32 devices in a mesh: rep: 16 (over z, y, core), shard: 2 (over x).
Axes of the slice: x: 2, y: 2, z: 4, core: 2. Of those that a mesh axis runs over, the one named last changes fastest.
Arguments:
- tokens: bfloat16 [4, 2048, 1024], P('shard', 'rep'), may hold values from -6 to 6
- first_values: bfloat16 [4, 2048, 1024], P('shard', 'rep'), may hold values from -6 to 6
- prefix_len: int32 [4], P('shard'), may hold values from 204 to 1024
- cotangent: bfloat16 [4, 2048, 1024], P('shard', 'rep'), may hold values from -6 to 6
- w_query: bfloat16 [1024, 1024], P('shard'), may hold values from -0.25 to 0.25
- w_key: bfloat16 [1024, 1024], P('shard'), may hold values from -0.25 to 0.25
- w_value: bfloat16 [1024, 1024], P('shard'), may hold values from -0.1875 to 0.1875
- w_output: bfloat16 [1024, 1024], P('shard'), may hold values from -0.75 to 0.75
- w_gate: bfloat16 [1024, 2816], P('shard'), may hold values from -0.1875 to 0.1875
- w_up: bfloat16 [1024, 2816], P('shard'), may hold values from -0.1875 to 0.1875
- w_down: bfloat16 [2816, 1024], P('shard'), may hold values from -0.109375 to 0.109375
- gain_attn: bfloat16 [1024], P('shard'), may hold values from 0.5 to 1.5
- gain_ffn: bfloat16 [1024], P('shard'), may hold values from 0.5 to 1.5
Outputs:
- output: bfloat16 [4, 2048, 1024], P('shard', 'rep')
- grad_tokens: float32 [4, 2048, 1024], P('shard', 'rep')
- grad_first_values: float32 [4, 2048, 1024], P('shard', 'rep')
- grad_query: float32 [1024, 1024], P('shard')
- grad_key: float32 [1024, 1024], P('shard')
- grad_value: float32 [1024, 1024], P('shard')
- grad_output: float32 [1024, 1024], P('shard')
- grad_gate: float32 [1024, 2816], P('shard')
- grad_up: float32 [1024, 2816], P('shard')
- grad_down: float32 [2816, 1024], P('shard')
- grad_gain_attn: float32 [1024], P('shard')
- grad_gain_ffn: float32 [1024], P('shard')
The draws below stay inside these ranges and needn't reach their ends.
All inputs are finite; a program needn't handle non-finite values.
Results may differ from the reference program's by a relative error of at most 0.025.
Values may be sent and summed in bfloat16 or wider, within the bound.
No kernel may reach another device: no remote copies, remote signals or barrier semaphores. Data moves between devices by JAX's collectives and lax.ppermute only.
A program may use at most 384 MiB of HBM per device.

```python
import jax
import jax.numpy as jnp
from jax import lax

D = 1024
HEADS = 16
FF = 2816
LENGTH = 2048
SEQS = 4


def place_ends(array, stream_key, low, high):
    longest = array.shape.index(max(array.shape))
    spots = []
    for shift in (0, 1):
        where = [jax.random.randint(jax.random.fold_in(stream_key, axis), (), 0, length) for axis, length in enumerate(array.shape)]
        where[longest] = (where[longest] + shift) % array.shape[longest]
        spots.append(tuple(where))
    return array.at[spots[0]].set(low).at[spots[1]].set(high)


def block_levels(stream_key, shape, split, smallest, high):
    gain, own = 1.0, jax.random.fold_in(stream_key, 6)
    for position, blocks in split:
        steps = jnp.exp(jax.random.uniform(jax.random.fold_in(own, position), (blocks,), jnp.float32, smallest / len(split), high / len(split)))
        gain = gain * jnp.repeat(steps, shape[position] // blocks).reshape([-1 if axis == position else 1 for axis in range(len(shape))])
    return gain


def noise(key, extent, spread, limit, cuts=(), held_as=jnp.bfloat16):
    values = spread * jax.random.normal(key, extent, jnp.float32)
    if cuts:
        values = values * block_levels(key, extent, cuts, -0.22, 0.18)
    return jnp.clip(values, -limit, limit).astype(held_as)


def setup_inputs(seed: int = 0) -> dict:
    seeds = jax.random.split(jax.random.key(seed), 14)
    return {
        "tokens": noise(seeds[0], (SEQS, LENGTH, D), 1.0, 6.0, ((0, 2), (1, 16))),
        "first_values": noise(seeds[1], (SEQS, LENGTH, D), 1.0, 6.0, ((0, 2), (1, 16))),
        "prefix_len": place_ends(jax.random.randint(seeds[2], (SEQS,), LENGTH // 10, LENGTH // 2 + 1), jax.random.fold_in(seeds[2], 1), LENGTH // 10, (LENGTH // 2 + 1) - 1).astype(jnp.int32),
        "cotangent": noise(seeds[3], (SEQS, LENGTH, D), 1.0, 6.0, ((0, 2), (1, 16))),
        "w_query": noise(seeds[4], (D, D), (D // 2) ** -0.5, 0.25, ((0, 2),)),
        "w_key": noise(seeds[5], (D, D), (D // 2) ** -0.5, 0.25, ((0, 2),)),
        "w_value": noise(seeds[6], (D, D), D ** -0.5, 0.1875, ((0, 2),)),
        "w_output": noise(seeds[7], (D, D), (D // 16) ** -0.5, 0.75, ((0, 2),)),
        "w_gate": noise(seeds[8], (D, FF), D ** -0.5, 0.1875, ((0, 2),)),
        "w_up": noise(seeds[9], (D, FF), D ** -0.5, 0.1875, ((0, 2),)),
        "w_down": noise(seeds[10], (FF, D), FF ** -0.5, 0.109375, ((0, 2),)),
        "gain_attn": jnp.clip(1.0 + 0.1 * jax.random.normal(seeds[11], (D,), jnp.float32), 0.5, 1.5).astype(jnp.bfloat16),
        "gain_ffn": jnp.clip(1.0 + 0.1 * jax.random.normal(seeds[12], (D,), jnp.float32), 0.5, 1.5).astype(jnp.bfloat16),
    }


EPSILON = 1e-05
NEGATIVE = -1e+30
ROPE_BASE = 10000.0

@jax.custom_vjp
def low(v):
    return lax.optimization_barrier(v.astype(jnp.bfloat16)).astype(jnp.float32)

@jax.custom_vjp
def low_back(v):
    return v

def low_keep(v):
    return (low(v), None)

def low_pass(kept, grad):
    return (grad,)

def back_keep(v):
    return (v, None)

def back_low(kept, grad):
    return (low(grad),)
low.defvjp(low_keep, low_pass)
low_back.defvjp(back_keep, back_low)

def rotate_half(values):
    half_dim = values.shape[-1] // 2
    return jnp.concatenate([-values[..., half_dim:], values[..., :half_dim]], axis=-1)

def rope_tables(positions, head_dim):
    half_dim = head_dim // 2
    frequency = ROPE_BASE ** (-2.0 * jnp.arange(half_dim, dtype=jnp.float32) / head_dim)
    angles = positions.astype(jnp.float32)[:, None] * frequency[None, :]
    angles = jnp.concatenate([angles, angles], axis=-1)
    return (jnp.cos(angles), jnp.sin(angles))

def rope_apply(values, cosine_table, sine_table):
    return values * cosine_table + rotate_half(values) * sine_table

def matmul(left, right):
    return jnp.dot(left, right, precision=lax.Precision.HIGHEST)

def norm_rows(values):
    return values * lax.rsqrt(lax.optimization_barrier(jnp.mean(values * values, axis=-1, keepdims=True)) + EPSILON)

def attention(query_rows, key_rows, value_rows, prefix):
    length = query_rows.shape[0]
    block_width = min(512, length)
    key_pos = jnp.arange(length, dtype=jnp.int32)

    def one_block(block_index):
        offset = block_index * block_width
        query_block = lax.dynamic_slice_in_dim(query_rows, offset, block_width, 0)
        query_pos = offset + jnp.arange(block_width, dtype=jnp.int32)
        scores = low_back(jnp.einsum('qhd,khd->hqk', query_block, key_rows, precision=lax.Precision.HIGHEST))
        allowed = (key_pos[None, :] <= query_pos[:, None]) | (key_pos[None, :] < prefix)
        scores = jnp.where(allowed[None], scores, NEGATIVE)
        log_mass = jax.nn.logsumexp(scores, axis=-1, keepdims=True)
        weights = low(jnp.exp(scores - log_mass))
        mixed_rows = jnp.einsum('hqk,khd->qhd', weights, value_rows, precision=lax.Precision.HIGHEST)
        return mixed_rows.reshape(block_width, -1)
    blocks = lax.map(jax.checkpoint(one_block), jnp.arange(length // block_width, dtype=jnp.int32))
    return blocks.reshape(length, -1)

def layer(inputs, first_rows, params, prefix):
    w_query, w_key, w_value, w_output, w_gate, w_up, w_down, gain_attn, gain_ffn = params
    length, model_width = inputs.shape
    head_dim = model_width // HEADS
    cosine_table, sine_table = rope_tables(jnp.arange(length, dtype=jnp.int32), head_dim)
    cosine_table = cosine_table[:, None, :]
    sine_table = sine_table[:, None, :]
    hidden1 = low(norm_rows(inputs) * gain_attn)
    query_raw = low_back(matmul(hidden1, w_query)).reshape(length, HEADS, head_dim)
    key_raw = low_back(matmul(hidden1, w_key)).reshape(length, HEADS, head_dim)
    value_mix = low(low_back(0.5 * matmul(hidden1, w_value) + 0.5 * first_rows)).reshape(length, HEADS, head_dim)
    query_rot = low(rope_apply(query_raw, cosine_table, sine_table) * 0.125)
    key_rot = low(rope_apply(key_raw, cosine_table, sine_table))
    attended = low(low_back(attention(query_rot, key_rot, value_mix, prefix)))
    residual = inputs + low_back(matmul(attended, w_output))
    hidden2 = low(norm_rows(residual) * gain_ffn)
    gate_pre = low_back(matmul(hidden2, w_gate))
    up_pre = low_back(matmul(hidden2, w_up))
    swiglu = low(jax.nn.silu(gate_pre) * up_pre)
    return residual + matmul(swiglu, w_down)

def reference(tokens, first_values, prefix_len, cotangent, w_query, w_key, w_value, w_output, w_gate, w_up, w_down, gain_attn, gain_ffn):
    params = tuple((weight.astype(jnp.float32) for weight in (w_query, w_key, w_value, w_output, w_gate, w_up, w_down, gain_attn, gain_ffn)))
    initial = tuple((jnp.zeros(weight.shape, jnp.float32) for weight in params))

    def per_sequence(totals, sequence_item):
        inputs, first_rows, prefix, upstream = sequence_item

        def forward(inputs_in, first_in, params_in):
            return layer(inputs_in, first_in, params_in, prefix)
        result, pullback = jax.vjp(forward, inputs, first_rows, params)
        grad_inputs, grad_first, grad_params = pullback(upstream)
        totals = tuple((running + gradient for running, gradient in zip(totals, grad_params)))
        return (totals, (result.astype(jnp.bfloat16), grad_inputs, grad_first))
    sequence_items = (tokens.astype(jnp.float32), first_values.astype(jnp.float32), prefix_len, cotangent.astype(jnp.float32))
    totals, stacked = lax.scan(per_sequence, initial, sequence_items)
    return (stacked[0], stacked[1], stacked[2], totals[0], totals[1], totals[2], totals[3], totals[4], totals[5], totals[6], totals[7], totals[8])
```

```python
import functools

import jax
import jax.numpy as jnp
from jax import lax
from jax.experimental import pallas as pl
from jax.experimental.pallas import tpu as pltpu
from jax.sharding import PartitionSpec as P

HEADS = 16
EPSILON = 1e-05
NEGATIVE = -1e30
ROPE_BASE = 10000.0
BF16 = jnp.bfloat16
F32 = jnp.float32
VMEM_LIMIT = 60 * 1024 * 1024


def dot(left, right, contract):
    return lax.dot_general(
        left, right, ((contract[:1], contract[1:]), ((), ())), preferred_element_type=F32
    )


def norm_rows(values):
    scale = lax.rsqrt(jnp.mean(values * values, axis=-1, keepdims=True) + EPSILON)
    return (values * scale, scale)


def norm_back(gradient, normed, scale):
    return scale * (gradient - normed * jnp.mean(gradient * normed, axis=-1, keepdims=True))


def rope_lanes(positions, lanes, head_dim):
    half = head_dim // 2
    lane = jnp.arange(lanes, dtype=jnp.int32) % head_dim
    frequency = ROPE_BASE ** (-2.0 * (lane % half).astype(F32) / head_dim)
    angles = positions.astype(F32)[:, None] * frequency[None, :]
    sign = jnp.where(lane < half, 1.0, -1.0).astype(F32)
    return (jnp.cos(angles), jnp.sin(angles) * sign[None, :])


def partner(values, head_dim, roll):
    half = head_dim // 2
    lane = lax.broadcasted_iota(jnp.int32, values.shape, values.ndim - 1) % head_dim
    return jnp.where(lane < half, roll(values, half), roll(values, -half))


def lane_roll(values, shift):
    return jnp.roll(values, -shift, axis=-1)


def kernel_roll(values, shift):
    width = values.shape[-1]
    if width % 128 == 0:
        return pltpu.roll(values, (-shift) % width, axis=values.ndim - 1)
    shift = shift % width
    return jnp.concatenate([values[..., shift:], values[..., :shift]], axis=-1)


def head_rows(values, head, head_dim):
    if values.shape[-1] == head_dim:
        return values
    lane = lax.broadcasted_iota(jnp.int32, values.shape, values.ndim - 1)
    mine = (lane >= head * head_dim) & (lane < (head + 1) * head_dim)
    return jnp.where(mine, values, jnp.zeros_like(values))


def masked_scores(key_block, query_block, key_start, query_start, prefix):
    scores = dot(key_block, query_block, (1, 1))
    query_pos = query_start + lax.broadcasted_iota(jnp.int32, (1, scores.shape[1]), 1)
    last = jnp.maximum(query_pos, prefix - 1) - key_start
    key_pos = lax.broadcasted_iota(jnp.int32, scores.shape, 0)
    return jnp.where(key_pos <= last, scores, NEGATIVE)


def attend_kernel(
    head_dim, bq, bk, prefix_ref, q_ref, k_ref, v_ref, att_ref, att_t_ref, mass_ref, v_t, acc
):
    length, width = q_ref.shape
    heads = width // head_dim
    prefix = prefix_ref[0]
    for start in range(0, length, 128):
        v_t[:, start : start + 128] = v_ref[start : start + 128, :].T

    def query_step(i, carry):
        q0 = pl.multiple_of(i * bq, bq)
        q_all = q_ref[pl.ds(q0, bq), :]
        q_heads = [head_rows(q_all, h, head_dim) for h in range(heads)]
        acc[...] = jnp.zeros_like(acc)
        blocks = (jnp.maximum(q0 + bq, prefix) + bk - 1) // bk

        def key_step(j, stats):
            k0 = pl.multiple_of(j * bk, bk)
            k_block = k_ref[pl.ds(k0, bk), :]
            out = []
            for h in range(heads):
                peak, mass = stats[h]
                scores = masked_scores(k_block, q_heads[h], k0, q0, prefix)
                new_peak = jnp.maximum(peak, jnp.max(scores, axis=0, keepdims=True))
                alpha = jnp.exp(peak - new_peak)
                weights = jnp.exp(scores - new_peak)
                mass = mass * alpha + jnp.sum(weights, axis=0, keepdims=True)
                rows = slice(h * head_dim, (h + 1) * head_dim)
                acc[rows, :] = acc[rows, :] * alpha + dot(
                    v_t[rows, pl.ds(k0, bk)], weights.astype(BF16), (1, 0)
                )
                out.append((new_peak, mass))
            return tuple(out)

        first = tuple(
            (jnp.full((1, bq), NEGATIVE, F32), jnp.zeros((1, bq), F32)) for _ in range(heads)
        )
        stats = lax.fori_loop(0, blocks, key_step, first)
        for h in range(heads):
            peak, mass = stats[h]
            rows = slice(h * head_dim, (h + 1) * head_dim)
            att_t_ref[rows, pl.ds(q0, bq)] = acc[rows, :] / mass
            mass_ref[h : h + 1, pl.ds(q0, bq)] = peak + jnp.log(mass)
        for part in range(0, bq, 128):
            place = pl.ds(pl.multiple_of(q0 + part, 128), 128)
            att_ref[place, :] = att_t_ref[:, place].T.astype(BF16)
        return carry

    lax.fori_loop(0, length // bq, query_step, 0)


def attend_back_kernel(
    head_dim,
    bq,
    bk,
    prefix_ref,
    q_ref,
    k_ref,
    v_ref,
    do_ref,
    att_t_ref,
    mass_ref,
    cos_ref,
    sin_ref,
    dq_ref,
    dk_ref,
    dv_ref,
    k_t,
    delta,
    dq_t,
    dk_acc,
    dv_acc,
):
    length, width = q_ref.shape
    heads = width // head_dim
    prefix = prefix_ref[0]
    dq_t[...] = jnp.zeros_like(dq_t)
    for start in range(0, length, 128):
        place = slice(start, start + 128)
        k_t[:, place] = k_ref[place, :].T
        product = do_ref[place, :].astype(F32).T * att_t_ref[:, place]
        for h in range(heads):
            rows = slice(h * head_dim, (h + 1) * head_dim)
            delta[h : h + 1, place] = jnp.sum(product[rows, :], axis=0, keepdims=True)

    def rope_back(gradient, place):
        return gradient * cos_ref[place, :] + partner(gradient, head_dim, kernel_roll) * sin_ref[
            place, :
        ]

    def key_step(j, carry):
        k0 = pl.multiple_of(j * bk, bk)
        k_block = k_ref[pl.ds(k0, bk), :]
        v_block = v_ref[pl.ds(k0, bk), :]
        dk_acc[...] = jnp.zeros_like(dk_acc)
        dv_acc[...] = jnp.zeros_like(dv_acc)
        begin = jnp.where(k0 < prefix, 0, k0 // bq)

        def query_step(i, inner):
            q0 = pl.multiple_of(i * bq, bq)
            q_all = q_ref[pl.ds(q0, bq), :]
            do_all = do_ref[pl.ds(q0, bq), :]
            for h in range(heads):
                rows = slice(h * head_dim, (h + 1) * head_dim)
                q_head = head_rows(q_all, h, head_dim)
                do_head = head_rows(do_all, h, head_dim)
                scores = masked_scores(k_block, q_head, k0, q0, prefix)
                weights = jnp.exp(scores - mass_ref[h : h + 1, pl.ds(q0, bq)])
                grad_weights = dot(v_block, do_head, (1, 1))
                grad_scores = (weights * (grad_weights - delta[h : h + 1, pl.ds(q0, bq)])).astype(
                    BF16
                )
                dv_acc[...] += dot(weights.astype(BF16), do_head, (1, 0))
                dk_acc[...] += dot(grad_scores, q_head, (1, 0))
                dq_t[rows, pl.ds(q0, bq)] += dot(k_t[rows, pl.ds(k0, bk)], grad_scores, (1, 0))
            return inner

        lax.fori_loop(begin, length // bq, query_step, 0)
        place = pl.ds(k0, bk)
        dk_ref[place, :] = rope_back(dk_acc[...], place).astype(BF16)
        dv_ref[place, :] = dv_acc[...].astype(BF16)
        return carry

    lax.fori_loop(0, length // bk, key_step, 0)
    for start in range(0, length, 128):
        place = slice(start, start + 128)
        dq_ref[place, :] = rope_back(dq_t[:, place].T * 0.125, place).astype(BF16)


def whole(shape):
    return pl.BlockSpec(shape, lambda *_: (0,) * len(shape))


def attend(prefix, q, k, v, head_dim, bq, bk):
    length, width = q.shape
    heads = width // head_dim
    flops = 2 * 2 * heads * length * length * head_dim
    return pl.pallas_call(
        functools.partial(attend_kernel, head_dim, bq, bk),
        out_shape=(
            jax.ShapeDtypeStruct((length, width), BF16),
            jax.ShapeDtypeStruct((width, length), F32),
            jax.ShapeDtypeStruct((heads, length), F32),
        ),
        grid_spec=pltpu.PrefetchScalarGridSpec(
            num_scalar_prefetch=1,
            grid=(1,),
            in_specs=[whole((length, width))] * 3,
            out_specs=[whole((length, width)), whole((width, length)), whole((heads, length))],
            scratch_shapes=[pltpu.VMEM((width, length), BF16), pltpu.VMEM((width, bq), F32)],
        ),
        compiler_params=pltpu.CompilerParams(vmem_limit_bytes=VMEM_LIMIT),
        cost_estimate=pl.CostEstimate(
            flops=flops, transcendentals=heads * length * length, bytes_accessed=8 * length * width
        ),
    )(prefix, q, k, v)


def attend_back(prefix, q, k, v, do, att_t, mass, cosine, sine, head_dim, bq, bk):
    length, width = q.shape
    heads = width // head_dim
    flops = 5 * 2 * heads * length * length * head_dim
    rows = whole((length, width))
    return pl.pallas_call(
        functools.partial(attend_back_kernel, head_dim, bq, bk),
        out_shape=(jax.ShapeDtypeStruct((length, width), BF16),) * 3,
        grid_spec=pltpu.PrefetchScalarGridSpec(
            num_scalar_prefetch=1,
            grid=(1,),
            in_specs=[rows] * 4 + [whole((width, length)), whole((heads, length)), rows, rows],
            out_specs=[rows] * 3,
            scratch_shapes=[
                pltpu.VMEM((width, length), BF16),
                pltpu.VMEM((heads, length), F32),
                pltpu.VMEM((width, length), F32),
                pltpu.VMEM((bk, width), F32),
                pltpu.VMEM((bk, width), F32),
            ],
        ),
        compiler_params=pltpu.CompilerParams(vmem_limit_bytes=VMEM_LIMIT),
        cost_estimate=pl.CostEstimate(
            flops=flops, transcendentals=heads * length * length, bytes_accessed=22 * length * width
        ),
    )(prefix, q, k, v, do, att_t, mass, cosine, sine)


def local(
    reps,
    shards,
    tokens,
    first_values,
    prefix_len,
    cotangent,
    w_query,
    w_key,
    w_value,
    w_output,
    w_gate,
    w_up,
    w_down,
    gain_attn,
    gain_ffn,
):
    seqs, rows, width = tokens.shape
    head_dim = width // HEADS
    length = rows * reps
    groups = reps // seqs
    lanes = width // groups
    here = lax.axis_index("rep")
    my_seq = here // groups
    total = seqs * rows

    def gather(weights):
        height = weights[0].shape[0]
        share = height // reps
        if share * reps == height and share % 8 == 0:
            pieces = [lax.dynamic_slice_in_dim(w, here * share, share, 0) for w in weights]
            axes = ("shard", "rep")
        else:
            pieces, axes = list(weights), ("shard",)
        piece = pieces[0] if len(pieces) == 1 else jnp.concatenate(pieces, axis=1)
        return lax.all_gather(piece, axes, axis=0, tiled=True)

    gains = lax.all_gather(jnp.stack([gain_attn, gain_ffn]), "shard", axis=1, tiled=True)
    full_qkv = gather((w_query, w_key, w_value))
    full_output = gather((w_output,))
    full_gate_up = gather((w_gate, w_up))
    full_down = gather((w_down,))
    gain1 = gains[0].astype(F32)
    gain2 = gains[1].astype(F32)

    def to_heads(values, parts):
        chunks = values.reshape(seqs, rows, parts, groups, lanes).transpose(0, 3, 1, 2, 4)
        chunks = chunks.reshape(reps * rows, parts * lanes)
        return lax.all_to_all(chunks, "rep", 0, 0, tiled=True)

    def to_tokens(values, parts):
        chunks = lax.all_to_all(values, "rep", 0, 0, tiled=True)
        chunks = chunks.reshape(seqs, groups, rows, parts, lanes).transpose(0, 2, 3, 1, 4)
        return chunks.reshape(total, parts * width)

    local_pos = here * rows + jnp.arange(rows, dtype=jnp.int32)
    cosine, sine = rope_lanes(local_pos, width, head_dim)
    cosine = jnp.tile(cosine, (seqs, 1))
    sine = jnp.tile(sine, (seqs, 1))
    all_cosine, all_sine = rope_lanes(jnp.arange(length, dtype=jnp.int32), lanes, head_dim)
    prefix = lax.dynamic_slice_in_dim(prefix_len, my_seq, 1, 0)

    inputs = tokens.reshape(total, width).astype(F32)
    normed1, scale1 = norm_rows(inputs)
    hidden1 = (normed1 * gain1).astype(BF16)
    hidden1_all = lax.all_gather(hidden1.reshape(seqs, rows, width), "rep", axis=1, tiled=True)
    raw = dot(hidden1, full_qkv, (1, 0))

    def rope(values):
        return values * cosine - partner(values, head_dim, lane_roll) * sine

    query_rot = (rope(raw[:, :width]) * 0.125).astype(BF16)
    key_rot = rope(raw[:, width : 2 * width]).astype(BF16)
    first = first_values.reshape(total, width).astype(F32)
    value_mix = (0.5 * raw[:, 2 * width :] + 0.5 * first).astype(BF16)
    qkv = to_heads(jnp.concatenate([query_rot, key_rot, value_mix], axis=1), 3)
    q, k, v = qkv[:, :lanes], qkv[:, lanes : 2 * lanes], qkv[:, 2 * lanes :]
    block = min(512, length)
    att, att_t, mass = attend(prefix, q, k, v, head_dim, block, block)
    attended = to_tokens(att, 1)

    residual = inputs + dot(attended, full_output, (1, 0))
    normed2, scale2 = norm_rows(residual)
    hidden2 = (normed2 * gain2).astype(BF16)
    gate_up = dot(hidden2, full_gate_up, (1, 0))
    ff = gate_up.shape[1] // 2
    gate_pre, up_pre = gate_up[:, :ff], gate_up[:, ff:]
    sigma = jax.nn.sigmoid(gate_pre)
    swish = gate_pre * sigma
    swiglu = (swish * up_pre).astype(BF16)
    output = (residual + dot(swiglu, full_down, (1, 0))).astype(BF16)

    upstream = cotangent.reshape(total, width)
    grad_swiglu = dot(upstream, full_down, (1, 1))
    grad_gate_pre = (grad_swiglu * up_pre * sigma * (1.0 + gate_pre * (1.0 - sigma))).astype(BF16)
    grad_up_pre = (grad_swiglu * swish).astype(BF16)
    grad_gate_up = jnp.concatenate([grad_gate_pre, grad_up_pre], axis=1)
    grad_hidden2 = dot(grad_gate_up, full_gate_up, (1, 1))
    grad_residual = upstream.astype(F32) + norm_back(grad_hidden2 * gain2, normed2, scale2)
    grad_residual_low = grad_residual.astype(BF16)
    grad_attended = dot(grad_residual_low, full_output, (1, 1)).astype(BF16)

    def reduce_gather(partial):
        axes = ("shard", "rep")
        piece = lax.psum_scatter(partial.astype(BF16), axes, scatter_dimension=0, tiled=True)
        return lax.all_gather(piece, "rep", axis=0, tiled=True).astype(F32)

    grad_down = reduce_gather(dot(swiglu, upstream, (0, 0)))
    grad_wgate_up = reduce_gather(dot(hidden2, grad_gate_up, (0, 0)))
    grad_outproj = reduce_gather(dot(attended, grad_residual_low, (0, 0)))

    do = to_heads(grad_attended, 1)
    dq, dk, dv = attend_back(
        prefix, q, k, v, do, att_t, mass, all_cosine, all_sine, head_dim, block, block
    )
    grad_qkv_heads = jnp.concatenate([dq, dk, dv], axis=1)
    half_value = jnp.where(jnp.arange(3 * lanes) < 2 * lanes, 1.0, 0.5).astype(BF16)
    grad_raw_heads = grad_qkv_heads * half_value
    grad_raw = to_tokens(grad_raw_heads, 3)
    grad_first = grad_raw[:, 2 * width :].astype(F32)
    grad_hidden1 = dot(grad_raw, full_qkv, (1, 1))
    grad_inputs = grad_residual + norm_back(grad_hidden1 * gain1, normed1, scale1)

    hidden_mine = lax.dynamic_index_in_dim(hidden1_all, my_seq, 0, keepdims=False)
    columns = dot(hidden_mine, grad_raw_heads, (0, 0))
    columns = lax.psum_scatter(columns.astype(BF16), "shard", scatter_dimension=0, tiled=True)
    height = columns.shape[0]
    share = height // seqs
    mine = lax.dynamic_slice_in_dim(columns, my_seq * share, share, 0).astype(F32)
    for turn in range(1, seqs):
        sent = lax.dynamic_slice_in_dim(columns, ((my_seq + turn) % seqs) * share, share, 0)
        moves = [
            (s * groups + g, ((s + turn) % seqs) * groups + g)
            for s in range(seqs)
            for g in range(groups)
        ]
        mine = mine + lax.ppermute(sent, "rep", moves).astype(F32)
    gathered = lax.all_gather(mine.astype(BF16), "rep", axis=0, tiled=True)
    gathered = gathered.reshape(seqs, groups, share, 3, lanes).transpose(3, 0, 2, 1, 4)
    grad_wqkv = gathered.reshape(3, height, width).astype(F32)

    grad_gain1 = (
        jnp.sum(w_query.astype(F32) * grad_wqkv[0], axis=1)
        + jnp.sum(w_key.astype(F32) * grad_wqkv[1], axis=1)
        + jnp.sum(w_value.astype(F32) * grad_wqkv[2], axis=1)
    ) / gain_attn.astype(F32)
    grad_wgate, grad_wup = grad_wgate_up[:, :ff], grad_wgate_up[:, ff:]
    grad_gain2 = (
        jnp.sum(w_gate.astype(F32) * grad_wgate, axis=1)
        + jnp.sum(w_up.astype(F32) * grad_wup, axis=1)
    ) / gain_ffn.astype(F32)
    shape = tokens.shape
    return (
        output.reshape(shape),
        grad_inputs.reshape(shape),
        grad_first.reshape(shape),
        grad_wqkv[0],
        grad_wqkv[1],
        grad_wqkv[2],
        grad_outproj,
        grad_wgate,
        grad_wup,
        grad_down,
        grad_gain1,
        grad_gain2,
    )


def solution(mesh):
    sequence = P("shard", "rep", None)
    matrix = P("shard", None)
    vector = P("shard")
    return jax.shard_map(
        functools.partial(local, mesh.shape["rep"], mesh.shape["shard"]),
        mesh=mesh,
        in_specs=(sequence, sequence, vector, sequence) + (matrix,) * 7 + (vector,) * 2,
        out_specs=(sequence,) * 3 + (matrix,) * 7 + (vector,) * 2,
        check_vma=False,
    )
```

```python
import functools

import jax
import jax.numpy as jnp
from jax import lax
from jax.experimental import pallas as pl
from jax.experimental.pallas import tpu as pltpu
from jax.sharding import PartitionSpec as P

HEADS = 16
EPSILON = 1e-05
NEGATIVE = -1e30
ROPE_BASE = 10000.0
BF16 = jnp.bfloat16
F32 = jnp.float32
VMEM_LIMIT = 60 * 1024 * 1024


def dot(left, right, contract):
    return lax.dot_general(
        left, right, ((contract[:1], contract[1:]), ((), ())), preferred_element_type=F32
    )


def norm_rows(values):
    scale = lax.rsqrt(jnp.mean(values * values, axis=-1, keepdims=True) + EPSILON)
    return (values * scale, scale)


def norm_back(gradient, normed, scale):
    return scale * (gradient - normed * jnp.mean(gradient * normed, axis=-1, keepdims=True))


def rope_lanes(positions, lanes, head_dim):
    half = head_dim // 2
    lane = jnp.arange(lanes, dtype=jnp.int32) % head_dim
    frequency = ROPE_BASE ** (-2.0 * (lane % half).astype(F32) / head_dim)
    angles = positions.astype(F32)[:, None] * frequency[None, :]
    sign = jnp.where(lane < half, 1.0, -1.0).astype(F32)
    return (jnp.cos(angles), jnp.sin(angles) * sign[None, :])


def partner(values, head_dim, roll):
    half = head_dim // 2
    lane = lax.broadcasted_iota(jnp.int32, values.shape, values.ndim - 1) % head_dim
    return jnp.where(lane < half, roll(values, half), roll(values, -half))


def lane_roll(values, shift):
    return jnp.roll(values, -shift, axis=-1)


def kernel_roll(values, shift):
    width = values.shape[-1]
    if width % 128 == 0:
        return pltpu.roll(values, (-shift) % width, axis=values.ndim - 1)
    shift = shift % width
    return jnp.concatenate([values[..., shift:], values[..., :shift]], axis=-1)


def head_rows(values, head, head_dim):
    if values.shape[-1] == head_dim:
        return values
    lane = lax.broadcasted_iota(jnp.int32, values.shape, values.ndim - 1)
    mine = (lane >= head * head_dim) & (lane < (head + 1) * head_dim)
    return jnp.where(mine, values, jnp.zeros_like(values))


def masked_scores(key_block, query_block, key_start, query_start, prefix):
    scores = dot(key_block, query_block, (1, 1))
    query_pos = query_start + lax.broadcasted_iota(jnp.int32, (1, scores.shape[1]), 1)
    last = jnp.maximum(query_pos, prefix - 1) - key_start
    key_pos = lax.broadcasted_iota(jnp.int32, scores.shape, 0)
    return jnp.where(key_pos <= last, scores, NEGATIVE)


def attend_kernel(
    head_dim, bq, bk, prefix_ref, q_ref, k_ref, v_ref, att_ref, att_t_ref, mass_ref, v_t, acc
):
    length, width = q_ref.shape
    heads = width // head_dim
    prefix = prefix_ref[0]
    for start in range(0, length, 128):
        v_t[:, start : start + 128] = v_ref[start : start + 128, :].T

    def query_step(i, carry):
        q0 = pl.multiple_of(i * bq, bq)
        q_all = q_ref[pl.ds(q0, bq), :]
        q_heads = [head_rows(q_all, h, head_dim) for h in range(heads)]
        acc[...] = jnp.zeros_like(acc)
        blocks = (jnp.maximum(q0 + bq, prefix) + bk - 1) // bk

        def key_step(j, stats):
            k0 = pl.multiple_of(j * bk, bk)
            k_block = k_ref[pl.ds(k0, bk), :]
            out = []
            for h in range(heads):
                peak, mass = stats[h]
                scores = masked_scores(k_block, q_heads[h], k0, q0, prefix)
                new_peak = jnp.maximum(peak, jnp.max(scores, axis=0, keepdims=True))
                alpha = jnp.exp(peak - new_peak)
                weights = jnp.exp(scores - new_peak)
                mass = mass * alpha + jnp.sum(weights, axis=0, keepdims=True)
                rows = slice(h * head_dim, (h + 1) * head_dim)
                acc[rows, :] = acc[rows, :] * alpha + dot(
                    v_t[rows, pl.ds(k0, bk)], weights.astype(BF16), (1, 0)
                )
                out.append((new_peak, mass))
            return tuple(out)

        first = tuple(
            (jnp.full((1, bq), NEGATIVE, F32), jnp.zeros((1, bq), F32)) for _ in range(heads)
        )
        stats = lax.fori_loop(0, blocks, key_step, first)
        for h in range(heads):
            peak, mass = stats[h]
            rows = slice(h * head_dim, (h + 1) * head_dim)
            att_t_ref[rows, pl.ds(q0, bq)] = acc[rows, :] / mass
            mass_ref[h : h + 1, pl.ds(q0, bq)] = peak + jnp.log(mass)
        for part in range(0, bq, 128):
            place = pl.ds(pl.multiple_of(q0 + part, 128), 128)
            att_ref[place, :] = att_t_ref[:, place].T.astype(BF16)
        return carry

    lax.fori_loop(0, length // bq, query_step, 0)


def attend_back_kernel(
    head_dim,
    bq,
    bk,
    prefix_ref,
    q_ref,
    k_ref,
    v_ref,
    do_ref,
    att_t_ref,
    mass_ref,
    cos_ref,
    sin_ref,
    dq_ref,
    dk_ref,
    dv_ref,
    k_t,
    delta,
    dq_t,
    dk_acc,
    dv_acc,
):
    length, width = q_ref.shape
    heads = width // head_dim
    prefix = prefix_ref[0]
    dq_t[...] = jnp.zeros_like(dq_t)
    for start in range(0, length, 128):
        place = slice(start, start + 128)
        k_t[:, place] = k_ref[place, :].T
        product = do_ref[place, :].astype(F32).T * att_t_ref[:, place]
        for h in range(heads):
            rows = slice(h * head_dim, (h + 1) * head_dim)
            delta[h : h + 1, place] = jnp.sum(product[rows, :], axis=0, keepdims=True)

    def rope_back(gradient, place):
        return gradient * cos_ref[place, :] + partner(gradient, head_dim, kernel_roll) * sin_ref[
            place, :
        ]

    def key_step(j, carry):
        k0 = pl.multiple_of(j * bk, bk)
        k_block = k_ref[pl.ds(k0, bk), :]
        v_block = v_ref[pl.ds(k0, bk), :]
        dk_acc[...] = jnp.zeros_like(dk_acc)
        dv_acc[...] = jnp.zeros_like(dv_acc)
        begin = jnp.where(k0 < prefix, 0, k0 // bq)

        def query_step(i, inner):
            q0 = pl.multiple_of(i * bq, bq)
            q_all = q_ref[pl.ds(q0, bq), :]
            do_all = do_ref[pl.ds(q0, bq), :]
            for h in range(heads):
                rows = slice(h * head_dim, (h + 1) * head_dim)
                q_head = head_rows(q_all, h, head_dim)
                do_head = head_rows(do_all, h, head_dim)
                scores = masked_scores(k_block, q_head, k0, q0, prefix)
                weights = jnp.exp(scores - mass_ref[h : h + 1, pl.ds(q0, bq)])
                grad_weights = dot(v_block, do_head, (1, 1))
                grad_scores = (weights * (grad_weights - delta[h : h + 1, pl.ds(q0, bq)])).astype(
                    BF16
                )
                dv_acc[...] += dot(weights.astype(BF16), do_head, (1, 0))
                dk_acc[...] += dot(grad_scores, q_head, (1, 0))
                dq_t[rows, pl.ds(q0, bq)] += dot(k_t[rows, pl.ds(k0, bk)], grad_scores, (1, 0))
            return inner

        lax.fori_loop(begin, length // bq, query_step, 0)
        place = pl.ds(k0, bk)
        dk_ref[place, :] = rope_back(dk_acc[...], place).astype(BF16)
        dv_ref[place, :] = dv_acc[...].astype(BF16)
        return carry

    lax.fori_loop(0, length // bk, key_step, 0)
    for start in range(0, length, 128):
        place = slice(start, start + 128)
        dq_ref[place, :] = rope_back(dq_t[:, place].T * 0.125, place).astype(BF16)


def turns(reps, move):
    pairs = []
    for here in range(reps):
        z, y, core = move(here // 4, (here // 2) % 2, here % 2)
        pairs.append((here, (z % (reps // 4)) * 4 + y * 2 + core))
    return pairs


class Links:
    def __init__(self, reps):
        self.deep = reps // 4
        self.to_core = turns(reps, lambda z, y, core: (z, y, 1 - core))
        self.to_y = turns(reps, lambda z, y, core: (z, 1 - y, core))
        self.to_z = turns(reps, lambda z, y, core: (z + 1, y, core))
        here = lax.axis_index("rep")
        self.z, self.y, self.core = here // 4, (here // 2) % 2, here % 2
        self.x = lax.axis_index("shard")

    def over_core(self, value):
        return lax.ppermute(value, "rep", self.to_core)

    def over_x(self, value):
        return lax.ppermute(value, "shard", [(0, 1), (1, 0)])

    def over_y(self, value):
        return lax.ppermute(value, "rep", self.to_y)

    def next_z(self, value):
        return lax.ppermute(value, "rep", self.to_z)

    def reduce(self, keep, send, x_first):
        columns = keep.shape[1]
        height = keep.shape[0] // 2
        total = add(keep, self.over_core(send))
        if x_first:
            total = total.reshape(2, height, columns)
            total = add(pick(total, self.x), self.over_x(pick(total, 1 - self.x)))
            total = total.reshape(2, height // 2, columns)
            total = add(pick(total, self.y), self.over_y(pick(total, 1 - self.y)))
        else:
            total = total.reshape(2, 2, height // 2, columns)
            total = add(pick(total, self.y, 1), self.over_y(pick(total, 1 - self.y, 1)))
            total = add(pick(total, self.x), self.over_x(pick(total, 1 - self.x)))
        deep = self.deep
        total = total.reshape(deep, height // (2 * deep), columns)
        moving = pick(total, (self.z + deep - 1) % deep)
        for step in range(deep - 1):
            moving = add(pick(total, (self.z + 2 * deep - 2 - step) % deep), self.next_z(moving))
        return moving

    def collect(self, piece):
        deep = self.deep
        whole_z = jnp.zeros((deep,) + piece.shape, piece.dtype)
        for step in range(deep):
            whole_z = put(whole_z, piece, (self.z + deep - step) % deep)
            if step < deep - 1:
                piece = self.next_z(piece)
        whole_z = whole_z.reshape(-1, piece.shape[1])
        halves = join(whole_z, self.over_y(whole_z), self.y).reshape(-1, piece.shape[1])
        return join(halves, self.over_core(halves), self.core)


def pick(values, index, axis=0):
    return lax.dynamic_index_in_dim(values, index, axis, keepdims=False)


def put(values, part, index):
    return lax.dynamic_update_index_in_dim(values, part, index, 0)


def join(mine, other, index):
    both = jnp.zeros((2,) + mine.shape, mine.dtype)
    return put(put(both, mine, index), other, 1 - index)


def add(left, right):
    return (left.astype(F32) + right.astype(F32)).astype(BF16)


def whole(shape):
    return pl.BlockSpec(shape, lambda *_: (0,) * len(shape))


def attend(prefix, q, k, v, head_dim, bq, bk):
    length, width = q.shape
    heads = width // head_dim
    flops = 2 * 2 * heads * length * length * head_dim
    return pl.pallas_call(
        functools.partial(attend_kernel, head_dim, bq, bk),
        out_shape=(
            jax.ShapeDtypeStruct((length, width), BF16),
            jax.ShapeDtypeStruct((width, length), F32),
            jax.ShapeDtypeStruct((heads, length), F32),
        ),
        grid_spec=pltpu.PrefetchScalarGridSpec(
            num_scalar_prefetch=1,
            grid=(1,),
            in_specs=[whole((length, width))] * 3,
            out_specs=[whole((length, width)), whole((width, length)), whole((heads, length))],
            scratch_shapes=[pltpu.VMEM((width, length), BF16), pltpu.VMEM((width, bq), F32)],
        ),
        compiler_params=pltpu.CompilerParams(vmem_limit_bytes=VMEM_LIMIT),
        cost_estimate=pl.CostEstimate(
            flops=flops, transcendentals=heads * length * length, bytes_accessed=8 * length * width
        ),
    )(prefix, q, k, v)


def attend_back(prefix, q, k, v, do, att_t, mass, cosine, sine, head_dim, bq, bk):
    length, width = q.shape
    heads = width // head_dim
    flops = 5 * 2 * heads * length * length * head_dim
    rows = whole((length, width))
    return pl.pallas_call(
        functools.partial(attend_back_kernel, head_dim, bq, bk),
        out_shape=(jax.ShapeDtypeStruct((length, width), BF16),) * 3,
        grid_spec=pltpu.PrefetchScalarGridSpec(
            num_scalar_prefetch=1,
            grid=(1,),
            in_specs=[rows] * 4 + [whole((width, length)), whole((heads, length)), rows, rows],
            out_specs=[rows] * 3,
            scratch_shapes=[
                pltpu.VMEM((width, length), BF16),
                pltpu.VMEM((heads, length), F32),
                pltpu.VMEM((width, length), F32),
                pltpu.VMEM((bk, width), F32),
                pltpu.VMEM((bk, width), F32),
            ],
        ),
        compiler_params=pltpu.CompilerParams(vmem_limit_bytes=VMEM_LIMIT),
        cost_estimate=pl.CostEstimate(
            flops=flops, transcendentals=heads * length * length, bytes_accessed=22 * length * width
        ),
    )(prefix, q, k, v, do, att_t, mass, cosine, sine)


def local(
    reps,
    shards,
    tokens,
    first_values,
    prefix_len,
    cotangent,
    w_query,
    w_key,
    w_value,
    w_output,
    w_gate,
    w_up,
    w_down,
    gain_attn,
    gain_ffn,
):
    seqs, rows, width = tokens.shape
    head_dim = width // HEADS
    length = rows * reps
    groups = reps // seqs
    lanes = width // groups
    here = lax.axis_index("rep")
    my_seq = here // groups
    total = seqs * rows

    def gather(weights):
        height = weights[0].shape[0]
        share = height // reps
        if share * reps == height and share % 8 == 0:
            pieces = [lax.dynamic_slice_in_dim(w, here * share, share, 0) for w in weights]
            axes = ("shard", "rep")
        else:
            pieces, axes = list(weights), ("shard",)
        piece = pieces[0] if len(pieces) == 1 else jnp.concatenate(pieces, axis=1)
        return lax.all_gather(piece, axes, axis=0, tiled=True)

    linked = reps % 4 == 0 and reps <= 16 and shards == 2
    links = Links(reps) if linked else None

    def gather_linked(weights, by_rows):
        height = weights[0].shape[0]
        if by_rows:
            half = height // 2
            pieces = [lax.dynamic_slice_in_dim(w, links.core * half, half, 0) for w in weights]
            piece = pieces[0] if len(pieces) == 1 else jnp.concatenate(pieces, axis=1)
        else:
            half = weights[0].shape[1] // 2
            piece = lax.dynamic_slice_in_dim(weights[0], links.core * half, half, 1)
        near = links.over_x(piece)
        far = links.over_core(near)
        width_all = sum(w.shape[1] for w in weights)
        full = jnp.zeros((2 * height, width_all), BF16)
        at = 0
        for w in weights:
            full = lax.dynamic_update_slice(full, w, (links.x * height, at))
            at += w.shape[1]
        for part, core in ((near, links.core), (far, 1 - links.core)):
            base = (1 - links.x) * height
            place = (base + core * half, 0) if by_rows else (base, core * half)
            full = lax.dynamic_update_slice(full, part, place)
        return full

    gains = lax.all_gather(jnp.stack([gain_attn, gain_ffn]), "shard", axis=1, tiled=True)
    if linked:
        full_qkv = gather_linked((w_query, w_key, w_value), True)
        full_output = gather_linked((w_output,), True)
        full_gate_up = gather_linked((w_gate, w_up), True)
        full_down = gather_linked((w_down,), False)
    else:
        full_qkv = gather((w_query, w_key, w_value))
        full_output = gather((w_output,))
        full_gate_up = gather((w_gate, w_up))
        full_down = gather((w_down,))
    gain1 = gains[0].astype(F32)
    gain2 = gains[1].astype(F32)

    def to_heads(values, parts):
        chunks = values.reshape(seqs, rows, parts, groups, lanes).transpose(0, 3, 1, 2, 4)
        chunks = chunks.reshape(reps * rows, parts * lanes)
        return lax.all_to_all(chunks, "rep", 0, 0, tiled=True)

    def to_tokens(values, parts):
        chunks = lax.all_to_all(values, "rep", 0, 0, tiled=True)
        chunks = chunks.reshape(seqs, groups, rows, parts, lanes).transpose(0, 2, 3, 1, 4)
        return chunks.reshape(total, parts * width)

    local_pos = here * rows + jnp.arange(rows, dtype=jnp.int32)
    cosine, sine = rope_lanes(local_pos, width, head_dim)
    cosine = jnp.tile(cosine, (seqs, 1))
    sine = jnp.tile(sine, (seqs, 1))
    all_cosine, all_sine = rope_lanes(jnp.arange(length, dtype=jnp.int32), lanes, head_dim)
    prefix = lax.dynamic_slice_in_dim(prefix_len, my_seq, 1, 0)

    inputs = tokens.reshape(total, width).astype(F32)
    normed1, scale1 = norm_rows(inputs)
    hidden1 = (normed1 * gain1).astype(BF16)
    hidden1_all = lax.all_gather(hidden1.reshape(seqs, rows, width), "rep", axis=1, tiled=True)
    raw = dot(hidden1, full_qkv, (1, 0))

    def rope(values):
        return values * cosine - partner(values, head_dim, lane_roll) * sine

    query_rot = (rope(raw[:, :width]) * 0.125).astype(BF16)
    key_rot = rope(raw[:, width : 2 * width]).astype(BF16)
    first = first_values.reshape(total, width).astype(F32)
    value_mix = (0.5 * raw[:, 2 * width :] + 0.5 * first).astype(BF16)
    qkv = to_heads(jnp.concatenate([query_rot, key_rot, value_mix], axis=1), 3)
    q, k, v = qkv[:, :lanes], qkv[:, lanes : 2 * lanes], qkv[:, 2 * lanes :]
    block = min(512, length)
    att, att_t, mass = attend(prefix, q, k, v, head_dim, block, block)
    attended = to_tokens(att, 1)

    residual = inputs + dot(attended, full_output, (1, 0))
    normed2, scale2 = norm_rows(residual)
    hidden2 = (normed2 * gain2).astype(BF16)
    gate_up = dot(hidden2, full_gate_up, (1, 0))
    ff = gate_up.shape[1] // 2
    gate_pre, up_pre = gate_up[:, :ff], gate_up[:, ff:]
    sigma = jax.nn.sigmoid(gate_pre)
    swish = gate_pre * sigma
    swiglu = (swish * up_pre).astype(BF16)
    output = (residual + dot(swiglu, full_down, (1, 0))).astype(BF16)

    upstream = cotangent.reshape(total, width)
    grad_swiglu = dot(upstream, full_down, (1, 1))
    grad_gate_pre = (grad_swiglu * up_pre * sigma * (1.0 + gate_pre * (1.0 - sigma))).astype(BF16)
    grad_up_pre = (grad_swiglu * swish).astype(BF16)
    grad_gate_up = jnp.concatenate([grad_gate_pre, grad_up_pre], axis=1)
    grad_hidden2 = dot(grad_gate_up, full_gate_up, (1, 1))
    grad_residual = upstream.astype(F32) + norm_back(grad_hidden2 * gain2, normed2, scale2)
    grad_residual_low = grad_residual.astype(BF16)
    grad_attended = dot(grad_residual_low, full_output, (1, 1)).astype(BF16)

    def reduce_gather(partial):
        axes = ("shard", "rep")
        piece = lax.psum_scatter(partial.astype(BF16), axes, scatter_dimension=0, tiled=True)
        return lax.all_gather(piece, "rep", axis=0, tiled=True).astype(F32)

    def core_columns(values, core):
        half = values.shape[1] // 2
        return lax.dynamic_slice_in_dim(values, core * half, half, 1)

    def core_rows(values, core):
        parts = values.reshape(total, 2, 2, -1)
        return pick(parts, core, 2).reshape(total, -1)

    def linked_by_rows(left, right, x_first):
        keep = dot(core_rows(left, links.core), right, (0, 0))
        send = dot(core_rows(left, 1 - links.core), right, (0, 0)).astype(BF16)
        whole_rows = links.collect(links.reduce(keep, send, x_first))
        return whole_rows.reshape(-1, right.shape[1]).astype(F32)

    def linked_by_columns(left, right, x_first):
        keep = dot(left, core_columns(right, links.core), (0, 0))
        send = dot(left, core_columns(right, 1 - links.core), (0, 0)).astype(BF16)
        halves = links.collect(links.reduce(keep, send, x_first))
        return jnp.concatenate([halves[0], halves[1]], axis=1).astype(F32)

    if linked:
        grad_down = linked_by_columns(swiglu, upstream, True)
        grad_wgate = linked_by_rows(hidden2, grad_gate_pre, False)
        grad_wup = linked_by_rows(hidden2, grad_up_pre, True)
        grad_outproj = linked_by_rows(attended, grad_residual_low, False)
    else:
        grad_down = reduce_gather(dot(swiglu, upstream, (0, 0)))
        grad_wgate_up = reduce_gather(dot(hidden2, grad_gate_up, (0, 0)))
        grad_outproj = reduce_gather(dot(attended, grad_residual_low, (0, 0)))
        grad_wgate, grad_wup = grad_wgate_up[:, :ff], grad_wgate_up[:, ff:]

    do = to_heads(grad_attended, 1)
    dq, dk, dv = attend_back(
        prefix, q, k, v, do, att_t, mass, all_cosine, all_sine, head_dim, block, block
    )
    grad_qkv_heads = jnp.concatenate([dq, dk, dv], axis=1)
    half_value = jnp.where(jnp.arange(3 * lanes) < 2 * lanes, 1.0, 0.5).astype(BF16)
    grad_raw_heads = grad_qkv_heads * half_value
    grad_raw = to_tokens(grad_raw_heads, 3)
    grad_first = grad_raw[:, 2 * width :].astype(F32)
    grad_hidden1 = dot(grad_raw, full_qkv, (1, 1))
    grad_inputs = grad_residual + norm_back(grad_hidden1 * gain1, normed1, scale1)

    hidden_mine = lax.dynamic_index_in_dim(hidden1_all, my_seq, 0, keepdims=False)
    columns = dot(hidden_mine, grad_raw_heads, (0, 0))
    if linked:
        sides = columns.astype(BF16).reshape(2, -1, columns.shape[1])
        columns = add(pick(sides, links.x), links.over_x(pick(sides, 1 - links.x)))
    else:
        columns = lax.psum_scatter(columns.astype(BF16), "shard", scatter_dimension=0, tiled=True)
    height = columns.shape[0]
    share = height // seqs
    mine = lax.dynamic_slice_in_dim(columns, my_seq * share, share, 0).astype(F32)
    for turn in range(1, seqs):
        sent = lax.dynamic_slice_in_dim(columns, ((my_seq + turn) % seqs) * share, share, 0)
        moves = [
            (s * groups + g, ((s + turn) % seqs) * groups + g)
            for s in range(seqs)
            for g in range(groups)
        ]
        mine = mine + lax.ppermute(sent, "rep", moves).astype(F32)
    gathered = lax.all_gather(mine.astype(BF16), "rep", axis=0, tiled=True)
    gathered = gathered.reshape(seqs, groups, share, 3, lanes).transpose(3, 0, 2, 1, 4)
    grad_wqkv = gathered.reshape(3, height, width).astype(F32)

    grad_gain1 = (
        jnp.sum(w_query.astype(F32) * grad_wqkv[0], axis=1)
        + jnp.sum(w_key.astype(F32) * grad_wqkv[1], axis=1)
        + jnp.sum(w_value.astype(F32) * grad_wqkv[2], axis=1)
    ) / gain_attn.astype(F32)
    grad_gain2 = (
        jnp.sum(w_gate.astype(F32) * grad_wgate, axis=1)
        + jnp.sum(w_up.astype(F32) * grad_wup, axis=1)
    ) / gain_ffn.astype(F32)
    shape = tokens.shape
    return (
        output.reshape(shape),
        grad_inputs.reshape(shape),
        grad_first.reshape(shape),
        grad_wqkv[0],
        grad_wqkv[1],
        grad_wqkv[2],
        grad_outproj,
        grad_wgate,
        grad_wup,
        grad_down,
        grad_gain1,
        grad_gain2,
    )


def solution(mesh):
    sequence = P("shard", "rep", None)
    matrix = P("shard", None)
    vector = P("shard")
    return jax.shard_map(
        functools.partial(local, mesh.shape["rep"], mesh.shape["shard"]),
        mesh=mesh,
        in_specs=(sequence, sequence, vector, sequence) + (matrix,) * 7 + (vector,) * 2,
        out_specs=(sequence,) * 3 + (matrix,) * 7 + (vector,) * 2,
        check_vma=False,
    )
```

```python
import functools

import jax
import jax.numpy as jnp
from jax import lax
from jax.experimental import pallas as pl
from jax.experimental.pallas import tpu as pltpu
from jax.sharding import PartitionSpec as P

HEADS = 16
EPSILON = 1e-05
NEGATIVE = -1e30
ROPE_BASE = 10000.0
BF16 = jnp.bfloat16
F32 = jnp.float32
VMEM_LIMIT = 60 * 1024 * 1024


def dot(left, right, contract):
    return lax.dot_general(
        left, right, ((contract[:1], contract[1:]), ((), ())), preferred_element_type=F32
    )


def norm_rows(values):
    scale = lax.rsqrt(jnp.mean(values * values, axis=-1, keepdims=True) + EPSILON)
    return (values * scale, scale)


def norm_back(gradient, normed, scale):
    return scale * (gradient - normed * jnp.mean(gradient * normed, axis=-1, keepdims=True))


def rope_lanes(positions, lanes, head_dim):
    half = head_dim // 2
    lane = jnp.arange(lanes, dtype=jnp.int32) % head_dim
    frequency = ROPE_BASE ** (-2.0 * (lane % half).astype(F32) / head_dim)
    angles = positions.astype(F32)[:, None] * frequency[None, :]
    sign = jnp.where(lane < half, 1.0, -1.0).astype(F32)
    return (jnp.cos(angles), jnp.sin(angles) * sign[None, :])


def partner(values, head_dim, roll):
    half = head_dim // 2
    lane = lax.broadcasted_iota(jnp.int32, values.shape, values.ndim - 1) % head_dim
    return jnp.where(lane < half, roll(values, half), roll(values, -half))


def lane_roll(values, shift):
    return jnp.roll(values, -shift, axis=-1)


def kernel_roll(values, shift):
    width = values.shape[-1]
    if width % 128 == 0:
        return pltpu.roll(values, (-shift) % width, axis=values.ndim - 1)
    shift = shift % width
    return jnp.concatenate([values[..., shift:], values[..., :shift]], axis=-1)


def head_rows(values, head, head_dim):
    if values.shape[-1] == head_dim:
        return values
    lane = lax.broadcasted_iota(jnp.int32, values.shape, values.ndim - 1)
    mine = (lane >= head * head_dim) & (lane < (head + 1) * head_dim)
    return jnp.where(mine, values, jnp.zeros_like(values))


def masked_scores(key_block, query_block, key_start, query_start, prefix):
    scores = dot(key_block, query_block, (1, 1))
    query_pos = query_start + lax.broadcasted_iota(jnp.int32, (1, scores.shape[1]), 1)
    last = jnp.maximum(query_pos, prefix - 1) - key_start
    key_pos = lax.broadcasted_iota(jnp.int32, scores.shape, 0)
    return jnp.where(key_pos <= last, scores, NEGATIVE)


def attend_kernel(
    head_dim, bq, bk, prefix_ref, q_ref, k_ref, v_ref, att_ref, att_t_ref, mass_ref, v_t, acc
):
    length, width = q_ref.shape
    heads = width // head_dim
    prefix = prefix_ref[0]
    for start in range(0, length, 128):
        v_t[:, start : start + 128] = v_ref[start : start + 128, :].T

    def query_step(i, carry):
        q0 = pl.multiple_of(i * bq, bq)
        q_all = q_ref[pl.ds(q0, bq), :]
        q_heads = [head_rows(q_all, h, head_dim) for h in range(heads)]
        acc[...] = jnp.zeros_like(acc)
        blocks = (jnp.maximum(q0 + bq, prefix) + bk - 1) // bk

        def key_step(j, stats):
            k0 = pl.multiple_of(j * bk, bk)
            k_block = k_ref[pl.ds(k0, bk), :]
            out = []
            for h in range(heads):
                peak, mass = stats[h]
                scores = masked_scores(k_block, q_heads[h], k0, q0, prefix)
                new_peak = jnp.maximum(peak, jnp.max(scores, axis=0, keepdims=True))
                alpha = jnp.exp(peak - new_peak)
                weights = jnp.exp(scores - new_peak)
                mass = mass * alpha + jnp.sum(weights, axis=0, keepdims=True)
                rows = slice(h * head_dim, (h + 1) * head_dim)
                acc[rows, :] = acc[rows, :] * alpha + dot(
                    v_t[rows, pl.ds(k0, bk)], weights.astype(BF16), (1, 0)
                )
                out.append((new_peak, mass))
            return tuple(out)

        first = tuple(
            (jnp.full((1, bq), NEGATIVE, F32), jnp.zeros((1, bq), F32)) for _ in range(heads)
        )
        stats = lax.fori_loop(0, blocks, key_step, first)
        for h in range(heads):
            peak, mass = stats[h]
            rows = slice(h * head_dim, (h + 1) * head_dim)
            att_t_ref[rows, pl.ds(q0, bq)] = acc[rows, :] / mass
            mass_ref[h : h + 1, pl.ds(q0, bq)] = peak + jnp.log(mass)
        for part in range(0, bq, 128):
            place = pl.ds(pl.multiple_of(q0 + part, 128), 128)
            att_ref[place, :] = att_t_ref[:, place].T.astype(BF16)
        return carry

    lax.fori_loop(0, length // bq, query_step, 0)


def attend_back_kernel(
    head_dim,
    bq,
    bk,
    prefix_ref,
    q_ref,
    k_ref,
    v_ref,
    do_ref,
    att_t_ref,
    mass_ref,
    cos_ref,
    sin_ref,
    out_ref,
    k_t,
    delta,
    dq_t,
    dk_acc,
    dv_acc,
):
    length, width = q_ref.shape
    heads = width // head_dim
    prefix = prefix_ref[0]
    dq_t[...] = jnp.zeros_like(dq_t)
    for start in range(0, length, 128):
        place = slice(start, start + 128)
        k_t[:, place] = k_ref[place, :].T
        product = do_ref[place, :].astype(F32).T * att_t_ref[:, place]
        for h in range(heads):
            rows = slice(h * head_dim, (h + 1) * head_dim)
            delta[h : h + 1, place] = jnp.sum(product[rows, :], axis=0, keepdims=True)

    def rope_back(gradient, place):
        return gradient * cos_ref[place, :] + partner(gradient, head_dim, kernel_roll) * sin_ref[
            place, :
        ]

    def key_step(j, carry):
        k0 = pl.multiple_of(j * bk, bk)
        k_block = k_ref[pl.ds(k0, bk), :]
        v_block = v_ref[pl.ds(k0, bk), :]
        dk_acc[...] = jnp.zeros_like(dk_acc)
        dv_acc[...] = jnp.zeros_like(dv_acc)
        begin = jnp.where(k0 < prefix, 0, k0 // bq)

        def query_step(i, inner):
            q0 = pl.multiple_of(i * bq, bq)
            q_all = q_ref[pl.ds(q0, bq), :]
            do_all = do_ref[pl.ds(q0, bq), :]
            for h in range(heads):
                rows = slice(h * head_dim, (h + 1) * head_dim)
                q_head = head_rows(q_all, h, head_dim)
                do_head = head_rows(do_all, h, head_dim)
                scores = masked_scores(k_block, q_head, k0, q0, prefix)
                weights = jnp.exp(scores - mass_ref[h : h + 1, pl.ds(q0, bq)])
                grad_weights = dot(v_block, do_head, (1, 1))
                grad_scores = (weights * (grad_weights - delta[h : h + 1, pl.ds(q0, bq)])).astype(
                    BF16
                )
                dv_acc[...] += dot(weights.astype(BF16), do_head, (1, 0))
                dk_acc[...] += dot(grad_scores, q_head, (1, 0))
                dq_t[rows, pl.ds(q0, bq)] += dot(k_t[rows, pl.ds(k0, bk)], grad_scores, (1, 0))
            return inner

        lax.fori_loop(begin, length // bq, query_step, 0)
        place = pl.ds(k0, bk)
        out_ref[place, width : 2 * width] = rope_back(dk_acc[...], place).astype(BF16)
        out_ref[place, 2 * width :] = dv_acc[...].astype(BF16) * jnp.array(0.5, BF16)
        return carry

    lax.fori_loop(0, length // bk, key_step, 0)
    for start in range(0, length, 128):
        place = slice(start, start + 128)
        out_ref[place, :width] = rope_back(dq_t[:, place].T * 0.125, place).astype(BF16)


def turns(reps, move):
    pairs = []
    for here in range(reps):
        z, y, core = move(here // 4, (here // 2) % 2, here % 2)
        pairs.append((here, (z % (reps // 4)) * 4 + y * 2 + core))
    return pairs


class Links:
    def __init__(self, reps):
        self.deep = reps // 4
        self.to_core = turns(reps, lambda z, y, core: (z, y, 1 - core))
        self.to_y = turns(reps, lambda z, y, core: (z, 1 - y, core))
        self.to_z = turns(reps, lambda z, y, core: (z + 1, y, core))
        here = lax.axis_index("rep")
        self.z, self.y, self.core = here // 4, (here // 2) % 2, here % 2
        self.x = lax.axis_index("shard")

    def over_core(self, value):
        return lax.ppermute(value, "rep", self.to_core)

    def over_x(self, value):
        return lax.ppermute(value, "shard", [(0, 1), (1, 0)])

    def over_y(self, value):
        return lax.ppermute(value, "rep", self.to_y)

    def next_z(self, value):
        return lax.ppermute(value, "rep", self.to_z)

    def half(self, total, side):
        return pick(total.reshape(2, -1, total.shape[1]), side)

    def quarters(self, total, side):
        columns = total.shape[1]
        return pick(total.reshape(2, 2, -1, columns), side, 1).reshape(-1, columns)

    def part(self, total, turn):
        return pick(total.reshape(self.deep, -1, total.shape[1]), (self.z + turn) % self.deep)

    def ring_start(self, total):
        return self.next_z(self.part(total, self.deep - 1))

    def ring_step(self, total, arrived, step):
        return add(self.part(total, 2 * self.deep - 2 - step), arrived)

    def along_z(self, total):
        arrived = self.ring_start(total)
        for step in range(self.deep - 1):
            moving = self.ring_step(total, arrived, step)
            if step < self.deep - 2:
                arrived = self.next_z(moving)
        return moving

    def collect(self, piece):
        deep = self.deep
        whole_z = blank((deep,) + piece.shape, piece.dtype)
        for step in range(deep):
            whole_z = put(whole_z, piece, (self.z + deep - step) % deep)
            if step < deep - 1:
                piece = self.next_z(piece)
        whole_z = whole_z.reshape(-1, piece.shape[1])
        halves = join(whole_z, self.over_y(whole_z), self.y).reshape(-1, piece.shape[1])
        return join(halves, self.over_core(halves), self.core)


def pick(values, index, axis=0):
    return lax.dynamic_index_in_dim(values, index, axis, keepdims=False)


def put(values, part, index):
    return lax.dynamic_update_index_in_dim(values, part, index, 0)


def join(mine, other, index):
    both = blank((2,) + mine.shape, mine.dtype)
    return put(put(both, mine, index), other, 1 - index)


def fence(*values):
    return lax.optimization_barrier(values)


def after(value, *earlier):
    return lax.optimization_barrier((value,) + earlier)[0]


def blank(shape, dtype):
    return pl.pallas_call(
        lambda out_ref: None,
        out_shape=jax.ShapeDtypeStruct(shape, dtype),
        out_specs=pl.BlockSpec(memory_space=pl.ANY),
    )()


def add(left, right):
    return (left.astype(F32) + right.astype(F32)).astype(BF16)


def whole(shape):
    return pl.BlockSpec(shape, lambda *_: (0,) * len(shape))


def thirds(qkv):
    length, width = qkv.shape[0], qkv.shape[1] // 3
    if width % 128 == 0:
        specs = [pl.BlockSpec((length, width), lambda *_, at=at: (0, at)) for at in range(3)]
        return (qkv, qkv, qkv), specs
    parts = tuple(qkv[:, at * width : (at + 1) * width] for at in range(3))
    return parts, [whole((length, width))] * 3


def attend(prefix, qkv, head_dim, bq, bk):
    length, width = qkv.shape[0], qkv.shape[1] // 3
    heads = width // head_dim
    flops = 2 * 2 * heads * length * length * head_dim
    operands, specs = thirds(qkv)
    return pl.pallas_call(
        functools.partial(attend_kernel, head_dim, bq, bk),
        out_shape=(
            jax.ShapeDtypeStruct((length, width), BF16),
            jax.ShapeDtypeStruct((width, length), F32),
            jax.ShapeDtypeStruct((heads, length), F32),
        ),
        grid_spec=pltpu.PrefetchScalarGridSpec(
            num_scalar_prefetch=1,
            grid=(1,),
            in_specs=specs,
            out_specs=[whole((length, width)), whole((width, length)), whole((heads, length))],
            scratch_shapes=[pltpu.VMEM((width, length), BF16), pltpu.VMEM((width, bq), F32)],
        ),
        compiler_params=pltpu.CompilerParams(vmem_limit_bytes=VMEM_LIMIT),
        cost_estimate=pl.CostEstimate(
            flops=flops, transcendentals=heads * length * length, bytes_accessed=8 * length * width
        ),
    )(prefix, *operands)


def attend_back(prefix, qkv, do, att_t, mass, cosine, sine, head_dim, bq, bk):
    length, width = qkv.shape[0], qkv.shape[1] // 3
    heads = width // head_dim
    flops = 5 * 2 * heads * length * length * head_dim
    rows = whole((length, width))
    operands, specs = thirds(qkv)
    return pl.pallas_call(
        functools.partial(attend_back_kernel, head_dim, bq, bk),
        out_shape=jax.ShapeDtypeStruct((length, 3 * width), BF16),
        grid_spec=pltpu.PrefetchScalarGridSpec(
            num_scalar_prefetch=1,
            grid=(1,),
            in_specs=specs + [rows, whole((width, length)), whole((heads, length)), rows, rows],
            out_specs=whole((length, 3 * width)),
            scratch_shapes=[
                pltpu.VMEM((width, length), BF16),
                pltpu.VMEM((heads, length), F32),
                pltpu.VMEM((width, length), F32),
                pltpu.VMEM((bk, width), F32),
                pltpu.VMEM((bk, width), F32),
            ],
        ),
        compiler_params=pltpu.CompilerParams(vmem_limit_bytes=VMEM_LIMIT),
        cost_estimate=pl.CostEstimate(
            flops=flops, transcendentals=heads * length * length, bytes_accessed=22 * length * width
        ),
    )(prefix, *operands, do, att_t, mass, cosine, sine)


def spread_kernel(lanes, in_ref, wq_ref, wk_ref, wv_ref, q_ref, k_ref, v_ref, sum_ref):
    total = None
    for at, (w_ref, out_ref) in enumerate(((wq_ref, q_ref), (wk_ref, k_ref), (wv_ref, v_ref))):
        part = in_ref[0, :, at * lanes : (at + 1) * lanes].astype(F32)
        out_ref[...] = part
        term = part * w_ref[...].astype(F32)
        total = term if total is None else total + term

    @pl.when(pl.program_id(1) == 0)
    def _():
        sum_ref[...] = total

    @pl.when(pl.program_id(1) > 0)
    def _():
        sum_ref[...] += total


def spread(gathered, w_query, w_key, w_value, seqs, groups):
    height, width = w_query.shape
    share, lanes = height // seqs, width // groups
    tile = pl.BlockSpec((share, lanes), lambda s, g: (s, g))
    return pl.pallas_call(
        functools.partial(spread_kernel, lanes),
        out_shape=(jax.ShapeDtypeStruct((height, width), F32),) * 3
        + (jax.ShapeDtypeStruct((height, lanes), F32),),
        grid=(seqs, groups),
        in_specs=[
            pl.BlockSpec((1, share, 3 * lanes), lambda s, g: (s * groups + g, 0, 0)),
            tile,
            tile,
            tile,
        ],
        out_specs=[tile, tile, tile, pl.BlockSpec((share, lanes), lambda s, g: (s, 0))],
        cost_estimate=pl.CostEstimate(
            flops=6 * height * width, transcendentals=0, bytes_accessed=24 * height * width
        ),
    )(gathered.reshape(seqs * groups, share, 3 * lanes), w_query, w_key, w_value)


class Layer:
    def __init__(self, reps, tokens, prefix_len):
        self.reps = reps
        self.seqs, self.rows, self.width = tokens.shape
        self.head_dim = self.width // HEADS
        self.length = self.rows * reps
        self.groups = reps // self.seqs
        self.lanes = self.width // self.groups
        self.total = self.seqs * self.rows
        self.block = min(512, self.length)
        here = lax.axis_index("rep")
        self.my_seq = here // self.groups
        positions = here * self.rows + jnp.arange(self.rows, dtype=jnp.int32)
        cosine, sine = rope_lanes(positions, self.width, self.head_dim)
        self.cosine = jnp.tile(cosine, (self.seqs, 1))
        self.sine = jnp.tile(sine, (self.seqs, 1))
        self.all_tables = rope_lanes(
            jnp.arange(self.length, dtype=jnp.int32), self.lanes, self.head_dim
        )
        self.prefix = lax.dynamic_slice_in_dim(prefix_len, self.my_seq, 1, 0)

    def to_heads(self, values, parts):
        shape = (self.seqs, self.rows, parts, self.groups, self.lanes)
        chunks = values.reshape(shape).transpose(0, 3, 1, 2, 4)
        chunks = chunks.reshape(self.reps * self.rows, parts * self.lanes)
        return lax.all_to_all(chunks, "rep", 0, 0, tiled=True)

    def to_tokens(self, values, parts):
        chunks = lax.all_to_all(values, "rep", 0, 0, tiled=True)
        chunks = chunks.reshape(self.seqs, self.groups, self.rows, parts, self.lanes)
        return chunks.transpose(0, 2, 3, 1, 4).reshape(self.total, parts * self.width)

    def project(self, hidden, full_qkv, first_values):
        width = self.width
        raw = dot(hidden, full_qkv, (1, 0))

        def rope(values):
            return values * self.cosine - partner(values, self.head_dim, lane_roll) * self.sine

        query_rot = (rope(raw[:, :width]) * 0.125).astype(BF16)
        key_rot = rope(raw[:, width : 2 * width]).astype(BF16)
        first = first_values.reshape(self.total, width).astype(F32)
        value_mix = (0.5 * raw[:, 2 * width :] + 0.5 * first).astype(BF16)
        return jnp.concatenate([query_rot, key_rot, value_mix], axis=1)

    def attend(self, qkv):
        return attend(self.prefix, qkv, self.head_dim, self.block, self.block)

    def attend_back(self, qkv, do, att_t, mass):
        return attend_back(
            self.prefix, qkv, do, att_t, mass, *self.all_tables, self.head_dim, self.block, self.block
        )

    def sum_sequences(self, columns):
        share = columns.shape[0] // self.seqs
        mine = lax.dynamic_slice_in_dim(columns, self.my_seq * share, share, 0).astype(F32)
        for turn in range(1, self.seqs):
            slot = (self.my_seq + turn) % self.seqs
            sent = lax.dynamic_slice_in_dim(columns, slot * share, share, 0)
            moves = [
                (s * self.groups + g, ((s + turn) % self.seqs) * self.groups + g)
                for s in range(self.seqs)
                for g in range(self.groups)
            ]
            mine = mine + lax.ppermute(sent, "rep", moves).astype(F32)
        return mine.astype(BF16)


def gain_gradient(gain, *pairs):
    total = sum(jnp.sum(w.astype(F32) * gradient, axis=1) for w, gradient in pairs)
    return total / gain.astype(F32)


def gate_back(grad_swiglu, gate_pre, up_pre, sigma, swish):
    grad_gate_pre = grad_swiglu * up_pre * sigma * (1.0 + gate_pre * (1.0 - sigma))
    return (grad_gate_pre.astype(BF16), (grad_swiglu * swish).astype(BF16))


def local(
    reps,
    tokens,
    first_values,
    prefix_len,
    cotangent,
    w_query,
    w_key,
    w_value,
    w_output,
    w_gate,
    w_up,
    w_down,
    gain_attn,
    gain_ffn,
):
    layer = Layer(reps, tokens, prefix_len)
    total, width, ff = layer.total, layer.width, w_gate.shape[1]
    here = lax.axis_index("rep")

    def gather(weights):
        height = weights[0].shape[0]
        share = height // reps
        if share * reps == height and share % 8 == 0:
            pieces = [lax.dynamic_slice_in_dim(w, here * share, share, 0) for w in weights]
            axes = ("shard", "rep")
        else:
            pieces, axes = list(weights), ("shard",)
        piece = pieces[0] if len(pieces) == 1 else jnp.concatenate(pieces, axis=1)
        return lax.all_gather(piece, axes, axis=0, tiled=True)

    gains = lax.all_gather(jnp.stack([gain_attn, gain_ffn]), "shard", axis=1, tiled=True)
    full_qkv = gather((w_query, w_key, w_value))
    full_output = gather((w_output,))
    full_gate_up = gather((w_gate, w_up))
    full_down = gather((w_down,))
    gain1 = gains[0].astype(F32)
    gain2 = gains[1].astype(F32)

    inputs = tokens.reshape(total, width).astype(F32)
    normed1, scale1 = norm_rows(inputs)
    hidden1 = (normed1 * gain1).astype(BF16)
    hidden1_all = lax.all_gather(hidden1.reshape(tokens.shape), "rep", axis=1, tiled=True)
    qkv = layer.to_heads(layer.project(hidden1, full_qkv, first_values), 3)
    att, att_t, mass = layer.attend(qkv)
    attended = layer.to_tokens(att, 1)

    residual = inputs + dot(attended, full_output, (1, 0))
    normed2, scale2 = norm_rows(residual)
    hidden2 = (normed2 * gain2).astype(BF16)
    gate_up = dot(hidden2, full_gate_up, (1, 0))
    gate_pre, up_pre = gate_up[:, :ff], gate_up[:, ff:]
    sigma = jax.nn.sigmoid(gate_pre)
    swish = gate_pre * sigma
    swiglu = (swish * up_pre).astype(BF16)
    output = (residual + dot(swiglu, full_down, (1, 0))).astype(BF16)

    upstream = cotangent.reshape(total, width)
    grad_swiglu = dot(upstream, full_down, (1, 1))
    grad_gate_up = jnp.concatenate(gate_back(grad_swiglu, gate_pre, up_pre, sigma, swish), axis=1)
    grad_hidden2 = dot(grad_gate_up, full_gate_up, (1, 1))
    grad_residual = upstream.astype(F32) + norm_back(grad_hidden2 * gain2, normed2, scale2)
    grad_residual_low = grad_residual.astype(BF16)
    grad_attended = dot(grad_residual_low, full_output, (1, 1)).astype(BF16)

    def reduce_gather(partial):
        axes = ("shard", "rep")
        piece = lax.psum_scatter(partial.astype(BF16), axes, scatter_dimension=0, tiled=True)
        return lax.all_gather(piece, "rep", axis=0, tiled=True).astype(F32)

    grad_down = reduce_gather(dot(swiglu, upstream, (0, 0)))
    grad_wgate_up = reduce_gather(dot(hidden2, grad_gate_up, (0, 0)))
    grad_outproj = reduce_gather(dot(attended, grad_residual_low, (0, 0)))
    grad_wgate, grad_wup = grad_wgate_up[:, :ff], grad_wgate_up[:, ff:]

    do = layer.to_heads(grad_attended, 1)
    grad_raw_heads = layer.attend_back(qkv, do, att_t, mass)
    grad_raw = layer.to_tokens(grad_raw_heads, 3)
    grad_first = grad_raw[:, 2 * width :].astype(F32)
    grad_hidden1 = dot(grad_raw, full_qkv, (1, 1))
    grad_inputs = grad_residual + norm_back(grad_hidden1 * gain1, normed1, scale1)

    hidden_mine = lax.dynamic_index_in_dim(hidden1_all, layer.my_seq, 0, keepdims=False)
    columns = dot(hidden_mine, grad_raw_heads, (0, 0)).astype(BF16)
    columns = lax.psum_scatter(columns, "shard", scatter_dimension=0, tiled=True)
    height = columns.shape[0]
    mine = layer.sum_sequences(columns)
    gathered = lax.all_gather(mine, "rep", axis=0, tiled=True)
    gathered = gathered.reshape(layer.seqs, layer.groups, -1, 3, layer.lanes)
    grad_wqkv = gathered.transpose(3, 0, 2, 1, 4).reshape(3, height, width).astype(F32)
    shape = tokens.shape
    return (
        output.reshape(shape),
        grad_inputs.reshape(shape),
        grad_first.reshape(shape),
        grad_wqkv[0],
        grad_wqkv[1],
        grad_wqkv[2],
        grad_outproj,
        grad_wgate,
        grad_wup,
        grad_down,
        gain_gradient(
            gain_attn, (w_query, grad_wqkv[0]), (w_key, grad_wqkv[1]), (w_value, grad_wqkv[2])
        ),
        gain_gradient(gain_ffn, (w_gate, grad_wgate), (w_up, grad_wup)),
    )


def local_linked(
    reps,
    tokens,
    first_values,
    prefix_len,
    cotangent,
    w_query,
    w_key,
    w_value,
    w_output,
    w_gate,
    w_up,
    w_down,
    gain_attn,
    gain_ffn,
):
    layer = Layer(reps, tokens, prefix_len)
    links = Links(reps)
    total, width, ff = layer.total, layer.width, w_gate.shape[1]
    core, x = links.core, links.x

    own_gains = jnp.stack([gain_attn, gain_ffn])
    other_gains = links.over_x(own_gains)
    gains = jnp.where(
        x == 0,
        jnp.concatenate([own_gains, other_gains], axis=1),
        jnp.concatenate([other_gains, own_gains], axis=1),
    )
    gain1 = gains[0].astype(F32)
    gain2 = gains[1].astype(F32)

    def half_rows(weights):
        half = weights[0].shape[0] // 2
        pieces = [lax.dynamic_slice_in_dim(w, core * half, half, 0) for w in weights]
        return pieces[0] if len(pieces) == 1 else jnp.concatenate(pieces, axis=1)

    def assemble(weights, near, far, at):
        height = weights[0].shape[0]
        half = near.shape[0]
        columns = sum(w.shape[1] for w in weights)
        full = blank((2 * height, columns), BF16)
        place = 0
        for w in weights:
            full = lax.dynamic_update_slice(full, w, (x * height, place))
            place += w.shape[1]
        for part, owner in ((near, core), (far, 1 - core)):
            part = lax.slice_in_dim(part, at, at + columns, axis=1)
            full = lax.dynamic_update_slice(full, part, ((1 - x) * height + owner * half, 0))
        return full

    near_qkv = links.over_x(after(half_rows((w_query, w_key, w_value)), other_gains))
    near_ff = links.over_x(after(half_rows((w_output, w_gate, w_up)), near_qkv))
    near_down = links.over_x(after(half_rows((w_down,)), near_ff))
    full_qkv = assemble((w_query, w_key, w_value), near_qkv, links.over_core(near_qkv), 0)

    inputs = tokens.reshape(total, width).astype(F32)
    normed1, scale1 = norm_rows(inputs)
    hidden1 = (normed1 * gain1).astype(BF16)
    hidden1_all = lax.all_gather(hidden1.reshape(tokens.shape), "rep", axis=1, tiled=True)
    qkv = layer.to_heads(layer.project(hidden1, full_qkv, first_values), 3)
    qkv, hidden1_all = fence(qkv, hidden1_all)
    att, att_t, mass = layer.attend(qkv)
    att, near_ff = fence(att, near_ff)
    far_ff = links.over_core(near_ff)
    full_output = assemble((w_output,), near_ff, far_ff, 0)
    full_gate_up = assemble((w_gate, w_up), near_ff, far_ff, w_output.shape[1])
    attended = layer.to_tokens(att, 1)

    residual = inputs + dot(attended, full_output, (1, 0))
    normed2, scale2 = norm_rows(residual)
    hidden2 = (normed2 * gain2).astype(BF16)
    gate_up = dot(hidden2, full_gate_up, (1, 0))
    gate_pre, up_pre = gate_up[:, :ff], gate_up[:, ff:]
    sigma = jax.nn.sigmoid(gate_pre)
    swish = gate_pre * sigma
    swiglu = (swish * up_pre).astype(BF16)
    upstream = cotangent.reshape(total, width)

    def by_core(values, blocks):
        step = values.shape[1] // (2 * blocks)
        sides = [
            [values[:, (2 * b + side) * step : (2 * b + side + 1) * step] for b in range(blocks)]
            for side in range(2)
        ]
        low, high = (s[0] if blocks == 1 else jnp.concatenate(s, axis=1) for s in sides)
        return jnp.where(core == 0, low, high), jnp.where(core == 0, high, low)

    upstream_mine, upstream_other = by_core(upstream, 1)
    down_send = dot(swiglu, upstream_other, (0, 0)).astype(BF16)
    swiglu, down_send, near_down = fence(swiglu, down_send, near_down)
    full_down = assemble((w_down,), near_down, links.over_core(near_down), 0)
    grad_swiglu = dot(upstream, full_down, (1, 1))
    grad_gate_pre, grad_up_pre = gate_back(grad_swiglu, gate_pre, up_pre, sigma, swish)
    down_total = add(dot(swiglu, upstream_mine, (0, 0)), links.over_core(down_send))
    down_total, grad_gate_pre, grad_up_pre = fence(down_total, grad_gate_pre, grad_up_pre)

    hidden2_mine, hidden2_other = by_core(hidden2, 2)
    down_x = links.over_x(links.half(down_total, 1 - x))
    gate_send = dot(hidden2_other, grad_gate_pre, (0, 0)).astype(BF16)
    gate_total = add(dot(hidden2_mine, grad_gate_pre, (0, 0)), links.over_core(gate_send))
    gate_total, grad_gate_pre, grad_up_pre = fence(gate_total, grad_gate_pre, grad_up_pre)
    gate_y = links.over_y(links.quarters(gate_total, 1 - links.y))
    grad_gate_up = jnp.concatenate([grad_gate_pre, grad_up_pre], axis=1)
    up_send = dot(hidden2_other, grad_up_pre, (0, 0)).astype(BF16)
    grad_hidden2 = dot(grad_gate_up, full_gate_up, (1, 1))
    grad_residual = upstream.astype(F32) + norm_back(grad_hidden2 * gain2, normed2, scale2)
    grad_residual_low = grad_residual.astype(BF16)
    grad_attended = dot(grad_residual_low, full_output, (1, 1)).astype(BF16)
    up_total = add(dot(hidden2_mine, grad_up_pre, (0, 0)), links.over_core(up_send))
    attended_mine, attended_other = by_core(attended, 2)
    out_send = dot(attended_other, grad_residual_low, (0, 0)).astype(BF16)
    out_total = add(dot(attended_mine, grad_residual_low, (0, 0)), links.over_core(out_send))
    down_first = add(links.half(down_total, x), down_x)
    down_first, up_total, out_total, grad_attended = fence(
        down_first, up_total, out_total, grad_attended
    )

    up_x = links.over_x(links.half(up_total, 1 - x))
    down_y = links.over_y(links.half(down_first, 1 - links.y))
    do = layer.to_heads(grad_attended, 1)
    output = (residual + dot(swiglu, full_down, (1, 0))).astype(BF16)
    gate_first = add(links.quarters(gate_total, links.y), gate_y)
    down_second = add(links.half(down_first, links.y), down_y)
    do, gate_first, down_second, output = fence(do, gate_first, down_second, output)

    gate_x = links.over_x(links.half(gate_first, 1 - x))
    out_y = links.over_y(links.quarters(out_total, 1 - links.y))
    down_ring = links.ring_start(down_second)
    grad_raw_heads = layer.attend_back(qkv, do, att_t, mass)
    down_ring = links.ring_step(down_second, down_ring, 0)
    up_first = add(links.half(up_total, x), up_x)
    out_first = add(links.quarters(out_total, links.y), out_y)
    gate_second = add(links.half(gate_first, x), gate_x)
    grad_raw_heads, down_ring, up_first, out_first, gate_second = fence(
        grad_raw_heads, down_ring, up_first, out_first, gate_second
    )

    grad_raw = layer.to_tokens(grad_raw_heads, 3)
    hidden_mine = lax.dynamic_index_in_dim(hidden1_all, layer.my_seq, 0, keepdims=False)
    columns = dot(hidden_mine, grad_raw_heads, (0, 0)).astype(BF16)
    columns = add(links.half(columns, x), links.over_x(links.half(columns, 1 - x)))
    gathered = lax.all_gather(layer.sum_sequences(columns), "rep", axis=0, tiled=True)
    up_second = add(links.half(up_first, links.y), links.over_y(links.half(up_first, 1 - links.y)))
    out_second = add(links.half(out_first, x), links.over_x(links.half(out_first, 1 - x)))
    for step in range(1, links.deep - 1):
        down_ring = links.ring_step(down_second, links.next_z(down_ring), step)
    halves = links.collect(down_ring)
    grad_down = jnp.concatenate([halves[0], halves[1]], axis=1).astype(F32)
    grad_wgate = links.collect(links.along_z(gate_second)).reshape(-1, ff).astype(F32)
    grad_wup = links.collect(links.along_z(up_second)).reshape(-1, ff).astype(F32)
    grad_outproj = links.collect(links.along_z(out_second)).reshape(-1, width).astype(F32)

    grad_first = grad_raw[:, 2 * width :].astype(F32)
    grad_hidden1 = dot(grad_raw, full_qkv, (1, 1))
    grad_inputs = grad_residual + norm_back(grad_hidden1 * gain1, normed1, scale1)
    grad_wquery, grad_wkey, grad_wvalue, sums = spread(
        gathered, w_query, w_key, w_value, layer.seqs, layer.groups
    )
    shape = tokens.shape
    return (
        output.reshape(shape),
        grad_inputs.reshape(shape),
        grad_first.reshape(shape),
        grad_wquery,
        grad_wkey,
        grad_wvalue,
        grad_outproj,
        grad_wgate,
        grad_wup,
        grad_down,
        jnp.sum(sums, axis=1) / gain_attn.astype(F32),
        gain_gradient(gain_ffn, (w_gate, grad_wgate), (w_up, grad_wup)),
    )


def solution(mesh):
    sequence = P("shard", "rep", None)
    matrix = P("shard", None)
    vector = P("shard")
    reps, shards = mesh.shape["rep"], mesh.shape["shard"]
    linked = reps == 16 and shards == 2
    return jax.shard_map(
        functools.partial(local_linked if linked else local, reps),
        mesh=mesh,
        in_specs=(sequence, sequence, vector, sequence) + (matrix,) * 7 + (vector,) * 2,
        out_specs=(sequence,) * 3 + (matrix,) * 7 + (vector,) * 2,
        check_vma=False,
    )
```

```python
import functools

import jax
import jax.numpy as jnp
from jax import lax
from jax.experimental import pallas as pl
from jax.experimental.pallas import tpu as pltpu
from jax.sharding import PartitionSpec as P

HEADS = 16
EPSILON = 1e-05
NEGATIVE = -1e30
ROPE_BASE = 10000.0
BF16 = jnp.bfloat16
F32 = jnp.float32
VMEM_LIMIT = 60 * 1024 * 1024


def dot(left, right, contract):
    return lax.dot_general(
        left, right, ((contract[:1], contract[1:]), ((), ())), preferred_element_type=F32
    )


def norm_rows(values):
    scale = lax.rsqrt(jnp.mean(values * values, axis=-1, keepdims=True) + EPSILON)
    return (values * scale, scale)


def norm_back(gradient, normed, scale):
    return scale * (gradient - normed * jnp.mean(gradient * normed, axis=-1, keepdims=True))


def rope_lanes(positions, lanes, head_dim):
    half = head_dim // 2
    lane = jnp.arange(lanes, dtype=jnp.int32) % head_dim
    frequency = ROPE_BASE ** (-2.0 * (lane % half).astype(F32) / head_dim)
    angles = positions.astype(F32)[:, None] * frequency[None, :]
    sign = jnp.where(lane < half, 1.0, -1.0).astype(F32)
    return (jnp.cos(angles), jnp.sin(angles) * sign[None, :])


def partner(values, head_dim, roll):
    half = head_dim // 2
    lane = lax.broadcasted_iota(jnp.int32, values.shape, values.ndim - 1) % head_dim
    return jnp.where(lane < half, roll(values, half), roll(values, -half))


def lane_roll(values, shift):
    return jnp.roll(values, -shift, axis=-1)


def kernel_roll(values, shift):
    width = values.shape[-1]
    if width % 128 == 0:
        return pltpu.roll(values, (-shift) % width, axis=values.ndim - 1)
    shift = shift % width
    return jnp.concatenate([values[..., shift:], values[..., :shift]], axis=-1)


def head_rows(values, head, head_dim):
    if values.shape[-1] == head_dim:
        return values
    lane = lax.broadcasted_iota(jnp.int32, values.shape, values.ndim - 1)
    mine = (lane >= head * head_dim) & (lane < (head + 1) * head_dim)
    return jnp.where(mine, values, jnp.zeros_like(values))


def masked_scores(key_block, query_block, key_start, query_start, prefix):
    scores = dot(key_block, query_block, (1, 1))
    query_pos = query_start + lax.broadcasted_iota(jnp.int32, (1, scores.shape[1]), 1)
    last = jnp.maximum(query_pos, prefix - 1) - key_start
    key_pos = lax.broadcasted_iota(jnp.int32, scores.shape, 0)
    return jnp.where(key_pos <= last, scores, NEGATIVE)


def attend_kernel(
    head_dim, bq, bk, prefix_ref, q_ref, k_ref, v_ref, att_ref, att_t_ref, mass_ref, v_t, acc
):
    length, width = q_ref.shape
    heads = width // head_dim
    prefix = prefix_ref[0]
    for start in range(0, length, 128):
        v_t[:, start : start + 128] = v_ref[start : start + 128, :].T

    def query_step(i, carry):
        q0 = pl.multiple_of(i * bq, bq)
        q_all = q_ref[pl.ds(q0, bq), :]
        q_heads = [head_rows(q_all, h, head_dim) for h in range(heads)]
        acc[...] = jnp.zeros_like(acc)
        blocks = (jnp.maximum(q0 + bq, prefix) + bk - 1) // bk

        def key_step(j, stats):
            k0 = pl.multiple_of(j * bk, bk)
            k_block = k_ref[pl.ds(k0, bk), :]
            out = []
            for h in range(heads):
                peak, mass = stats[h]
                scores = masked_scores(k_block, q_heads[h], k0, q0, prefix)
                new_peak = jnp.maximum(peak, jnp.max(scores, axis=0, keepdims=True))
                alpha = jnp.exp(peak - new_peak)
                weights = jnp.exp(scores - new_peak)
                mass = mass * alpha + jnp.sum(weights, axis=0, keepdims=True)
                rows = slice(h * head_dim, (h + 1) * head_dim)
                acc[rows, :] = acc[rows, :] * alpha + dot(
                    v_t[rows, pl.ds(k0, bk)], weights.astype(BF16), (1, 0)
                )
                out.append((new_peak, mass))
            return tuple(out)

        first = tuple(
            (jnp.full((1, bq), NEGATIVE, F32), jnp.zeros((1, bq), F32)) for _ in range(heads)
        )
        stats = lax.fori_loop(0, blocks, key_step, first)
        for h in range(heads):
            peak, mass = stats[h]
            rows = slice(h * head_dim, (h + 1) * head_dim)
            att_t_ref[rows, pl.ds(q0, bq)] = acc[rows, :] / mass
            mass_ref[h : h + 1, pl.ds(q0, bq)] = peak + jnp.log(mass)
        for part in range(0, bq, 128):
            place = pl.ds(pl.multiple_of(q0 + part, 128), 128)
            att_ref[place, :] = att_t_ref[:, place].T.astype(BF16)
        return carry

    lax.fori_loop(0, length // bq, query_step, 0)


def attend_back_kernel(
    head_dim,
    bq,
    bk,
    prefix_ref,
    q_ref,
    k_ref,
    v_ref,
    do_ref,
    att_t_ref,
    mass_ref,
    cos_ref,
    sin_ref,
    out_ref,
    k_t,
    delta,
    dq_t,
    dk_acc,
    dv_acc,
):
    length, width = q_ref.shape
    heads = width // head_dim
    prefix = prefix_ref[0]
    dq_t[...] = jnp.zeros_like(dq_t)
    for start in range(0, length, 128):
        place = slice(start, start + 128)
        k_t[:, place] = k_ref[place, :].T
        product = do_ref[place, :].astype(F32).T * att_t_ref[:, place]
        for h in range(heads):
            rows = slice(h * head_dim, (h + 1) * head_dim)
            delta[h : h + 1, place] = jnp.sum(product[rows, :], axis=0, keepdims=True)

    def rope_back(gradient, place):
        return gradient * cos_ref[place, :] + partner(gradient, head_dim, kernel_roll) * sin_ref[
            place, :
        ]

    def key_step(j, carry):
        k0 = pl.multiple_of(j * bk, bk)
        k_block = k_ref[pl.ds(k0, bk), :]
        v_block = v_ref[pl.ds(k0, bk), :]
        dk_acc[...] = jnp.zeros_like(dk_acc)
        dv_acc[...] = jnp.zeros_like(dv_acc)
        begin = jnp.where(k0 < prefix, 0, k0 // bq)

        def query_step(i, inner):
            q0 = pl.multiple_of(i * bq, bq)
            q_all = q_ref[pl.ds(q0, bq), :]
            do_all = do_ref[pl.ds(q0, bq), :]
            for h in range(heads):
                rows = slice(h * head_dim, (h + 1) * head_dim)
                q_head = head_rows(q_all, h, head_dim)
                do_head = head_rows(do_all, h, head_dim)
                scores = masked_scores(k_block, q_head, k0, q0, prefix)
                weights = jnp.exp(scores - mass_ref[h : h + 1, pl.ds(q0, bq)])
                grad_weights = dot(v_block, do_head, (1, 1))
                grad_scores = (weights * (grad_weights - delta[h : h + 1, pl.ds(q0, bq)])).astype(
                    BF16
                )
                dv_acc[...] += dot(weights.astype(BF16), do_head, (1, 0))
                dk_acc[...] += dot(grad_scores, q_head, (1, 0))
                dq_t[rows, pl.ds(q0, bq)] += dot(k_t[rows, pl.ds(k0, bk)], grad_scores, (1, 0))
            return inner

        lax.fori_loop(begin, length // bq, query_step, 0)
        place = pl.ds(k0, bk)
        out_ref[place, width : 2 * width] = rope_back(dk_acc[...], place).astype(BF16)
        out_ref[place, 2 * width :] = dv_acc[...].astype(BF16) * jnp.array(0.5, BF16)
        return carry

    lax.fori_loop(0, length // bk, key_step, 0)
    for start in range(0, length, 128):
        place = slice(start, start + 128)
        out_ref[place, :width] = rope_back(dq_t[:, place].T * 0.125, place).astype(BF16)


def turns(reps, move):
    pairs = []
    for here in range(reps):
        z, y, core = move(here // 4, (here // 2) % 2, here % 2)
        pairs.append((here, (z % (reps // 4)) * 4 + y * 2 + core))
    return pairs


class Links:
    def __init__(self, reps):
        self.to_core = turns(reps, lambda z, y, core: (z, y, 1 - core))
        self.to_y = turns(reps, lambda z, y, core: (z, 1 - y, core))
        self.to_pair = turns(reps, lambda z, y, core: (z ^ 1, y, core))
        self.to_far = turns(reps, lambda z, y, core: (z ^ 2, y, core))
        here = lax.axis_index("rep")
        self.near, self.far = (here // 4) % 2, here // 8
        self.y, self.core = (here // 2) % 2, here % 2
        self.x = lax.axis_index("shard")

    def over_core(self, value):
        return lax.ppermute(value, "rep", self.to_core)

    def over_x(self, value):
        return lax.ppermute(value, "shard", [(0, 1), (1, 0)])

    def over_y(self, value):
        return lax.ppermute(value, "rep", self.to_y)

    def over_pair(self, value):
        return lax.ppermute(value, "rep", self.to_pair)

    def over_far(self, value):
        return lax.ppermute(value, "rep", self.to_far)

    def half(self, total, side):
        return pick(total.reshape(2, -1, total.shape[1]), side)

    def quarters(self, total, side):
        columns = total.shape[1]
        return pick(total.reshape(2, 2, -1, columns), side, 1).reshape(-1, columns)


def pick(values, index, axis=0):
    return lax.dynamic_index_in_dim(values, index, axis, keepdims=False)


def put(values, part, index):
    return lax.dynamic_update_index_in_dim(values, part, index, 0)


def join(mine, other, index):
    first = jnp.concatenate([mine, other], axis=0)
    second = jnp.concatenate([other, mine], axis=0)
    return jnp.where(index == 0, first, second)


def fence(*values):
    return lax.optimization_barrier(values)


def after(value, *earlier):
    return lax.optimization_barrier((value,) + earlier)[0]


def blank(shape, dtype):
    return pl.pallas_call(
        lambda out_ref: None,
        out_shape=jax.ShapeDtypeStruct(shape, dtype),
        out_specs=pl.BlockSpec(memory_space=pl.ANY),
    )()


def add(left, right):
    return (left.astype(F32) + right.astype(F32)).astype(BF16)


def whole(shape):
    return pl.BlockSpec(shape, lambda *_: (0,) * len(shape))


def thirds(qkv):
    length, width = qkv.shape[0], qkv.shape[1] // 3
    if width % 128 == 0:
        specs = [pl.BlockSpec((length, width), lambda *_, at=at: (0, at)) for at in range(3)]
        return (qkv, qkv, qkv), specs
    parts = tuple(qkv[:, at * width : (at + 1) * width] for at in range(3))
    return parts, [whole((length, width))] * 3


def attend(prefix, qkv, head_dim, bq, bk):
    length, width = qkv.shape[0], qkv.shape[1] // 3
    heads = width // head_dim
    flops = 2 * 2 * heads * length * length * head_dim
    operands, specs = thirds(qkv)
    return pl.pallas_call(
        functools.partial(attend_kernel, head_dim, bq, bk),
        out_shape=(
            jax.ShapeDtypeStruct((length, width), BF16),
            jax.ShapeDtypeStruct((width, length), F32),
            jax.ShapeDtypeStruct((heads, length), F32),
        ),
        grid_spec=pltpu.PrefetchScalarGridSpec(
            num_scalar_prefetch=1,
            grid=(1,),
            in_specs=specs,
            out_specs=[whole((length, width)), whole((width, length)), whole((heads, length))],
            scratch_shapes=[pltpu.VMEM((width, length), BF16), pltpu.VMEM((width, bq), F32)],
        ),
        compiler_params=pltpu.CompilerParams(vmem_limit_bytes=VMEM_LIMIT),
        cost_estimate=pl.CostEstimate(
            flops=flops, transcendentals=heads * length * length, bytes_accessed=8 * length * width
        ),
    )(prefix, *operands)


def attend_back(prefix, qkv, do, att_t, mass, cosine, sine, head_dim, bq, bk):
    length, width = qkv.shape[0], qkv.shape[1] // 3
    heads = width // head_dim
    flops = 5 * 2 * heads * length * length * head_dim
    rows = whole((length, width))
    operands, specs = thirds(qkv)
    return pl.pallas_call(
        functools.partial(attend_back_kernel, head_dim, bq, bk),
        out_shape=jax.ShapeDtypeStruct((length, 3 * width), BF16),
        grid_spec=pltpu.PrefetchScalarGridSpec(
            num_scalar_prefetch=1,
            grid=(1,),
            in_specs=specs + [rows, whole((width, length)), whole((heads, length)), rows, rows],
            out_specs=whole((length, 3 * width)),
            scratch_shapes=[
                pltpu.VMEM((width, length), BF16),
                pltpu.VMEM((heads, length), F32),
                pltpu.VMEM((width, length), F32),
                pltpu.VMEM((bk, width), F32),
                pltpu.VMEM((bk, width), F32),
            ],
        ),
        compiler_params=pltpu.CompilerParams(vmem_limit_bytes=VMEM_LIMIT),
        cost_estimate=pl.CostEstimate(
            flops=flops, transcendentals=heads * length * length, bytes_accessed=22 * length * width
        ),
    )(prefix, *operands, do, att_t, mass, cosine, sine)


def spread_kernel(lanes, in_ref, wq_ref, wk_ref, wv_ref, q_ref, k_ref, v_ref, sum_ref):
    total = None
    for at, (w_ref, out_ref) in enumerate(((wq_ref, q_ref), (wk_ref, k_ref), (wv_ref, v_ref))):
        part = in_ref[0, :, at * lanes : (at + 1) * lanes].astype(F32)
        out_ref[...] = part
        term = part * w_ref[...].astype(F32)
        total = term if total is None else total + term

    @pl.when(pl.program_id(1) == 0)
    def _():
        sum_ref[...] = total

    @pl.when(pl.program_id(1) > 0)
    def _():
        sum_ref[...] += total


def spread(gathered, w_query, w_key, w_value, seqs, groups):
    height, width = w_query.shape
    share, lanes = height // seqs, width // groups
    tile = pl.BlockSpec((share, lanes), lambda s, g: (s, g))
    return pl.pallas_call(
        functools.partial(spread_kernel, lanes),
        out_shape=(jax.ShapeDtypeStruct((height, width), F32),) * 3
        + (jax.ShapeDtypeStruct((height, lanes), F32),),
        grid=(seqs, groups),
        in_specs=[
            pl.BlockSpec((1, share, 3 * lanes), lambda s, g: (s * groups + g, 0, 0)),
            tile,
            tile,
            tile,
        ],
        out_specs=[tile, tile, tile, pl.BlockSpec((share, lanes), lambda s, g: (s, 0))],
        cost_estimate=pl.CostEstimate(
            flops=6 * height * width, transcendentals=0, bytes_accessed=24 * height * width
        ),
    )(gathered.reshape(seqs * groups, share, 3 * lanes), w_query, w_key, w_value)


def finish_kernel(count, ff, slots_ref, *refs):
    parts, (gate_ref, up_ref) = refs[:count], refs[count : count + 2]
    grad_gate_ref, grad_up_ref, grad_out_ref, sum_ref, buffer, arrived = refs[-6:]
    step = pl.program_id(0)

    def fetch(at):
        return pltpu.make_async_copy(parts[at], buffer.at[at % 2], arrived.at[at % 2])

    for at in range(count):

        @pl.when(step == max(at - 1, 0))
        def _():
            fetch(at).start()

    for at in range(count):

        @pl.when(step == at)
        def _():
            fetch(at).wait()

    here = lax.rem(step, 2)
    lanes = sum_ref.shape[1]
    total = jnp.zeros(sum_ref.shape, F32)
    for start in range(0, ff, lanes):
        place = slice(start, start + lanes)
        grad_gate = buffer[here, :, place].astype(F32)
        grad_up = buffer[here, :, ff + start : ff + start + lanes].astype(F32)
        grad_gate_ref[:, place] = grad_gate
        grad_up_ref[:, place] = grad_up
        total += grad_gate * gate_ref[:, place].astype(F32)
        total += grad_up * up_ref[:, place].astype(F32)
    sum_ref[...] = total
    grad_out_ref[...] = buffer[here, :, 2 * ff :].astype(F32)


def finish(slots, parts, w_gate, w_up, filled):
    height, ff = w_gate.shape
    share, columns = parts[0].shape
    count = len(parts)

    def rows(width):
        return pl.BlockSpec((share, width), lambda i, slots: (slots[i], 0))

    anywhere = pl.BlockSpec(memory_space=pl.ANY)
    widths = (ff, ff, columns - 2 * ff, 128)
    return pl.pallas_call(
        functools.partial(finish_kernel, count, ff),
        out_shape=tuple(jax.ShapeDtypeStruct((height, width), F32) for width in widths),
        grid_spec=pltpu.PrefetchScalarGridSpec(
            num_scalar_prefetch=1,
            grid=(count,),
            in_specs=[anywhere] * count + [rows(ff), rows(ff)] + [anywhere] * len(filled),
            out_specs=[rows(width) for width in widths],
            scratch_shapes=[
                pltpu.VMEM((2, share, columns), BF16),
                pltpu.SemaphoreType.DMA((2,)),
            ],
        ),
        input_output_aliases={count + 3 + at: at for at in range(len(filled))},
        compiler_params=pltpu.CompilerParams(vmem_limit_bytes=VMEM_LIMIT),
        cost_estimate=pl.CostEstimate(
            flops=4 * count * share * columns,
            transcendentals=0,
            bytes_accessed=8 * count * share * columns,
        ),
    )(slots, *parts, w_gate, w_up, *filled)


class Layer:
    def __init__(self, reps, tokens, prefix_len):
        self.reps = reps
        self.seqs, self.rows, self.width = tokens.shape
        self.head_dim = self.width // HEADS
        self.length = self.rows * reps
        self.groups = reps // self.seqs
        self.lanes = self.width // self.groups
        self.total = self.seqs * self.rows
        self.block = min(512, self.length)
        here = lax.axis_index("rep")
        self.my_seq = here // self.groups
        positions = here * self.rows + jnp.arange(self.rows, dtype=jnp.int32)
        cosine, sine = rope_lanes(positions, self.width, self.head_dim)
        self.cosine = jnp.tile(cosine, (self.seqs, 1))
        self.sine = jnp.tile(sine, (self.seqs, 1))
        self.all_tables = rope_lanes(
            jnp.arange(self.length, dtype=jnp.int32), self.lanes, self.head_dim
        )
        self.prefix = lax.dynamic_slice_in_dim(prefix_len, self.my_seq, 1, 0)

    def to_heads(self, values, parts):
        shape = (self.seqs, self.rows, parts, self.groups, self.lanes)
        chunks = values.reshape(shape).transpose(0, 3, 1, 2, 4)
        chunks = chunks.reshape(self.reps * self.rows, parts * self.lanes)
        return lax.all_to_all(chunks, "rep", 0, 0, tiled=True)

    def to_tokens(self, values, parts):
        chunks = lax.all_to_all(values, "rep", 0, 0, tiled=True)
        chunks = chunks.reshape(self.seqs, self.groups, self.rows, parts, self.lanes)
        return chunks.transpose(0, 2, 3, 1, 4).reshape(self.total, parts * self.width)

    def project(self, hidden, full_qkv, first_values):
        width = self.width
        raw = dot(hidden, full_qkv, (1, 0))

        def rope(values):
            return values * self.cosine - partner(values, self.head_dim, lane_roll) * self.sine

        query_rot = (rope(raw[:, :width]) * 0.125).astype(BF16)
        key_rot = rope(raw[:, width : 2 * width]).astype(BF16)
        first = first_values.reshape(self.total, width).astype(F32)
        value_mix = (0.5 * raw[:, 2 * width :] + 0.5 * first).astype(BF16)
        return jnp.concatenate([query_rot, key_rot, value_mix], axis=1)

    def attend(self, qkv):
        return attend(self.prefix, qkv, self.head_dim, self.block, self.block)

    def attend_back(self, qkv, do, att_t, mass):
        return attend_back(
            self.prefix, qkv, do, att_t, mass, *self.all_tables, self.head_dim, self.block, self.block
        )

    def sum_sequences(self, columns):
        share = columns.shape[0] // self.seqs
        mine = lax.dynamic_slice_in_dim(columns, self.my_seq * share, share, 0).astype(F32)
        for turn in range(1, self.seqs):
            slot = (self.my_seq + turn) % self.seqs
            sent = lax.dynamic_slice_in_dim(columns, slot * share, share, 0)
            moves = [
                (s * self.groups + g, ((s + turn) % self.seqs) * self.groups + g)
                for s in range(self.seqs)
                for g in range(self.groups)
            ]
            mine = mine + lax.ppermute(sent, "rep", moves).astype(F32)
        return mine.astype(BF16)


def gain_gradient(gain, *pairs):
    total = sum(jnp.sum(w.astype(F32) * gradient, axis=1) for w, gradient in pairs)
    return total / gain.astype(F32)


def gate_back(grad_swiglu, gate_pre, up_pre, sigma, swish):
    grad_gate_pre = grad_swiglu * up_pre * sigma * (1.0 + gate_pre * (1.0 - sigma))
    return (grad_gate_pre.astype(BF16), (grad_swiglu * swish).astype(BF16))


def local(
    reps,
    tokens,
    first_values,
    prefix_len,
    cotangent,
    w_query,
    w_key,
    w_value,
    w_output,
    w_gate,
    w_up,
    w_down,
    gain_attn,
    gain_ffn,
):
    layer = Layer(reps, tokens, prefix_len)
    total, width, ff = layer.total, layer.width, w_gate.shape[1]
    here = lax.axis_index("rep")

    def gather(weights):
        height = weights[0].shape[0]
        share = height // reps
        if share * reps == height and share % 8 == 0:
            pieces = [lax.dynamic_slice_in_dim(w, here * share, share, 0) for w in weights]
            axes = ("shard", "rep")
        else:
            pieces, axes = list(weights), ("shard",)
        piece = pieces[0] if len(pieces) == 1 else jnp.concatenate(pieces, axis=1)
        return lax.all_gather(piece, axes, axis=0, tiled=True)

    gains = lax.all_gather(jnp.stack([gain_attn, gain_ffn]), "shard", axis=1, tiled=True)
    full_qkv = gather((w_query, w_key, w_value))
    full_output = gather((w_output,))
    full_gate_up = gather((w_gate, w_up))
    full_down = gather((w_down,))
    gain1 = gains[0].astype(F32)
    gain2 = gains[1].astype(F32)

    inputs = tokens.reshape(total, width).astype(F32)
    normed1, scale1 = norm_rows(inputs)
    hidden1 = (normed1 * gain1).astype(BF16)
    hidden1_all = lax.all_gather(hidden1.reshape(tokens.shape), "rep", axis=1, tiled=True)
    qkv = layer.to_heads(layer.project(hidden1, full_qkv, first_values), 3)
    att, att_t, mass = layer.attend(qkv)
    attended = layer.to_tokens(att, 1)

    residual = inputs + dot(attended, full_output, (1, 0))
    normed2, scale2 = norm_rows(residual)
    hidden2 = (normed2 * gain2).astype(BF16)
    gate_up = dot(hidden2, full_gate_up, (1, 0))
    gate_pre, up_pre = gate_up[:, :ff], gate_up[:, ff:]
    sigma = jax.nn.sigmoid(gate_pre)
    swish = gate_pre * sigma
    swiglu = (swish * up_pre).astype(BF16)
    output = (residual + dot(swiglu, full_down, (1, 0))).astype(BF16)

    upstream = cotangent.reshape(total, width)
    grad_swiglu = dot(upstream, full_down, (1, 1))
    grad_gate_up = jnp.concatenate(gate_back(grad_swiglu, gate_pre, up_pre, sigma, swish), axis=1)
    grad_hidden2 = dot(grad_gate_up, full_gate_up, (1, 1))
    grad_residual = upstream.astype(F32) + norm_back(grad_hidden2 * gain2, normed2, scale2)
    grad_residual_low = grad_residual.astype(BF16)
    grad_attended = dot(grad_residual_low, full_output, (1, 1)).astype(BF16)

    def reduce_gather(partial):
        axes = ("shard", "rep")
        piece = lax.psum_scatter(partial.astype(BF16), axes, scatter_dimension=0, tiled=True)
        return lax.all_gather(piece, "rep", axis=0, tiled=True).astype(F32)

    grad_down = reduce_gather(dot(swiglu, upstream, (0, 0)))
    grad_wgate_up = reduce_gather(dot(hidden2, grad_gate_up, (0, 0)))
    grad_outproj = reduce_gather(dot(attended, grad_residual_low, (0, 0)))
    grad_wgate, grad_wup = grad_wgate_up[:, :ff], grad_wgate_up[:, ff:]

    do = layer.to_heads(grad_attended, 1)
    grad_raw_heads = layer.attend_back(qkv, do, att_t, mass)
    grad_raw = layer.to_tokens(grad_raw_heads, 3)
    grad_first = grad_raw[:, 2 * width :].astype(F32)
    grad_hidden1 = dot(grad_raw, full_qkv, (1, 1))
    grad_inputs = grad_residual + norm_back(grad_hidden1 * gain1, normed1, scale1)

    hidden_mine = lax.dynamic_index_in_dim(hidden1_all, layer.my_seq, 0, keepdims=False)
    columns = dot(hidden_mine, grad_raw_heads, (0, 0)).astype(BF16)
    columns = lax.psum_scatter(columns, "shard", scatter_dimension=0, tiled=True)
    height = columns.shape[0]
    mine = layer.sum_sequences(columns)
    gathered = lax.all_gather(mine, "rep", axis=0, tiled=True)
    gathered = gathered.reshape(layer.seqs, layer.groups, -1, 3, layer.lanes)
    grad_wqkv = gathered.transpose(3, 0, 2, 1, 4).reshape(3, height, width).astype(F32)
    shape = tokens.shape
    return (
        output.reshape(shape),
        grad_inputs.reshape(shape),
        grad_first.reshape(shape),
        grad_wqkv[0],
        grad_wqkv[1],
        grad_wqkv[2],
        grad_outproj,
        grad_wgate,
        grad_wup,
        grad_down,
        gain_gradient(
            gain_attn, (w_query, grad_wqkv[0]), (w_key, grad_wqkv[1]), (w_value, grad_wqkv[2])
        ),
        gain_gradient(gain_ffn, (w_gate, grad_wgate), (w_up, grad_wup)),
    )


def local_linked(
    reps,
    tokens,
    first_values,
    prefix_len,
    cotangent,
    w_query,
    w_key,
    w_value,
    w_output,
    w_gate,
    w_up,
    w_down,
    gain_attn,
    gain_ffn,
):
    layer = Layer(reps, tokens, prefix_len)
    links = Links(reps)
    total, width, ff = layer.total, layer.width, w_gate.shape[1]
    core, x = links.core, links.x

    own_gains = jnp.stack([gain_attn, gain_ffn])
    other_gains = links.over_x(own_gains)
    gains = jnp.where(
        x == 0,
        jnp.concatenate([own_gains, other_gains], axis=1),
        jnp.concatenate([other_gains, own_gains], axis=1),
    )
    gain1 = gains[0].astype(F32)
    gain2 = gains[1].astype(F32)

    def half_rows(weights):
        half = weights[0].shape[0] // 2
        pieces = [lax.dynamic_slice_in_dim(w, core * half, half, 0) for w in weights]
        return pieces[0] if len(pieces) == 1 else jnp.concatenate(pieces, axis=1)

    def assemble(weights, near, far, at):
        height = weights[0].shape[0]
        half = near.shape[0]
        columns = sum(w.shape[1] for w in weights)
        full = blank((2 * height, columns), BF16)
        place = 0
        for w in weights:
            full = lax.dynamic_update_slice(full, w, (x * height, place))
            place += w.shape[1]
        for part, owner in ((near, core), (far, 1 - core)):
            part = lax.slice_in_dim(part, at, at + columns, axis=1)
            full = lax.dynamic_update_slice(full, part, ((1 - x) * height + owner * half, 0))
        return full

    half_qkv = after(half_rows((w_query, w_key, w_value)), other_gains)
    near_qkv = links.over_x(half_qkv)
    near_ff = links.over_x(after(half_rows((w_output, w_gate, w_up)), near_qkv))
    full_qkv = assemble((w_query, w_key, w_value), near_qkv, links.over_core(near_qkv), 0)

    inputs = tokens.reshape(total, width).astype(F32)
    normed1, scale1 = norm_rows(inputs)
    hidden1 = (normed1 * gain1).astype(BF16)
    by_seq = after(hidden1, half_qkv).reshape(tokens.shape)
    mine, theirs = pick(by_seq, links.far), pick(by_seq, 1 - links.far)
    halves = join(mine[None], links.over_far(theirs)[None], links.far)
    groups = [list(range(layer.groups)), list(range(layer.groups, reps))]
    hidden1, halves, *layer.all_tables = fence(hidden1, halves, *layer.all_tables)
    hidden_mine = lax.all_gather(halves, "rep", axis_index_groups=groups, axis=1, tiled=True)
    hidden_mine = hidden_mine.reshape(layer.length, width)
    qkv = layer.to_heads(layer.project(hidden1, full_qkv, first_values), 3)
    qkv, hidden_mine = fence(qkv, hidden_mine)
    att, att_t, mass = layer.attend(qkv)
    att, near_ff, down_half = fence(att, near_ff, half_rows((w_down,)))
    near_down = links.over_x(down_half)
    far_ff = links.over_core(near_ff)
    full_output = assemble((w_output,), near_ff, far_ff, 0)
    full_gate_up = assemble((w_gate, w_up), near_ff, far_ff, w_output.shape[1])
    near_down = after(near_down, full_output, full_gate_up)
    full_down = assemble((w_down,), near_down, links.over_core(near_down), 0)
    attended = layer.to_tokens(att, 1)

    residual = inputs + dot(attended, full_output, (1, 0))
    normed2, scale2 = norm_rows(residual)
    hidden2 = (normed2 * gain2).astype(BF16)
    gate_up = dot(hidden2, full_gate_up, (1, 0))
    gate_pre, up_pre = gate_up[:, :ff], gate_up[:, ff:]
    sigma = jax.nn.sigmoid(gate_pre)
    swish = gate_pre * sigma
    swiglu = (swish * up_pre).astype(BF16)
    upstream = cotangent.reshape(total, width)

    def by_core(values, blocks):
        step = values.shape[1] // (2 * blocks)
        sides = [
            [values[:, (2 * b + side) * step : (2 * b + side + 1) * step] for b in range(blocks)]
            for side in range(2)
        ]
        low, high = (s[0] if blocks == 1 else jnp.concatenate(s, axis=1) for s in sides)
        return jnp.where(core == 0, low, high), jnp.where(core == 0, high, low)

    upstream_mine, upstream_other = by_core(upstream, 1)
    hidden2_mine, hidden2_other = by_core(hidden2, 2)
    down_send = dot(swiglu, upstream_other, (0, 0)).astype(BF16)
    grad_swiglu = dot(upstream, full_down, (1, 1))
    grad_gate_pre, grad_up_pre = gate_back(grad_swiglu, gate_pre, up_pre, sigma, swish)
    gate_send = dot(hidden2_other, grad_gate_pre, (0, 0)).astype(BF16)
    swiglu, gate_send, grad_gate_pre, grad_up_pre = fence(
        swiglu, gate_send, grad_gate_pre, grad_up_pre
    )
    gate_core = links.over_core(gate_send)
    down_total = add(dot(swiglu, upstream_mine, (0, 0)), links.over_core(down_send))
    down_half = links.half(down_total, 1 - x)
    down_total, down_half, grad_gate_pre, grad_up_pre = fence(
        down_total, down_half, grad_gate_pre, grad_up_pre
    )
    down_x = links.over_x(down_half)

    up_send = dot(hidden2_other, grad_up_pre, (0, 0)).astype(BF16)
    grad_gate_pre, up_send = fence(grad_gate_pre, up_send)
    up_core = links.over_core(up_send)
    gate_total = add(dot(hidden2_mine, grad_gate_pre, (0, 0)), gate_core)
    gate_half = links.quarters(gate_total, 1 - links.y)
    gate_total, gate_half, grad_gate_pre, grad_up_pre = fence(
        gate_total, gate_half, grad_gate_pre, grad_up_pre
    )
    gate_y = links.over_y(gate_half)

    up_total = add(dot(hidden2_mine, grad_up_pre, (0, 0)), up_core)
    up_half = links.half(up_total, 1 - x)
    up_total, up_half, grad_gate_pre, grad_up_pre = fence(
        up_total, up_half, grad_gate_pre, grad_up_pre
    )
    up_x = links.over_x(up_half)

    grad_gate_up = jnp.concatenate([grad_gate_pre, grad_up_pre], axis=1)
    grad_hidden2 = dot(grad_gate_up, full_gate_up, (1, 1))
    grad_residual = upstream.astype(F32) + norm_back(grad_hidden2 * gain2, normed2, scale2)
    grad_residual_low = grad_residual.astype(BF16)
    grad_attended = dot(grad_residual_low, full_output, (1, 1)).astype(BF16)
    grad_attended, grad_residual_low = fence(grad_attended, grad_residual_low)
    do = layer.to_heads(grad_attended, 1)
    attended_mine, attended_other = by_core(attended, 2)
    out_send = dot(attended_other, grad_residual_low, (0, 0)).astype(BF16)
    out_total = add(dot(attended_mine, grad_residual_low, (0, 0)), links.over_core(out_send))
    out_total, down_x = fence(out_total, down_x)
    down_first = add(links.half(down_total, x), down_x)
    down_y = links.over_y(links.half(down_first, 1 - links.y))
    out_y = links.over_y(links.quarters(out_total, 1 - links.y))
    output = (residual + dot(swiglu, full_down, (1, 0))).astype(BF16)
    do, out_total, down_first, output = fence(do, out_total, down_first, output)

    grad_raw_heads = layer.attend_back(qkv, do, att_t, mass)
    grad_raw_heads, gate_y, up_x, out_y, down_y = fence(grad_raw_heads, gate_y, up_x, out_y, down_y)
    down_second = add(links.half(down_first, links.y), down_y)
    down_pair = links.over_pair(links.half(down_second, 1 - links.near))
    gate_first = add(links.quarters(gate_total, links.y), gate_y)
    gate_x = links.over_x(links.half(gate_first, 1 - x))

    up_first = add(links.half(up_total, x), up_x)
    out_first = add(links.quarters(out_total, links.y), out_y)
    up_y = links.over_y(links.half(up_first, 1 - links.y))
    out_x = links.over_x(links.half(out_first, 1 - x))
    columns = dot(hidden_mine, grad_raw_heads, (0, 0)).astype(BF16)
    columns_x = links.over_x(links.half(columns, 1 - x))
    columns_x, grad_raw_heads, down_pair = fence(columns_x, grad_raw_heads, down_pair)
    down_third = add(links.half(down_second, links.near), down_pair)
    down_far = links.over_far(links.half(down_third, 1 - links.far))
    grad_raw = layer.to_tokens(grad_raw_heads, 3)
    summed = layer.sum_sequences(add(links.half(columns, x), columns_x))
    gate_second = add(links.half(gate_first, x), gate_x)
    down_piece = add(links.half(down_third, links.far), down_far)
    joined = jnp.concatenate(
        [
            gate_second,
            add(links.half(up_first, links.y), up_y),
            add(links.half(out_first, x), out_x),
        ],
        axis=1,
    )

    joined, down_piece, summed = fence(joined, down_piece, summed)
    gathered = lax.all_gather(summed, "rep", axis=0, tiled=True)
    joined_pair = links.over_pair(links.half(joined, 1 - links.near))
    down_piece = join(down_piece, links.over_far(down_piece), links.far)
    joined_third = add(links.half(joined, links.near), joined_pair)
    joined_third, down_piece, grad_raw = fence(joined_third, down_piece, grad_raw)

    joined_far = links.over_far(links.half(joined_third, 1 - links.far))
    down_piece = join(down_piece, links.over_pair(down_piece), links.near)
    grad_first = grad_raw[:, 2 * width :].astype(F32)
    grad_hidden1 = dot(grad_raw, full_qkv, (1, 1))
    grad_inputs = grad_residual + norm_back(grad_hidden1 * gain1, normed1, scale1)
    joined_piece = add(links.half(joined_third, links.far), joined_far)
    joined_piece, down_piece, grad_inputs, grad_first, gathered = fence(
        joined_piece, down_piece, grad_inputs, grad_first, gathered
    )

    joined_far = links.over_far(joined_piece)
    down_y = links.over_y(down_piece)
    grad_wquery, grad_wkey, grad_wvalue, sums = spread(
        gathered, w_query, w_key, w_value, layer.seqs, layer.groups
    )
    down_piece = join(down_piece, down_y, links.y)
    part = join(joined_piece, joined_far, links.far)
    part, down_piece, grad_wquery, grad_wkey, grad_wvalue = fence(
        part, down_piece, grad_wquery, grad_wkey, grad_wvalue
    )

    part_pair = links.over_pair(part)
    part_y = links.over_y(part)
    part_core = links.over_core(part)
    down_other = links.over_core(down_piece)
    grad_down = jnp.where(
        core == 0,
        jnp.concatenate([down_piece, down_other], axis=1),
        jnp.concatenate([down_other, down_piece], axis=1),
    ).astype(F32)
    part_pair, part_y, part_core, grad_down = fence(part_pair, part_y, part_core, grad_down)
    middle = part.shape[0] // 2
    last = (links.over_y(part_pair[:middle]), links.over_pair(part_y[middle:]))
    pair_core, y_core = links.over_core(part_pair), links.over_core(part_y)

    def slots(*bits):
        place = [
            (core ^ c) * 4 + (links.y ^ y) * 2 + (links.near ^ near) for c, y, near in bits
        ]
        return jnp.stack(place).astype(jnp.int32)

    early = slots((0, 0, 0), (0, 0, 1), (0, 1, 0), (1, 0, 0), (1, 0, 1), (1, 1, 0))
    early_parts = (part, part_pair, part_y, part_core, pair_core, y_core)
    low, high, *filled = fence(*last, *finish(early, early_parts, w_gate, w_up, ()))
    late = slots((0, 1, 1), (1, 1, 1))
    late = jnp.concatenate([2 * late, 2 * late + 1])
    late_parts = (low, links.over_core(low), high, links.over_core(high))
    grad_wgate, grad_wup, grad_outproj, ff_sums = finish(late, late_parts, w_gate, w_up, filled)
    shape = tokens.shape
    return (
        output.reshape(shape),
        grad_inputs.reshape(shape),
        grad_first.reshape(shape),
        grad_wquery,
        grad_wkey,
        grad_wvalue,
        grad_outproj,
        grad_wgate,
        grad_wup,
        grad_down,
        jnp.sum(sums, axis=1) / gain_attn.astype(F32),
        jnp.sum(ff_sums, axis=1) / gain_ffn.astype(F32),
    )


def solution(mesh):
    sequence = P("shard", "rep", None)
    matrix = P("shard", None)
    vector = P("shard")
    reps, shards = mesh.shape["rep"], mesh.shape["shard"]
    linked = reps == 16 and shards == 2
    return jax.shard_map(
        functools.partial(local_linked if linked else local, reps),
        mesh=mesh,
        in_specs=(sequence, sequence, vector, sequence) + (matrix,) * 7 + (vector,) * 2,
        out_specs=(sequence,) * 3 + (matrix,) * 7 + (vector,) * 2,
        check_vma=False,
    )
```

```python
import functools

import jax
import jax.numpy as jnp
from jax import lax
from jax.experimental import pallas as pl
from jax.experimental.pallas import tpu as pltpu
from jax.sharding import PartitionSpec as P

HEADS = 16
EPSILON = 1e-05
NEGATIVE = -1e30
ROPE_BASE = 10000.0
BF16 = jnp.bfloat16
F32 = jnp.float32
VMEM_LIMIT = 60 * 1024 * 1024


def dot(left, right, contract):
    return lax.dot_general(
        left, right, ((contract[:1], contract[1:]), ((), ())), preferred_element_type=F32
    )


def norm_rows(values):
    scale = lax.rsqrt(jnp.mean(values * values, axis=-1, keepdims=True) + EPSILON)
    return (values * scale, scale)


def norm_back(gradient, normed, scale):
    return scale * (gradient - normed * jnp.mean(gradient * normed, axis=-1, keepdims=True))


def rope_lanes(positions, lanes, head_dim):
    half = head_dim // 2
    lane = jnp.arange(lanes, dtype=jnp.int32) % head_dim
    frequency = ROPE_BASE ** (-2.0 * (lane % half).astype(F32) / head_dim)
    angles = positions.astype(F32)[:, None] * frequency[None, :]
    sign = jnp.where(lane < half, 1.0, -1.0).astype(F32)
    return (jnp.cos(angles), jnp.sin(angles) * sign[None, :])


def partner(values, head_dim, roll):
    half = head_dim // 2
    lane = lax.broadcasted_iota(jnp.int32, values.shape, values.ndim - 1) % head_dim
    return jnp.where(lane < half, roll(values, half), roll(values, -half))


def lane_roll(values, shift):
    return jnp.roll(values, -shift, axis=-1)


def kernel_roll(values, shift):
    width = values.shape[-1]
    if width % 128 == 0:
        return pltpu.roll(values, (-shift) % width, axis=values.ndim - 1)
    shift = shift % width
    return jnp.concatenate([values[..., shift:], values[..., :shift]], axis=-1)


def head_rows(values, head, head_dim):
    if values.shape[-1] == head_dim:
        return values
    lane = lax.broadcasted_iota(jnp.int32, values.shape, values.ndim - 1)
    mine = (lane >= head * head_dim) & (lane < (head + 1) * head_dim)
    return jnp.where(mine, values, jnp.zeros_like(values))


def masked_scores(key_block, query_block, key_start, query_start, prefix):
    scores = dot(key_block, query_block, (1, 1))
    query_pos = query_start + lax.broadcasted_iota(jnp.int32, (1, scores.shape[1]), 1)
    last = jnp.maximum(query_pos, prefix - 1) - key_start
    key_pos = lax.broadcasted_iota(jnp.int32, scores.shape, 0)
    return jnp.where(key_pos <= last, scores, NEGATIVE)


def attend_kernel(
    head_dim, bq, bk, prefix_ref, q_ref, k_ref, v_ref, att_ref, att_t_ref, mass_ref, v_t, acc
):
    length, width = q_ref.shape
    heads = width // head_dim
    prefix = prefix_ref[0]
    for start in range(0, length, 128):
        v_t[:, start : start + 128] = v_ref[start : start + 128, :].T

    def query_step(i, carry):
        q0 = pl.multiple_of(i * bq, bq)
        q_all = q_ref[pl.ds(q0, bq), :]
        q_heads = [head_rows(q_all, h, head_dim) for h in range(heads)]
        acc[...] = jnp.zeros_like(acc)
        blocks = (jnp.maximum(q0 + bq, prefix) + bk - 1) // bk

        def key_step(j, stats):
            k0 = pl.multiple_of(j * bk, bk)
            k_block = k_ref[pl.ds(k0, bk), :]
            out = []
            for h in range(heads):
                peak, mass = stats[h]
                scores = masked_scores(k_block, q_heads[h], k0, q0, prefix)
                new_peak = jnp.maximum(peak, jnp.max(scores, axis=0, keepdims=True))
                alpha = jnp.exp(peak - new_peak)
                weights = jnp.exp(scores - new_peak)
                mass = mass * alpha + jnp.sum(weights, axis=0, keepdims=True)
                rows = slice(h * head_dim, (h + 1) * head_dim)
                acc[rows, :] = acc[rows, :] * alpha + dot(
                    v_t[rows, pl.ds(k0, bk)], weights.astype(BF16), (1, 0)
                )
                out.append((new_peak, mass))
            return tuple(out)

        first = tuple(
            (jnp.full((1, bq), NEGATIVE, F32), jnp.zeros((1, bq), F32)) for _ in range(heads)
        )
        stats = lax.fori_loop(0, blocks, key_step, first)
        for h in range(heads):
            peak, mass = stats[h]
            rows = slice(h * head_dim, (h + 1) * head_dim)
            att_t_ref[rows, pl.ds(q0, bq)] = acc[rows, :] / mass
            mass_ref[h : h + 1, pl.ds(q0, bq)] = peak + jnp.log(mass)
        for part in range(0, bq, 128):
            place = pl.ds(pl.multiple_of(q0 + part, 128), 128)
            att_ref[place, :] = att_t_ref[:, place].T.astype(BF16)
        return carry

    lax.fori_loop(0, length // bq, query_step, 0)


def attend_back_kernel(
    head_dim,
    bq,
    bk,
    prefix_ref,
    q_ref,
    k_ref,
    v_ref,
    do_ref,
    att_t_ref,
    mass_ref,
    cos_ref,
    sin_ref,
    out_ref,
    k_t,
    delta,
    dq_t,
    dk_acc,
    dv_acc,
):
    length, width = q_ref.shape
    heads = width // head_dim
    prefix = prefix_ref[0]
    dq_t[...] = jnp.zeros_like(dq_t)
    for start in range(0, length, 128):
        place = slice(start, start + 128)
        k_t[:, place] = k_ref[place, :].T
        product = do_ref[place, :].astype(F32).T * att_t_ref[:, place]
        for h in range(heads):
            rows = slice(h * head_dim, (h + 1) * head_dim)
            delta[h : h + 1, place] = jnp.sum(product[rows, :], axis=0, keepdims=True)

    def rope_back(gradient, place):
        return gradient * cos_ref[place, :] + partner(gradient, head_dim, kernel_roll) * sin_ref[
            place, :
        ]

    def key_step(j, carry):
        k0 = pl.multiple_of(j * bk, bk)
        k_block = k_ref[pl.ds(k0, bk), :]
        v_block = v_ref[pl.ds(k0, bk), :]
        dk_acc[...] = jnp.zeros_like(dk_acc)
        dv_acc[...] = jnp.zeros_like(dv_acc)
        begin = jnp.where(k0 < prefix, 0, k0 // bq)

        def query_step(i, inner):
            q0 = pl.multiple_of(i * bq, bq)
            q_all = q_ref[pl.ds(q0, bq), :]
            do_all = do_ref[pl.ds(q0, bq), :]
            for h in range(heads):
                rows = slice(h * head_dim, (h + 1) * head_dim)
                q_head = head_rows(q_all, h, head_dim)
                do_head = head_rows(do_all, h, head_dim)
                scores = masked_scores(k_block, q_head, k0, q0, prefix)
                weights = jnp.exp(scores - mass_ref[h : h + 1, pl.ds(q0, bq)])
                grad_weights = dot(v_block, do_head, (1, 1))
                grad_scores = (weights * (grad_weights - delta[h : h + 1, pl.ds(q0, bq)])).astype(
                    BF16
                )
                dv_acc[...] += dot(weights.astype(BF16), do_head, (1, 0))
                dk_acc[...] += dot(grad_scores, q_head, (1, 0))
                dq_t[rows, pl.ds(q0, bq)] += dot(k_t[rows, pl.ds(k0, bk)], grad_scores, (1, 0))
            return inner

        lax.fori_loop(begin, length // bq, query_step, 0)
        place = pl.ds(k0, bk)
        out_ref[place, width : 2 * width] = rope_back(dk_acc[...], place).astype(BF16)
        out_ref[place, 2 * width :] = dv_acc[...].astype(BF16) * jnp.array(0.5, BF16)
        return carry

    lax.fori_loop(0, length // bk, key_step, 0)
    for start in range(0, length, 128):
        place = slice(start, start + 128)
        out_ref[place, :width] = rope_back(dq_t[:, place].T * 0.125, place).astype(BF16)


def turns(reps, move):
    pairs = []
    for here in range(reps):
        z, y, core = move(here // 4, (here // 2) % 2, here % 2)
        pairs.append((here, (z % (reps // 4)) * 4 + y * 2 + core))
    return pairs


class Links:
    def __init__(self, reps):
        self.to_core = turns(reps, lambda z, y, core: (z, y, 1 - core))
        self.to_y = turns(reps, lambda z, y, core: (z, 1 - y, core))
        self.to_pair = turns(reps, lambda z, y, core: (z ^ 1, y, core))
        self.to_far = turns(reps, lambda z, y, core: (z ^ 2, y, core))
        here = lax.axis_index("rep")
        self.near, self.far = (here // 4) % 2, here // 8
        self.y, self.core = (here // 2) % 2, here % 2
        self.x = lax.axis_index("shard")

    def over_core(self, value):
        return lax.ppermute(value, "rep", self.to_core)

    def over_x(self, value):
        return lax.ppermute(value, "shard", [(0, 1), (1, 0)])

    def over_y(self, value):
        return lax.ppermute(value, "rep", self.to_y)

    def over_pair(self, value):
        return lax.ppermute(value, "rep", self.to_pair)

    def over_far(self, value):
        return lax.ppermute(value, "rep", self.to_far)

    def half(self, total, side):
        return pick(total.reshape(2, -1, total.shape[1]), side)

    def quarters(self, total, side):
        columns = total.shape[1]
        return pick(total.reshape(2, 2, -1, columns), side, 1).reshape(-1, columns)


def pick(values, index, axis=0):
    return lax.dynamic_index_in_dim(values, index, axis, keepdims=False)


def put(values, part, index):
    return lax.dynamic_update_index_in_dim(values, part, index, 0)


def join(mine, other, index):
    first = jnp.concatenate([mine, other], axis=0)
    second = jnp.concatenate([other, mine], axis=0)
    return jnp.where(index == 0, first, second)


def fence(*values):
    return lax.optimization_barrier(values)


def after(value, *earlier):
    return lax.optimization_barrier((value,) + earlier)[0]


def blank(shape, dtype):
    return pl.pallas_call(
        lambda out_ref: None,
        out_shape=jax.ShapeDtypeStruct(shape, dtype),
        out_specs=pl.BlockSpec(memory_space=pl.ANY),
    )()


def add(left, right):
    return (left.astype(F32) + right.astype(F32)).astype(BF16)


def whole(shape):
    return pl.BlockSpec(shape, lambda *_: (0,) * len(shape))


def thirds(qkv):
    length, width = qkv.shape[0], qkv.shape[1] // 3
    if width % 128 == 0:
        specs = [pl.BlockSpec((length, width), lambda *_, at=at: (0, at)) for at in range(3)]
        return (qkv, qkv, qkv), specs
    parts = tuple(qkv[:, at * width : (at + 1) * width] for at in range(3))
    return parts, [whole((length, width))] * 3


def attend(prefix, qkv, head_dim, bq, bk):
    length, width = qkv.shape[0], qkv.shape[1] // 3
    heads = width // head_dim
    flops = 2 * 2 * heads * length * length * head_dim
    operands, specs = thirds(qkv)
    return pl.pallas_call(
        functools.partial(attend_kernel, head_dim, bq, bk),
        out_shape=(
            jax.ShapeDtypeStruct((length, width), BF16),
            jax.ShapeDtypeStruct((width, length), F32),
            jax.ShapeDtypeStruct((heads, length), F32),
        ),
        grid_spec=pltpu.PrefetchScalarGridSpec(
            num_scalar_prefetch=1,
            grid=(1,),
            in_specs=specs,
            out_specs=[whole((length, width)), whole((width, length)), whole((heads, length))],
            scratch_shapes=[pltpu.VMEM((width, length), BF16), pltpu.VMEM((width, bq), F32)],
        ),
        compiler_params=pltpu.CompilerParams(vmem_limit_bytes=VMEM_LIMIT),
        cost_estimate=pl.CostEstimate(flops=1, transcendentals=0, bytes_accessed=1),
    )(prefix, *operands)


def attend_back(prefix, qkv, do, att_t, mass, cosine, sine, head_dim, bq, bk):
    length, width = qkv.shape[0], qkv.shape[1] // 3
    heads = width // head_dim
    flops = 5 * 2 * heads * length * length * head_dim
    rows = whole((length, width))
    operands, specs = thirds(qkv)
    return pl.pallas_call(
        functools.partial(attend_back_kernel, head_dim, bq, bk),
        out_shape=jax.ShapeDtypeStruct((length, 3 * width), BF16),
        grid_spec=pltpu.PrefetchScalarGridSpec(
            num_scalar_prefetch=1,
            grid=(1,),
            in_specs=specs + [rows, whole((width, length)), whole((heads, length)), rows, rows],
            out_specs=whole((length, 3 * width)),
            scratch_shapes=[
                pltpu.VMEM((width, length), BF16),
                pltpu.VMEM((heads, length), F32),
                pltpu.VMEM((width, length), F32),
                pltpu.VMEM((bk, width), F32),
                pltpu.VMEM((bk, width), F32),
            ],
        ),
        compiler_params=pltpu.CompilerParams(vmem_limit_bytes=VMEM_LIMIT),
        cost_estimate=pl.CostEstimate(flops=1, transcendentals=0, bytes_accessed=1),
    )(prefix, *operands, do, att_t, mass, cosine, sine)


def spread_kernel(lanes, core_ref, mine_ref, other_ref, wq_ref, wk_ref, wv_ref, *out_refs):
    sum_ref = out_refs[3]
    core = core_ref[0]
    total = jnp.zeros(sum_ref.shape, F32)
    for near in range(2):
        for y in range(2):
            mine, other = mine_ref[near, y, 0], other_ref[near, y, 0]
            for side, part in enumerate((mine, other)):
                part = jnp.where(core == 0, part, other if side == 0 else mine)
                group = near * 4 + y * 2 + side
                place = slice(group * lanes, (group + 1) * lanes)
                for at, w_ref in enumerate((wq_ref, wk_ref, wv_ref)):
                    values = part[:, at * lanes : (at + 1) * lanes].astype(F32)
                    out_refs[at][:, place] = values
                    total += values * w_ref[:, place].astype(F32)
    sum_ref[...] = total


def spread(core, mine, other, w_query, w_key, w_value, seqs, groups):
    height, width = w_query.shape
    share, lanes = height // seqs, width // groups
    steps = 4
    rows = share // steps
    tile = pl.BlockSpec((rows, width), lambda s, i, core: (s * steps + i, 0))
    part = pl.BlockSpec((2, 2, 1, rows, 3 * lanes), lambda s, i, core: (0, 0, s, i, 0))
    shape = (2, 2, seqs, share, 3 * lanes)
    return pl.pallas_call(
        functools.partial(spread_kernel, lanes),
        out_shape=(jax.ShapeDtypeStruct((height, width), F32),) * 3
        + (jax.ShapeDtypeStruct((height, lanes), F32),),
        grid_spec=pltpu.PrefetchScalarGridSpec(
            num_scalar_prefetch=1,
            grid=(seqs, steps),
            in_specs=[part, part, tile, tile, tile],
            out_specs=[tile, tile, tile]
            + [pl.BlockSpec((rows, lanes), lambda s, i, core: (s * steps + i, 0))],
        ),
        cost_estimate=pl.CostEstimate(flops=1, transcendentals=0, bytes_accessed=1),
    )(
        core.reshape(1).astype(jnp.int32),
        mine.reshape(shape),
        other.reshape(shape),
        w_query,
        w_key,
        w_value,
    )


def finish_kernel(count, ff, slots_ref, *refs):
    parts, (gate_ref, up_ref) = refs[:count], refs[count : count + 2]
    grad_gate_ref, grad_up_ref, grad_out_ref, sum_ref, buffer, arrived = refs[-6:]
    step = pl.program_id(0)

    def fetch(at):
        return pltpu.make_async_copy(parts[at], buffer.at[at % 2], arrived.at[at % 2])

    for at in range(count):

        @pl.when(step == max(at - 1, 0))
        def _():
            fetch(at).start()

    for at in range(count):

        @pl.when(step == at)
        def _():
            fetch(at).wait()

    here = lax.rem(step, 2)
    lanes = sum_ref.shape[1]
    total = jnp.zeros(sum_ref.shape, F32)
    for start in range(0, ff, lanes):
        place = slice(start, start + lanes)
        grad_gate = buffer[here, :, place].astype(F32)
        grad_up = buffer[here, :, ff + start : ff + start + lanes].astype(F32)
        grad_gate_ref[:, place] = grad_gate
        grad_up_ref[:, place] = grad_up
        total += grad_gate * gate_ref[:, place].astype(F32)
        total += grad_up * up_ref[:, place].astype(F32)
    sum_ref[...] = total
    grad_out_ref[...] = buffer[here, :, 2 * ff :].astype(F32)


def finish(slots, parts, w_gate, w_up, filled):
    height, ff = w_gate.shape
    share, columns = parts[0].shape
    count = len(parts)

    def rows(width):
        return pl.BlockSpec((share, width), lambda i, slots: (slots[i], 0))

    anywhere = pl.BlockSpec(memory_space=pl.ANY)
    widths = (ff, ff, columns - 2 * ff, 128)
    return pl.pallas_call(
        functools.partial(finish_kernel, count, ff),
        out_shape=tuple(jax.ShapeDtypeStruct((height, width), F32) for width in widths),
        grid_spec=pltpu.PrefetchScalarGridSpec(
            num_scalar_prefetch=1,
            grid=(count,),
            in_specs=[anywhere] * count + [rows(ff), rows(ff)] + [anywhere] * len(filled),
            out_specs=[rows(width) for width in widths],
            scratch_shapes=[
                pltpu.VMEM((2, share, columns), BF16),
                pltpu.SemaphoreType.DMA((2,)),
            ],
        ),
        input_output_aliases={count + 3 + at: at for at in range(len(filled))},
        compiler_params=pltpu.CompilerParams(vmem_limit_bytes=VMEM_LIMIT),
        cost_estimate=pl.CostEstimate(flops=1, transcendentals=0, bytes_accessed=1),
    )(slots, *parts, w_gate, w_up, *filled)


class Layer:
    def __init__(self, reps, tokens, prefix_len):
        self.reps = reps
        self.seqs, self.rows, self.width = tokens.shape
        self.head_dim = self.width // HEADS
        self.length = self.rows * reps
        self.groups = reps // self.seqs
        self.lanes = self.width // self.groups
        self.total = self.seqs * self.rows
        self.block = min(512, self.length)
        here = lax.axis_index("rep")
        self.my_seq = here // self.groups
        positions = here * self.rows + jnp.arange(self.rows, dtype=jnp.int32)
        cosine, sine = rope_lanes(positions, self.width, self.head_dim)
        self.cosine = jnp.tile(cosine, (self.seqs, 1))
        self.sine = jnp.tile(sine, (self.seqs, 1))
        self.all_tables = rope_lanes(
            jnp.arange(self.length, dtype=jnp.int32), self.lanes, self.head_dim
        )
        self.prefix = lax.dynamic_slice_in_dim(prefix_len, self.my_seq, 1, 0)

    def to_heads(self, values, parts):
        shape = (self.seqs, self.rows, parts, self.groups, self.lanes)
        chunks = values.reshape(shape).transpose(0, 3, 1, 2, 4)
        chunks = chunks.reshape(self.reps * self.rows, parts * self.lanes)
        return lax.all_to_all(chunks, "rep", 0, 0, tiled=True)

    def to_tokens(self, values, parts):
        chunks = lax.all_to_all(values, "rep", 0, 0, tiled=True)
        chunks = chunks.reshape(self.seqs, self.groups, self.rows, parts, self.lanes)
        return chunks.transpose(0, 2, 3, 1, 4).reshape(self.total, parts * self.width)

    def project(self, hidden, full_qkv, first_values):
        width = self.width
        raw = dot(hidden, full_qkv, (1, 0))

        def rope(values):
            return values * self.cosine - partner(values, self.head_dim, lane_roll) * self.sine

        query_rot = (rope(raw[:, :width]) * 0.125).astype(BF16)
        key_rot = rope(raw[:, width : 2 * width]).astype(BF16)
        first = first_values.reshape(self.total, width).astype(F32)
        value_mix = (0.5 * raw[:, 2 * width :] + 0.5 * first).astype(BF16)
        return jnp.concatenate([query_rot, key_rot, value_mix], axis=1)

    def attend(self, qkv):
        return attend(self.prefix, qkv, self.head_dim, self.block, self.block)

    def attend_back(self, qkv, do, att_t, mass):
        return attend_back(
            self.prefix, qkv, do, att_t, mass, *self.all_tables, self.head_dim, self.block, self.block
        )

    def sum_sequences(self, columns):
        share = columns.shape[0] // self.seqs
        mine = lax.dynamic_slice_in_dim(columns, self.my_seq * share, share, 0).astype(F32)
        for turn in range(1, self.seqs):
            slot = (self.my_seq + turn) % self.seqs
            sent = lax.dynamic_slice_in_dim(columns, slot * share, share, 0)
            moves = [
                (s * self.groups + g, ((s + turn) % self.seqs) * self.groups + g)
                for s in range(self.seqs)
                for g in range(self.groups)
            ]
            mine = mine + lax.ppermute(sent, "rep", moves).astype(F32)
        return mine.astype(BF16)


def gain_gradient(gain, *pairs):
    total = sum(jnp.sum(w.astype(F32) * gradient, axis=1) for w, gradient in pairs)
    return total / gain.astype(F32)


def gate_back(grad_swiglu, gate_pre, up_pre, sigma, swish):
    grad_gate_pre = grad_swiglu * up_pre * sigma * (1.0 + gate_pre * (1.0 - sigma))
    return (grad_gate_pre.astype(BF16), (grad_swiglu * swish).astype(BF16))


def local(
    reps,
    tokens,
    first_values,
    prefix_len,
    cotangent,
    w_query,
    w_key,
    w_value,
    w_output,
    w_gate,
    w_up,
    w_down,
    gain_attn,
    gain_ffn,
):
    layer = Layer(reps, tokens, prefix_len)
    total, width, ff = layer.total, layer.width, w_gate.shape[1]
    here = lax.axis_index("rep")

    def gather(weights):
        height = weights[0].shape[0]
        share = height // reps
        if share * reps == height and share % 8 == 0:
            pieces = [lax.dynamic_slice_in_dim(w, here * share, share, 0) for w in weights]
            axes = ("shard", "rep")
        else:
            pieces, axes = list(weights), ("shard",)
        piece = pieces[0] if len(pieces) == 1 else jnp.concatenate(pieces, axis=1)
        return lax.all_gather(piece, axes, axis=0, tiled=True)

    gains = lax.all_gather(jnp.stack([gain_attn, gain_ffn]), "shard", axis=1, tiled=True)
    full_qkv = gather((w_query, w_key, w_value))
    full_output = gather((w_output,))
    full_gate_up = gather((w_gate, w_up))
    full_down = gather((w_down,))
    gain1 = gains[0].astype(F32)
    gain2 = gains[1].astype(F32)

    inputs = tokens.reshape(total, width).astype(F32)
    normed1, scale1 = norm_rows(inputs)
    hidden1 = (normed1 * gain1).astype(BF16)
    hidden1_all = lax.all_gather(hidden1.reshape(tokens.shape), "rep", axis=1, tiled=True)
    qkv = layer.to_heads(layer.project(hidden1, full_qkv, first_values), 3)
    att, att_t, mass = layer.attend(qkv)
    attended = layer.to_tokens(att, 1)

    residual = inputs + dot(attended, full_output, (1, 0))
    normed2, scale2 = norm_rows(residual)
    hidden2 = (normed2 * gain2).astype(BF16)
    gate_up = dot(hidden2, full_gate_up, (1, 0))
    gate_pre, up_pre = gate_up[:, :ff], gate_up[:, ff:]
    sigma = jax.nn.sigmoid(gate_pre)
    swish = gate_pre * sigma
    swiglu = (swish * up_pre).astype(BF16)
    output = (residual + dot(swiglu, full_down, (1, 0))).astype(BF16)

    upstream = cotangent.reshape(total, width)
    grad_swiglu = dot(upstream, full_down, (1, 1))
    grad_gate_up = jnp.concatenate(gate_back(grad_swiglu, gate_pre, up_pre, sigma, swish), axis=1)
    grad_hidden2 = dot(grad_gate_up, full_gate_up, (1, 1))
    grad_residual = upstream.astype(F32) + norm_back(grad_hidden2 * gain2, normed2, scale2)
    grad_residual_low = grad_residual.astype(BF16)
    grad_attended = dot(grad_residual_low, full_output, (1, 1)).astype(BF16)

    def reduce_gather(partial):
        axes = ("shard", "rep")
        piece = lax.psum_scatter(partial.astype(BF16), axes, scatter_dimension=0, tiled=True)
        return lax.all_gather(piece, "rep", axis=0, tiled=True).astype(F32)

    grad_down = reduce_gather(dot(swiglu, upstream, (0, 0)))
    grad_wgate_up = reduce_gather(dot(hidden2, grad_gate_up, (0, 0)))
    grad_outproj = reduce_gather(dot(attended, grad_residual_low, (0, 0)))
    grad_wgate, grad_wup = grad_wgate_up[:, :ff], grad_wgate_up[:, ff:]

    do = layer.to_heads(grad_attended, 1)
    grad_raw_heads = layer.attend_back(qkv, do, att_t, mass)
    grad_raw = layer.to_tokens(grad_raw_heads, 3)
    grad_first = grad_raw[:, 2 * width :].astype(F32)
    grad_hidden1 = dot(grad_raw, full_qkv, (1, 1))
    grad_inputs = grad_residual + norm_back(grad_hidden1 * gain1, normed1, scale1)

    hidden_mine = lax.dynamic_index_in_dim(hidden1_all, layer.my_seq, 0, keepdims=False)
    columns = dot(hidden_mine, grad_raw_heads, (0, 0)).astype(BF16)
    columns = lax.psum_scatter(columns, "shard", scatter_dimension=0, tiled=True)
    height = columns.shape[0]
    mine = layer.sum_sequences(columns)
    gathered = lax.all_gather(mine, "rep", axis=0, tiled=True)
    gathered = gathered.reshape(layer.seqs, layer.groups, -1, 3, layer.lanes)
    grad_wqkv = gathered.transpose(3, 0, 2, 1, 4).reshape(3, height, width).astype(F32)
    shape = tokens.shape
    return (
        output.reshape(shape),
        grad_inputs.reshape(shape),
        grad_first.reshape(shape),
        grad_wqkv[0],
        grad_wqkv[1],
        grad_wqkv[2],
        grad_outproj,
        grad_wgate,
        grad_wup,
        grad_down,
        gain_gradient(
            gain_attn, (w_query, grad_wqkv[0]), (w_key, grad_wqkv[1]), (w_value, grad_wqkv[2])
        ),
        gain_gradient(gain_ffn, (w_gate, grad_wgate), (w_up, grad_wup)),
    )


def local_linked(
    reps,
    tokens,
    first_values,
    prefix_len,
    cotangent,
    w_query,
    w_key,
    w_value,
    w_output,
    w_gate,
    w_up,
    w_down,
    gain_attn,
    gain_ffn,
):
    layer = Layer(reps, tokens, prefix_len)
    links = Links(reps)
    total, width, ff = layer.total, layer.width, w_gate.shape[1]
    core, x = links.core, links.x

    own_gains = jnp.stack([gain_attn, gain_ffn])
    other_gains = links.over_x(own_gains)
    gains = jnp.where(
        x == 0,
        jnp.concatenate([own_gains, other_gains], axis=1),
        jnp.concatenate([other_gains, own_gains], axis=1),
    )
    gain1 = gains[0].astype(F32)
    gain2 = gains[1].astype(F32)

    def half_rows(weights):
        half = weights[0].shape[0] // 2
        pieces = [lax.dynamic_slice_in_dim(w, core * half, half, 0) for w in weights]
        return pieces[0] if len(pieces) == 1 else jnp.concatenate(pieces, axis=1)

    def assemble(weights, near, far, at):
        height = weights[0].shape[0]
        half = near.shape[0]
        columns = sum(w.shape[1] for w in weights)
        full = blank((2 * height, columns), BF16)
        place = 0
        for w in weights:
            full = lax.dynamic_update_slice(full, w, (x * height, place))
            place += w.shape[1]
        for part, owner in ((near, core), (far, 1 - core)):
            part = lax.slice_in_dim(part, at, at + columns, axis=1)
            full = lax.dynamic_update_slice(full, part, ((1 - x) * height + owner * half, 0))
        return full

    half_qkv = after(half_rows((w_query, w_key, w_value)), own_gains)
    near_qkv = links.over_x(half_qkv)
    near_ff = links.over_x(after(half_rows((w_output, w_gate, w_up)), near_qkv))
    full_qkv = assemble((w_query, w_key, w_value), near_qkv, links.over_core(near_qkv), 0)

    inputs = tokens.reshape(total, width).astype(F32)
    normed1, scale1 = norm_rows(inputs)
    hidden1 = (normed1 * gain1).astype(BF16)
    by_seq = after(hidden1, half_qkv).reshape(tokens.shape)
    mine, theirs = pick(by_seq, links.far), pick(by_seq, 1 - links.far)
    halves = join(mine[None], links.over_far(theirs)[None], links.far)
    groups = [list(range(layer.groups)), list(range(layer.groups, reps))]
    hidden1, halves, *layer.all_tables = fence(hidden1, halves, *layer.all_tables)
    hidden_mine = lax.all_gather(halves, "rep", axis_index_groups=groups, axis=1, tiled=True)
    hidden_mine = hidden_mine.reshape(layer.length, width)
    qkv = layer.to_heads(layer.project(hidden1, full_qkv, first_values), 3)
    qkv, hidden_mine = fence(qkv, hidden_mine)
    att, att_t, mass = layer.attend(qkv)
    att, near_ff, down_half = fence(att, near_ff, half_rows((w_down,)))
    near_down = links.over_x(down_half)
    far_ff = links.over_core(near_ff)
    full_output = assemble((w_output,), near_ff, far_ff, 0)
    full_gate_up = assemble((w_gate, w_up), near_ff, far_ff, w_output.shape[1])
    near_down = after(near_down, full_output, full_gate_up)
    full_down = assemble((w_down,), near_down, links.over_core(near_down), 0)
    attended = layer.to_tokens(att, 1)

    residual = inputs + dot(attended, full_output, (1, 0))
    normed2, scale2 = norm_rows(residual)
    hidden2 = (normed2 * gain2).astype(BF16)
    gate_up = dot(hidden2, full_gate_up, (1, 0))
    gate_pre, up_pre = gate_up[:, :ff], gate_up[:, ff:]
    sigma = jax.nn.sigmoid(gate_pre)
    swish = gate_pre * sigma
    swiglu = (swish * up_pre).astype(BF16)
    upstream = cotangent.reshape(total, width)

    def by_core(values, blocks):
        step = values.shape[1] // (2 * blocks)
        sides = [
            [values[:, (2 * b + side) * step : (2 * b + side + 1) * step] for b in range(blocks)]
            for side in range(2)
        ]
        low, high = (s[0] if blocks == 1 else jnp.concatenate(s, axis=1) for s in sides)
        return jnp.where(core == 0, low, high), jnp.where(core == 0, high, low)

    upstream_mine, upstream_other = by_core(upstream, 1)
    hidden2_mine, hidden2_other = by_core(hidden2, 2)
    down_send = dot(swiglu, upstream_other, (0, 0)).astype(BF16)
    grad_swiglu = dot(upstream, full_down, (1, 1))
    grad_gate_pre, grad_up_pre = gate_back(grad_swiglu, gate_pre, up_pre, sigma, swish)
    gate_send = dot(hidden2_other, grad_gate_pre, (0, 0)).astype(BF16)
    swiglu, gate_send, grad_gate_pre, grad_up_pre = fence(
        swiglu, gate_send, grad_gate_pre, grad_up_pre
    )
    gate_core = links.over_core(gate_send)
    down_total = add(dot(swiglu, upstream_mine, (0, 0)), links.over_core(down_send))
    down_half = links.half(down_total, 1 - x)
    down_total, down_half, grad_gate_pre, grad_up_pre = fence(
        down_total, down_half, grad_gate_pre, grad_up_pre
    )
    down_x = links.over_x(down_half)

    up_send = dot(hidden2_other, grad_up_pre, (0, 0)).astype(BF16)
    grad_gate_pre, up_send = fence(grad_gate_pre, up_send)
    up_core = links.over_core(up_send)
    gate_total = add(dot(hidden2_mine, grad_gate_pre, (0, 0)), gate_core)
    gate_half = links.quarters(gate_total, 1 - links.y)
    gate_total, gate_half, grad_gate_pre, grad_up_pre = fence(
        gate_total, gate_half, grad_gate_pre, grad_up_pre
    )

    up_total = add(dot(hidden2_mine, grad_up_pre, (0, 0)), up_core)
    up_half = links.half(up_total, 1 - x)
    up_total, up_half, grad_gate_pre, grad_up_pre = fence(
        up_total, up_half, grad_gate_pre, grad_up_pre
    )
    up_x = links.over_x(up_half)

    grad_gate_up = jnp.concatenate([grad_gate_pre, grad_up_pre], axis=1)
    grad_hidden2 = dot(grad_gate_up, full_gate_up, (1, 1))
    grad_residual = upstream.astype(F32) + norm_back(grad_hidden2 * gain2, normed2, scale2)
    grad_residual_low = grad_residual.astype(BF16)
    grad_attended = dot(grad_residual_low, full_output, (1, 1)).astype(BF16)
    grad_attended, grad_residual_low = fence(grad_attended, grad_residual_low)
    do = layer.to_heads(grad_attended, 1)
    attended_mine, attended_other = by_core(attended, 2)
    out_send = dot(attended_other, grad_residual_low, (0, 0)).astype(BF16)
    out_total = add(dot(attended_mine, grad_residual_low, (0, 0)), links.over_core(out_send))
    out_total, down_x = fence(out_total, down_x)
    down_first = add(links.half(down_total, x), down_x)
    down_y = links.over_y(links.half(down_first, 1 - links.y))
    out_x = links.over_x(links.half(out_total, 1 - x))
    output = (residual + dot(swiglu, full_down, (1, 0))).astype(BF16)
    do, gate_half, down_first, output = fence(do, gate_half, down_first, output)
    gate_y = links.over_y(gate_half)

    grad_raw_heads = layer.attend_back(qkv, do, att_t, mass)
    grad_raw_heads, up_x, out_x, down_y = fence(grad_raw_heads, up_x, out_x, down_y)
    down_second = add(links.half(down_first, links.y), down_y)
    down_pair = links.over_pair(links.half(down_second, 1 - links.near))

    up_first = add(links.half(up_total, x), up_x)
    out_first = add(links.half(out_total, x), out_x)
    up_y = links.over_y(links.half(up_first, 1 - links.y))
    out_y = links.over_y(links.half(out_first, 1 - links.y))
    columns = dot(hidden_mine, grad_raw_heads, (0, 0)).astype(BF16)
    columns_x = links.over_x(links.half(columns, 1 - x))
    columns_x, grad_raw_heads, down_pair, gate_y = fence(
        columns_x, grad_raw_heads, down_pair, gate_y
    )
    gate_first = add(links.quarters(gate_total, links.y), gate_y)
    gate_x = links.over_x(links.half(gate_first, 1 - x))
    down_third = add(links.half(down_second, links.near), down_pair)
    down_far = links.over_far(links.half(down_third, 1 - links.far))
    grad_raw = layer.to_tokens(grad_raw_heads, 3)
    summed = layer.sum_sequences(add(links.half(columns, x), columns_x))
    gate_x, up_y, out_y, down_far, summed = fence(gate_x, up_y, out_y, down_far, summed)
    gate_second = add(links.half(gate_first, x), gate_x)
    down_piece = add(links.half(down_third, links.far), down_far)
    joined = jnp.concatenate(
        [
            gate_second,
            add(links.half(up_first, links.y), up_y),
            add(links.half(out_first, links.y), out_y),
        ],
        axis=1,
    )

    joined, down_piece, summed = fence(joined, down_piece, summed)
    joined_pair = links.over_pair(links.half(joined, 1 - links.near))
    summed = join(summed, links.over_far(summed), links.far)
    down_piece = join(down_piece, links.over_far(down_piece), links.far)
    joined_third = add(links.half(joined, links.near), joined_pair)
    joined_third, down_piece, summed, grad_raw = fence(joined_third, down_piece, summed, grad_raw)

    joined_far = links.over_far(links.half(joined_third, 1 - links.far))
    summed = join(summed, links.over_y(summed), links.y)
    down_piece = join(down_piece, links.over_pair(down_piece), links.near)
    grad_first = grad_raw[:, 2 * width :].astype(F32)
    grad_hidden1 = dot(grad_raw, full_qkv, (1, 1))
    grad_inputs = grad_residual + norm_back(grad_hidden1 * gain1, normed1, scale1)
    joined_piece = add(links.half(joined_third, links.far), joined_far)
    joined_piece, down_piece, summed, grad_inputs, grad_first = fence(
        joined_piece, down_piece, summed, grad_inputs, grad_first
    )

    joined_far = links.over_far(joined_piece)
    summed = join(summed, links.over_pair(summed), links.near)
    down_y = links.over_y(down_piece)
    down_piece = join(down_piece, down_y, links.y)
    part = join(joined_piece, joined_far, links.far)
    part, down_piece, summed = fence(part, down_piece, summed)

    def slots(*bits):
        place = [
            (core ^ c) * 4 + (links.y ^ y) * 2 + (links.near ^ near) for c, y, near in bits
        ]
        return jnp.stack(place).astype(jnp.int32)

    part_pair = links.over_pair(part)
    part_y = links.over_y(part)
    part_core = links.over_core(part)
    down_other = links.over_core(down_piece)
    grad_down = jnp.where(
        core == 0,
        jnp.concatenate([down_piece, down_other], axis=1),
        jnp.concatenate([down_other, down_piece], axis=1),
    ).astype(F32)
    grad_wquery, grad_wkey, grad_wvalue, sums = spread(
        core,
        summed,
        links.over_core(summed),
        w_query,
        w_key,
        w_value,
        layer.seqs,
        layer.groups,
    )
    part_pair, part_y, grad_down, grad_wquery, grad_wkey, grad_wvalue = fence(
        part_pair, part_y, grad_down, grad_wquery, grad_wkey, grad_wvalue
    )
    middle = part.shape[0] // 2
    last = (links.over_y(part_pair[:middle]), links.over_pair(part_y[middle:]))
    pair_core, y_core = links.over_core(part_pair), links.over_core(part_y)

    early = slots((0, 0, 0), (1, 0, 0), (0, 0, 1), (0, 1, 0), (1, 0, 1), (1, 1, 0))
    early_parts = (part, part_core, part_pair, part_y, pair_core, y_core)
    low, high, *filled = fence(*last, *finish(early, early_parts, w_gate, w_up, ()))
    late = slots((0, 1, 1), (1, 1, 1))
    late = jnp.concatenate([2 * late, 2 * late + 1])
    late_parts = (low, links.over_core(low), high, links.over_core(high))
    grad_wgate, grad_wup, grad_outproj, ff_sums = finish(late, late_parts, w_gate, w_up, filled)
    shape = tokens.shape
    return (
        output.reshape(shape),
        grad_inputs.reshape(shape),
        grad_first.reshape(shape),
        grad_wquery,
        grad_wkey,
        grad_wvalue,
        grad_outproj,
        grad_wgate,
        grad_wup,
        grad_down,
        jnp.sum(sums, axis=1) / gain_attn.astype(F32),
        jnp.sum(ff_sums, axis=1) / gain_ffn.astype(F32),
    )


def solution(mesh):
    sequence = P("shard", "rep", None)
    matrix = P("shard", None)
    vector = P("shard")
    reps, shards = mesh.shape["rep"], mesh.shape["shard"]
    linked = reps == 16 and shards == 2
    return jax.shard_map(
        functools.partial(local_linked if linked else local, reps),
        mesh=mesh,
        in_specs=(sequence, sequence, vector, sequence) + (matrix,) * 7 + (vector,) * 2,
        out_specs=(sequence,) * 3 + (matrix,) * 7 + (vector,) * 2,
        check_vma=False,
    )
```

```python
import functools

import jax
import jax.numpy as jnp
from jax import lax
from jax.experimental import pallas as pl
from jax.experimental.pallas import tpu as pltpu
from jax.sharding import PartitionSpec as P

HEADS = 16
EPSILON = 1e-05
NEGATIVE = -1e30
ROPE_BASE = 10000.0
BF16 = jnp.bfloat16
F32 = jnp.float32
VMEM_LIMIT = 60 * 1024 * 1024


def dot(left, right, contract):
    return lax.dot_general(
        left, right, ((contract[:1], contract[1:]), ((), ())), preferred_element_type=F32
    )


def norm_rows(values):
    scale = lax.rsqrt(jnp.mean(values * values, axis=-1, keepdims=True) + EPSILON)
    return (values * scale, scale)


def norm_back(gradient, normed, scale):
    return scale * (gradient - normed * jnp.mean(gradient * normed, axis=-1, keepdims=True))


def rope_lanes(positions, lanes, head_dim):
    half = head_dim // 2
    lane = jnp.arange(lanes, dtype=jnp.int32) % head_dim
    frequency = ROPE_BASE ** (-2.0 * (lane % half).astype(F32) / head_dim)
    angles = positions.astype(F32)[:, None] * frequency[None, :]
    sign = jnp.where(lane < half, 1.0, -1.0).astype(F32)
    return (jnp.cos(angles), jnp.sin(angles) * sign[None, :])


def partner(values, head_dim, roll):
    half = head_dim // 2
    lane = lax.broadcasted_iota(jnp.int32, values.shape, values.ndim - 1) % head_dim
    return jnp.where(lane < half, roll(values, half), roll(values, -half))


def lane_roll(values, shift):
    return jnp.roll(values, -shift, axis=-1)


def kernel_roll(values, shift):
    width = values.shape[-1]
    if width % 128 == 0:
        return pltpu.roll(values, (-shift) % width, axis=values.ndim - 1)
    shift = shift % width
    return jnp.concatenate([values[..., shift:], values[..., :shift]], axis=-1)


def head_rows(values, head, head_dim):
    if values.shape[-1] == head_dim:
        return values
    lane = lax.broadcasted_iota(jnp.int32, values.shape, values.ndim - 1)
    mine = (lane >= head * head_dim) & (lane < (head + 1) * head_dim)
    return jnp.where(mine, values, jnp.zeros_like(values))


def masked_scores(key_block, query_block, key_start, query_start, prefix):
    scores = dot(key_block, query_block, (1, 1))
    query_pos = query_start + lax.broadcasted_iota(jnp.int32, (1, scores.shape[1]), 1)
    last = jnp.maximum(query_pos, prefix - 1) - key_start
    key_pos = lax.broadcasted_iota(jnp.int32, scores.shape, 0)
    return jnp.where(key_pos <= last, scores, NEGATIVE)


def attend_kernel(
    head_dim, bq, bk, prefix_ref, q_ref, k_ref, v_ref, att_ref, att_t_ref, mass_ref, v_t, acc
):
    length, width = q_ref.shape
    heads = width // head_dim
    prefix = prefix_ref[0]
    for start in range(0, length, 128):
        v_t[:, start : start + 128] = v_ref[start : start + 128, :].T

    def query_step(i, carry):
        q0 = pl.multiple_of(i * bq, bq)
        q_all = q_ref[pl.ds(q0, bq), :]
        q_heads = [head_rows(q_all, h, head_dim) for h in range(heads)]
        acc[...] = jnp.zeros_like(acc)
        blocks = (jnp.maximum(q0 + bq, prefix) + bk - 1) // bk

        def key_step(j, stats):
            k0 = pl.multiple_of(j * bk, bk)
            k_block = k_ref[pl.ds(k0, bk), :]
            out = []
            for h in range(heads):
                peak, mass = stats[h]
                scores = masked_scores(k_block, q_heads[h], k0, q0, prefix)
                new_peak = jnp.maximum(peak, jnp.max(scores, axis=0, keepdims=True))
                alpha = jnp.exp(peak - new_peak)
                weights = jnp.exp(scores - new_peak)
                mass = mass * alpha + jnp.sum(weights, axis=0, keepdims=True)
                rows = slice(h * head_dim, (h + 1) * head_dim)
                acc[rows, :] = acc[rows, :] * alpha + dot(
                    v_t[rows, pl.ds(k0, bk)], weights.astype(BF16), (1, 0)
                )
                out.append((new_peak, mass))
            return tuple(out)

        first = tuple(
            (jnp.full((1, bq), NEGATIVE, F32), jnp.zeros((1, bq), F32)) for _ in range(heads)
        )
        stats = lax.fori_loop(0, blocks, key_step, first)
        for h in range(heads):
            peak, mass = stats[h]
            rows = slice(h * head_dim, (h + 1) * head_dim)
            att_t_ref[rows, pl.ds(q0, bq)] = acc[rows, :] / mass
            mass_ref[h : h + 1, pl.ds(q0, bq)] = peak + jnp.log(mass)
        for part in range(0, bq, 128):
            place = pl.ds(pl.multiple_of(q0 + part, 128), 128)
            att_ref[place, :] = att_t_ref[:, place].T.astype(BF16)
        return carry

    lax.fori_loop(0, length // bq, query_step, 0)


def attend_back_kernel(
    head_dim,
    bq,
    bk,
    prefix_ref,
    q_ref,
    k_ref,
    v_ref,
    do_ref,
    att_t_ref,
    mass_ref,
    cos_ref,
    sin_ref,
    out_ref,
    k_t,
    delta,
    dq_t,
    dk_acc,
    dv_acc,
):
    length, width = q_ref.shape
    heads = width // head_dim
    prefix = prefix_ref[0]
    dq_t[...] = jnp.zeros_like(dq_t)
    for start in range(0, length, 128):
        place = slice(start, start + 128)
        k_t[:, place] = k_ref[place, :].T
        product = do_ref[place, :].astype(F32).T * att_t_ref[:, place]
        for h in range(heads):
            rows = slice(h * head_dim, (h + 1) * head_dim)
            delta[h : h + 1, place] = jnp.sum(product[rows, :], axis=0, keepdims=True)

    def rope_back(gradient, place):
        return gradient * cos_ref[place, :] + partner(gradient, head_dim, kernel_roll) * sin_ref[
            place, :
        ]

    def key_step(j, carry):
        k0 = pl.multiple_of(j * bk, bk)
        k_block = k_ref[pl.ds(k0, bk), :]
        v_block = v_ref[pl.ds(k0, bk), :]
        dk_acc[...] = jnp.zeros_like(dk_acc)
        dv_acc[...] = jnp.zeros_like(dv_acc)
        begin = jnp.where(k0 < prefix, 0, k0 // bq)

        def query_step(i, inner):
            q0 = pl.multiple_of(i * bq, bq)
            q_all = q_ref[pl.ds(q0, bq), :]
            do_all = do_ref[pl.ds(q0, bq), :]
            for h in range(heads):
                rows = slice(h * head_dim, (h + 1) * head_dim)
                q_head = head_rows(q_all, h, head_dim)
                do_head = head_rows(do_all, h, head_dim)
                scores = masked_scores(k_block, q_head, k0, q0, prefix)
                weights = jnp.exp(scores - mass_ref[h : h + 1, pl.ds(q0, bq)])
                grad_weights = dot(v_block, do_head, (1, 1))
                grad_scores = (weights * (grad_weights - delta[h : h + 1, pl.ds(q0, bq)])).astype(
                    BF16
                )
                dv_acc[...] += dot(weights.astype(BF16), do_head, (1, 0))
                dk_acc[...] += dot(grad_scores, q_head, (1, 0))
                dq_t[rows, pl.ds(q0, bq)] += dot(k_t[rows, pl.ds(k0, bk)], grad_scores, (1, 0))
            return inner

        lax.fori_loop(begin, length // bq, query_step, 0)
        place = pl.ds(k0, bk)
        out_ref[place, width : 2 * width] = rope_back(dk_acc[...], place).astype(BF16)
        out_ref[place, 2 * width :] = dv_acc[...].astype(BF16) * jnp.array(0.5, BF16)
        return carry

    lax.fori_loop(0, length // bk, key_step, 0)
    for start in range(0, length, 128):
        place = slice(start, start + 128)
        out_ref[place, :width] = rope_back(dq_t[:, place].T * 0.125, place).astype(BF16)


def turns(reps, move):
    pairs = []
    for here in range(reps):
        z, y, core = move(here // 4, (here // 2) % 2, here % 2)
        pairs.append((here, (z % (reps // 4)) * 4 + y * 2 + core))
    return pairs


class Links:
    def __init__(self, reps):
        self.to_core = turns(reps, lambda z, y, core: (z, y, 1 - core))
        self.to_y = turns(reps, lambda z, y, core: (z, 1 - y, core))
        self.to_pair = turns(reps, lambda z, y, core: (z ^ 1, y, core))
        self.to_far = turns(reps, lambda z, y, core: (z ^ 2, y, core))
        here = lax.axis_index("rep")
        self.near, self.far = (here // 4) % 2, here // 8
        self.y, self.core = (here // 2) % 2, here % 2
        self.x = lax.axis_index("shard")

    def over_core(self, value):
        return lax.ppermute(value, "rep", self.to_core)

    def over_x(self, value):
        return lax.ppermute(value, "shard", [(0, 1), (1, 0)])

    def over_y(self, value):
        return lax.ppermute(value, "rep", self.to_y)

    def over_pair(self, value):
        return lax.ppermute(value, "rep", self.to_pair)

    def over_far(self, value):
        return lax.ppermute(value, "rep", self.to_far)

    def half(self, total, side):
        return pick(total.reshape(2, -1, total.shape[1]), side)

    def quarters(self, total, side):
        columns = total.shape[1]
        return pick(total.reshape(2, 2, -1, columns), side, 1).reshape(-1, columns)


def pick(values, index, axis=0):
    return lax.dynamic_index_in_dim(values, index, axis, keepdims=False)


def put(values, part, index):
    return lax.dynamic_update_index_in_dim(values, part, index, 0)


def join(mine, other, index):
    first = jnp.concatenate([mine, other], axis=0)
    second = jnp.concatenate([other, mine], axis=0)
    return jnp.where(index == 0, first, second)


def fence(*values):
    return lax.optimization_barrier(values)


def after(value, *earlier):
    return lax.optimization_barrier((value,) + earlier)[0]


def blank(shape, dtype):
    return pl.pallas_call(
        lambda out_ref: None,
        out_shape=jax.ShapeDtypeStruct(shape, dtype),
        out_specs=pl.BlockSpec(memory_space=pl.ANY),
    )()


def add(left, right):
    return (left.astype(F32) + right.astype(F32)).astype(BF16)


def whole(shape):
    return pl.BlockSpec(shape, lambda *_: (0,) * len(shape))


def thirds(qkv):
    length, width = qkv.shape[0], qkv.shape[1] // 3
    if width % 128 == 0:
        specs = [pl.BlockSpec((length, width), lambda *_, at=at: (0, at)) for at in range(3)]
        return (qkv, qkv, qkv), specs
    parts = tuple(qkv[:, at * width : (at + 1) * width] for at in range(3))
    return parts, [whole((length, width))] * 3


def attend(prefix, qkv, head_dim, bq, bk):
    length, width = qkv.shape[0], qkv.shape[1] // 3
    heads = width // head_dim
    flops = 2 * 2 * heads * length * length * head_dim
    operands, specs = thirds(qkv)
    return pl.pallas_call(
        functools.partial(attend_kernel, head_dim, bq, bk),
        out_shape=(
            jax.ShapeDtypeStruct((length, width), BF16),
            jax.ShapeDtypeStruct((width, length), F32),
            jax.ShapeDtypeStruct((heads, length), F32),
        ),
        grid_spec=pltpu.PrefetchScalarGridSpec(
            num_scalar_prefetch=1,
            grid=(1,),
            in_specs=specs,
            out_specs=[whole((length, width)), whole((width, length)), whole((heads, length))],
            scratch_shapes=[pltpu.VMEM((width, length), BF16), pltpu.VMEM((width, bq), F32)],
        ),
        compiler_params=pltpu.CompilerParams(vmem_limit_bytes=VMEM_LIMIT),
        cost_estimate=pl.CostEstimate(flops=1, transcendentals=0, bytes_accessed=1),
    )(prefix, *operands)


def attend_back(prefix, qkv, do, att_t, mass, cosine, sine, head_dim, bq, bk):
    length, width = qkv.shape[0], qkv.shape[1] // 3
    heads = width // head_dim
    flops = 5 * 2 * heads * length * length * head_dim
    rows = whole((length, width))
    operands, specs = thirds(qkv)
    return pl.pallas_call(
        functools.partial(attend_back_kernel, head_dim, bq, bk),
        out_shape=jax.ShapeDtypeStruct((length, 3 * width), BF16),
        grid_spec=pltpu.PrefetchScalarGridSpec(
            num_scalar_prefetch=1,
            grid=(1,),
            in_specs=specs + [rows, whole((width, length)), whole((heads, length)), rows, rows],
            out_specs=whole((length, 3 * width)),
            scratch_shapes=[
                pltpu.VMEM((width, length), BF16),
                pltpu.VMEM((heads, length), F32),
                pltpu.VMEM((width, length), F32),
                pltpu.VMEM((bk, width), F32),
                pltpu.VMEM((bk, width), F32),
            ],
        ),
        compiler_params=pltpu.CompilerParams(vmem_limit_bytes=VMEM_LIMIT),
        cost_estimate=pl.CostEstimate(flops=1, transcendentals=0, bytes_accessed=1),
    )(prefix, *operands, do, att_t, mass, cosine, sine)


def spread_kernel(lanes, core_ref, mine_ref, other_ref, wq_ref, wk_ref, wv_ref, *out_refs):
    sum_ref = out_refs[3]
    core = core_ref[0]
    total = jnp.zeros(sum_ref.shape, F32)
    for near in range(2):
        for y in range(2):
            mine, other = mine_ref[near, y, 0], other_ref[near, y, 0]
            for side, part in enumerate((mine, other)):
                part = jnp.where(core == 0, part, other if side == 0 else mine)
                group = near * 4 + y * 2 + side
                place = slice(group * lanes, (group + 1) * lanes)
                for at, w_ref in enumerate((wq_ref, wk_ref, wv_ref)):
                    values = part[:, at * lanes : (at + 1) * lanes].astype(F32)
                    out_refs[at][:, place] = values
                    total += values * w_ref[:, place].astype(F32)
    sum_ref[...] = total


def spread(core, mine, other, w_query, w_key, w_value, seqs, groups):
    height, width = w_query.shape
    share, lanes = height // seqs, width // groups
    steps = 4
    rows = share // steps
    tile = pl.BlockSpec((rows, width), lambda s, i, core: (s * steps + i, 0))
    part = pl.BlockSpec((2, 2, 1, rows, 3 * lanes), lambda s, i, core: (0, 0, s, i, 0))
    shape = (2, 2, seqs, share, 3 * lanes)
    return pl.pallas_call(
        functools.partial(spread_kernel, lanes),
        out_shape=(jax.ShapeDtypeStruct((height, width), F32),) * 3
        + (jax.ShapeDtypeStruct((height, lanes), F32),),
        grid_spec=pltpu.PrefetchScalarGridSpec(
            num_scalar_prefetch=1,
            grid=(seqs, steps),
            in_specs=[part, part, tile, tile, tile],
            out_specs=[tile, tile, tile]
            + [pl.BlockSpec((rows, lanes), lambda s, i, core: (s * steps + i, 0))],
        ),
        cost_estimate=pl.CostEstimate(flops=1, transcendentals=0, bytes_accessed=1),
    )(
        core.reshape(1).astype(jnp.int32),
        mine.reshape(shape),
        other.reshape(shape),
        w_query,
        w_key,
        w_value,
    )


def finish_kernel(count, ff, slots_ref, *refs):
    parts, (gate_ref, up_ref) = refs[:count], refs[count : count + 2]
    grad_gate_ref, grad_up_ref, grad_out_ref, sum_ref, buffer, arrived = refs[-6:]
    step = pl.program_id(0)

    def fetch(at):
        return pltpu.make_async_copy(parts[at], buffer.at[at % 2], arrived.at[at % 2])

    for at in range(count):

        @pl.when(step == max(at - 1, 0))
        def _():
            fetch(at).start()

    for at in range(count):

        @pl.when(step == at)
        def _():
            fetch(at).wait()

    here = lax.rem(step, 2)
    lanes = sum_ref.shape[1]
    total = jnp.zeros(sum_ref.shape, F32)
    for start in range(0, ff, lanes):
        place = slice(start, start + lanes)
        grad_gate = buffer[here, :, place].astype(F32)
        grad_up = buffer[here, :, ff + start : ff + start + lanes].astype(F32)
        grad_gate_ref[:, place] = grad_gate
        grad_up_ref[:, place] = grad_up
        total += grad_gate * gate_ref[:, place].astype(F32)
        total += grad_up * up_ref[:, place].astype(F32)
    sum_ref[...] = total
    grad_out_ref[...] = buffer[here, :, 2 * ff :].astype(F32)


def finish(slots, parts, w_gate, w_up, filled):
    height, ff = w_gate.shape
    share, columns = parts[0].shape
    count = len(parts)

    def rows(width):
        return pl.BlockSpec((share, width), lambda i, slots: (slots[i], 0))

    anywhere = pl.BlockSpec(memory_space=pl.ANY)
    widths = (ff, ff, columns - 2 * ff, 128)
    return pl.pallas_call(
        functools.partial(finish_kernel, count, ff),
        out_shape=tuple(jax.ShapeDtypeStruct((height, width), F32) for width in widths),
        grid_spec=pltpu.PrefetchScalarGridSpec(
            num_scalar_prefetch=1,
            grid=(count,),
            in_specs=[anywhere] * count + [rows(ff), rows(ff)] + [anywhere] * len(filled),
            out_specs=[rows(width) for width in widths],
            scratch_shapes=[
                pltpu.VMEM((2, share, columns), BF16),
                pltpu.SemaphoreType.DMA((2,)),
            ],
        ),
        input_output_aliases={count + 3 + at: at for at in range(len(filled))},
        compiler_params=pltpu.CompilerParams(vmem_limit_bytes=VMEM_LIMIT),
        cost_estimate=pl.CostEstimate(flops=1, transcendentals=0, bytes_accessed=1),
    )(slots, *parts, w_gate, w_up, *filled)


class Layer:
    def __init__(self, reps, tokens, prefix_len):
        self.reps = reps
        self.seqs, self.rows, self.width = tokens.shape
        self.head_dim = self.width // HEADS
        self.length = self.rows * reps
        self.groups = reps // self.seqs
        self.lanes = self.width // self.groups
        self.total = self.seqs * self.rows
        self.block = min(512, self.length)
        here = lax.axis_index("rep")
        self.my_seq = here // self.groups
        positions = here * self.rows + jnp.arange(self.rows, dtype=jnp.int32)
        cosine, sine = rope_lanes(positions, self.width, self.head_dim)
        self.cosine = jnp.tile(cosine, (self.seqs, 1))
        self.sine = jnp.tile(sine, (self.seqs, 1))
        self.all_tables = rope_lanes(
            jnp.arange(self.length, dtype=jnp.int32), self.lanes, self.head_dim
        )
        self.prefix = lax.dynamic_slice_in_dim(prefix_len, self.my_seq, 1, 0)

    def to_heads(self, values, parts):
        shape = (self.seqs, self.rows, parts, self.groups, self.lanes)
        chunks = values.reshape(shape).transpose(0, 3, 1, 2, 4)
        chunks = chunks.reshape(self.reps * self.rows, parts * self.lanes)
        return lax.all_to_all(chunks, "rep", 0, 0, tiled=True)

    def to_tokens(self, values, parts):
        chunks = lax.all_to_all(values, "rep", 0, 0, tiled=True)
        chunks = chunks.reshape(self.seqs, self.groups, self.rows, parts, self.lanes)
        return chunks.transpose(0, 2, 3, 1, 4).reshape(self.total, parts * self.width)

    def project(self, hidden, full_qkv, first_values):
        width = self.width
        raw = dot(hidden, full_qkv, (1, 0))

        def rope(values):
            return values * self.cosine - partner(values, self.head_dim, lane_roll) * self.sine

        query_rot = (rope(raw[:, :width]) * 0.125).astype(BF16)
        key_rot = rope(raw[:, width : 2 * width]).astype(BF16)
        first = first_values.reshape(self.total, width).astype(F32)
        value_mix = (0.5 * raw[:, 2 * width :] + 0.5 * first).astype(BF16)
        return jnp.concatenate([query_rot, key_rot, value_mix], axis=1)

    def attend(self, qkv):
        return attend(self.prefix, qkv, self.head_dim, self.block, self.block)

    def attend_back(self, qkv, do, att_t, mass):
        return attend_back(
            self.prefix, qkv, do, att_t, mass, *self.all_tables, self.head_dim, self.block, self.block
        )

    def sum_sequences(self, columns):
        share = columns.shape[0] // self.seqs
        mine = lax.dynamic_slice_in_dim(columns, self.my_seq * share, share, 0).astype(F32)
        for turn in range(1, self.seqs):
            slot = (self.my_seq + turn) % self.seqs
            sent = lax.dynamic_slice_in_dim(columns, slot * share, share, 0)
            moves = [
                (s * self.groups + g, ((s + turn) % self.seqs) * self.groups + g)
                for s in range(self.seqs)
                for g in range(self.groups)
            ]
            mine = mine + lax.ppermute(sent, "rep", moves).astype(F32)
        return mine.astype(BF16)


def gain_gradient(gain, *pairs):
    total = sum(jnp.sum(w.astype(F32) * gradient, axis=1) for w, gradient in pairs)
    return total / gain.astype(F32)


def gate_back(grad_swiglu, gate_pre, up_pre, sigma, swish):
    grad_gate_pre = grad_swiglu * up_pre * sigma * (1.0 + gate_pre * (1.0 - sigma))
    return (grad_gate_pre.astype(BF16), (grad_swiglu * swish).astype(BF16))


def local(
    reps,
    tokens,
    first_values,
    prefix_len,
    cotangent,
    w_query,
    w_key,
    w_value,
    w_output,
    w_gate,
    w_up,
    w_down,
    gain_attn,
    gain_ffn,
):
    layer = Layer(reps, tokens, prefix_len)
    total, width, ff = layer.total, layer.width, w_gate.shape[1]
    here = lax.axis_index("rep")

    def gather(weights):
        height = weights[0].shape[0]
        share = height // reps
        if share * reps == height and share % 8 == 0:
            pieces = [lax.dynamic_slice_in_dim(w, here * share, share, 0) for w in weights]
            axes = ("shard", "rep")
        else:
            pieces, axes = list(weights), ("shard",)
        piece = pieces[0] if len(pieces) == 1 else jnp.concatenate(pieces, axis=1)
        return lax.all_gather(piece, axes, axis=0, tiled=True)

    gains = lax.all_gather(jnp.stack([gain_attn, gain_ffn]), "shard", axis=1, tiled=True)
    full_qkv = gather((w_query, w_key, w_value))
    full_output = gather((w_output,))
    full_gate_up = gather((w_gate, w_up))
    full_down = gather((w_down,))
    gain1 = gains[0].astype(F32)
    gain2 = gains[1].astype(F32)

    inputs = tokens.reshape(total, width).astype(F32)
    normed1, scale1 = norm_rows(inputs)
    hidden1 = (normed1 * gain1).astype(BF16)
    hidden1_all = lax.all_gather(hidden1.reshape(tokens.shape), "rep", axis=1, tiled=True)
    qkv = layer.to_heads(layer.project(hidden1, full_qkv, first_values), 3)
    att, att_t, mass = layer.attend(qkv)
    attended = layer.to_tokens(att, 1)

    residual = inputs + dot(attended, full_output, (1, 0))
    normed2, scale2 = norm_rows(residual)
    hidden2 = (normed2 * gain2).astype(BF16)
    gate_up = dot(hidden2, full_gate_up, (1, 0))
    gate_pre, up_pre = gate_up[:, :ff], gate_up[:, ff:]
    sigma = jax.nn.sigmoid(gate_pre)
    swish = gate_pre * sigma
    swiglu = (swish * up_pre).astype(BF16)
    output = (residual + dot(swiglu, full_down, (1, 0))).astype(BF16)

    upstream = cotangent.reshape(total, width)
    grad_swiglu = dot(upstream, full_down, (1, 1))
    grad_gate_up = jnp.concatenate(gate_back(grad_swiglu, gate_pre, up_pre, sigma, swish), axis=1)
    grad_hidden2 = dot(grad_gate_up, full_gate_up, (1, 1))
    grad_residual = upstream.astype(F32) + norm_back(grad_hidden2 * gain2, normed2, scale2)
    grad_residual_low = grad_residual.astype(BF16)
    grad_attended = dot(grad_residual_low, full_output, (1, 1)).astype(BF16)

    def reduce_gather(partial):
        axes = ("shard", "rep")
        piece = lax.psum_scatter(partial.astype(BF16), axes, scatter_dimension=0, tiled=True)
        return lax.all_gather(piece, "rep", axis=0, tiled=True).astype(F32)

    grad_down = reduce_gather(dot(swiglu, upstream, (0, 0)))
    grad_wgate_up = reduce_gather(dot(hidden2, grad_gate_up, (0, 0)))
    grad_outproj = reduce_gather(dot(attended, grad_residual_low, (0, 0)))
    grad_wgate, grad_wup = grad_wgate_up[:, :ff], grad_wgate_up[:, ff:]

    do = layer.to_heads(grad_attended, 1)
    grad_raw_heads = layer.attend_back(qkv, do, att_t, mass)
    grad_raw = layer.to_tokens(grad_raw_heads, 3)
    grad_first = grad_raw[:, 2 * width :].astype(F32)
    grad_hidden1 = dot(grad_raw, full_qkv, (1, 1))
    grad_inputs = grad_residual + norm_back(grad_hidden1 * gain1, normed1, scale1)

    hidden_mine = lax.dynamic_index_in_dim(hidden1_all, layer.my_seq, 0, keepdims=False)
    columns = dot(hidden_mine, grad_raw_heads, (0, 0)).astype(BF16)
    columns = lax.psum_scatter(columns, "shard", scatter_dimension=0, tiled=True)
    height = columns.shape[0]
    mine = layer.sum_sequences(columns)
    gathered = lax.all_gather(mine, "rep", axis=0, tiled=True)
    gathered = gathered.reshape(layer.seqs, layer.groups, -1, 3, layer.lanes)
    grad_wqkv = gathered.transpose(3, 0, 2, 1, 4).reshape(3, height, width).astype(F32)
    shape = tokens.shape
    return (
        output.reshape(shape),
        grad_inputs.reshape(shape),
        grad_first.reshape(shape),
        grad_wqkv[0],
        grad_wqkv[1],
        grad_wqkv[2],
        grad_outproj,
        grad_wgate,
        grad_wup,
        grad_down,
        gain_gradient(
            gain_attn, (w_query, grad_wqkv[0]), (w_key, grad_wqkv[1]), (w_value, grad_wqkv[2])
        ),
        gain_gradient(gain_ffn, (w_gate, grad_wgate), (w_up, grad_wup)),
    )


def local_linked(
    reps,
    tokens,
    first_values,
    prefix_len,
    cotangent,
    w_query,
    w_key,
    w_value,
    w_output,
    w_gate,
    w_up,
    w_down,
    gain_attn,
    gain_ffn,
):
    layer = Layer(reps, tokens, prefix_len)
    links = Links(reps)
    total, width, ff = layer.total, layer.width, w_gate.shape[1]
    core, x = links.core, links.x

    own_gains = jnp.stack([gain_attn, gain_ffn])
    other_gains = links.over_x(own_gains)
    gains = jnp.where(
        x == 0,
        jnp.concatenate([own_gains, other_gains], axis=1),
        jnp.concatenate([other_gains, own_gains], axis=1),
    )
    gain1 = gains[0].astype(F32)
    gain2 = gains[1].astype(F32)

    def half_rows(weights):
        half = weights[0].shape[0] // 2
        pieces = [lax.dynamic_slice_in_dim(w, core * half, half, 0) for w in weights]
        return pieces[0] if len(pieces) == 1 else jnp.concatenate(pieces, axis=1)

    def assemble(weights, near, far, at):
        height = weights[0].shape[0]
        half = near.shape[0]
        columns = sum(w.shape[1] for w in weights)
        full = blank((2 * height, columns), BF16)
        place = 0
        for w in weights:
            full = lax.dynamic_update_slice(full, w, (x * height, place))
            place += w.shape[1]
        for part, owner in ((near, core), (far, 1 - core)):
            part = lax.slice_in_dim(part, at, at + columns, axis=1)
            full = lax.dynamic_update_slice(full, part, ((1 - x) * height + owner * half, 0))
        return full

    half_qkv = after(half_rows((w_query, w_key, w_value)), own_gains)
    near_qkv = links.over_x(half_qkv)
    near_ff = links.over_x(after(half_rows((w_output, w_gate, w_up)), near_qkv))
    full_qkv = assemble((w_query, w_key, w_value), near_qkv, links.over_core(near_qkv), 0)

    inputs = tokens.reshape(total, width).astype(F32)
    normed1, scale1 = norm_rows(inputs)
    hidden1 = (normed1 * gain1).astype(BF16)
    by_seq = after(hidden1, half_qkv).reshape(tokens.shape)
    mine, theirs = pick(by_seq, links.far), pick(by_seq, 1 - links.far)
    halves = join(mine[None], links.over_far(theirs)[None], links.far)
    groups = [list(range(layer.groups)), list(range(layer.groups, reps))]
    hidden1, halves, *layer.all_tables = fence(hidden1, halves, *layer.all_tables)
    hidden_mine = lax.all_gather(halves, "rep", axis_index_groups=groups, axis=1, tiled=True)
    hidden_mine = hidden_mine.reshape(layer.length, width)
    qkv = layer.to_heads(layer.project(hidden1, full_qkv, first_values), 3)
    qkv, hidden_mine = fence(qkv, hidden_mine)
    att, att_t, mass = layer.attend(qkv)
    att, near_ff, down_half = fence(att, near_ff, half_rows((w_down,)))
    near_down = links.over_x(down_half)
    far_ff = links.over_core(near_ff)
    full_output = assemble((w_output,), near_ff, far_ff, 0)
    full_gate_up = assemble((w_gate, w_up), near_ff, far_ff, w_output.shape[1])
    attended = layer.to_tokens(att, 1)
    height = w_down.shape[0]
    own_down = lax.dynamic_update_slice(blank((2 * height, width), BF16), w_down, (x * height, 0))
    attended, own_down = fence(attended, own_down)

    residual = inputs + dot(attended, full_output, (1, 0))
    normed2, scale2 = norm_rows(residual)
    hidden2 = (normed2 * gain2).astype(BF16)
    gate_up = dot(hidden2, full_gate_up, (1, 0))
    gate_pre, up_pre = gate_up[:, :ff], gate_up[:, ff:]
    sigma = jax.nn.sigmoid(gate_pre)
    swish = gate_pre * sigma
    swiglu = (swish * up_pre).astype(BF16)
    near_down = after(near_down, swiglu)
    full_down = own_down
    for part, owner in ((near_down, core), (links.over_core(near_down), 1 - core)):
        row = (1 - x) * height + owner * (height // 2)
        full_down = lax.dynamic_update_slice(full_down, part, (row, 0))
    upstream = cotangent.reshape(total, width)

    def by_core(values, blocks):
        step = values.shape[1] // (2 * blocks)
        sides = [
            [values[:, (2 * b + side) * step : (2 * b + side + 1) * step] for b in range(blocks)]
            for side in range(2)
        ]
        low, high = (s[0] if blocks == 1 else jnp.concatenate(s, axis=1) for s in sides)
        return jnp.where(core == 0, low, high), jnp.where(core == 0, high, low)

    upstream_mine, upstream_other = by_core(upstream, 1)
    hidden2_mine, hidden2_other = by_core(hidden2, 2)
    down_send = dot(swiglu, upstream_other, (0, 0)).astype(BF16)
    grad_swiglu = dot(upstream, full_down, (1, 1))
    grad_gate_pre, grad_up_pre = gate_back(grad_swiglu, gate_pre, up_pre, sigma, swish)
    gate_send = dot(hidden2_other, grad_gate_pre, (0, 0)).astype(BF16)
    swiglu, gate_send, grad_gate_pre, grad_up_pre = fence(
        swiglu, gate_send, grad_gate_pre, grad_up_pre
    )
    gate_core = links.over_core(gate_send)
    down_total = add(dot(swiglu, upstream_mine, (0, 0)), links.over_core(down_send))
    down_half = links.half(down_total, 1 - x)
    down_total, down_half, grad_gate_pre, grad_up_pre = fence(
        down_total, down_half, grad_gate_pre, grad_up_pre
    )
    down_x = links.over_x(down_half)

    up_send = dot(hidden2_other, grad_up_pre, (0, 0)).astype(BF16)
    grad_gate_pre, up_send = fence(grad_gate_pre, up_send)
    up_core = links.over_core(up_send)
    gate_total = add(dot(hidden2_mine, grad_gate_pre, (0, 0)), gate_core)
    gate_half = links.quarters(gate_total, 1 - links.y)
    gate_total, gate_half, grad_gate_pre, grad_up_pre = fence(
        gate_total, gate_half, grad_gate_pre, grad_up_pre
    )

    up_total = add(dot(hidden2_mine, grad_up_pre, (0, 0)), up_core)
    up_half = links.half(up_total, 1 - x)
    up_total, up_half, grad_gate_pre, grad_up_pre = fence(
        up_total, up_half, grad_gate_pre, grad_up_pre
    )
    up_x = links.over_x(up_half)

    grad_gate_up = jnp.concatenate([grad_gate_pre, grad_up_pre], axis=1)
    grad_hidden2 = dot(grad_gate_up, full_gate_up, (1, 1))
    grad_residual = upstream.astype(F32) + norm_back(grad_hidden2 * gain2, normed2, scale2)
    grad_residual_low = grad_residual.astype(BF16)
    grad_attended = dot(grad_residual_low, full_output, (1, 1)).astype(BF16)
    grad_attended, grad_residual_low = fence(grad_attended, grad_residual_low)
    do = layer.to_heads(grad_attended, 1)
    attended_mine, attended_other = by_core(attended, 2)
    out_send = dot(attended_other, grad_residual_low, (0, 0)).astype(BF16)
    out_total = add(dot(attended_mine, grad_residual_low, (0, 0)), links.over_core(out_send))
    out_total, down_x = fence(out_total, down_x)
    down_first = add(links.half(down_total, x), down_x)
    down_y = links.over_y(links.half(down_first, 1 - links.y))
    out_x = links.over_x(links.half(out_total, 1 - x))
    output = (residual + dot(swiglu, full_down, (1, 0))).astype(BF16)
    do, gate_half, down_first, output = fence(do, gate_half, down_first, output)
    gate_y = links.over_y(gate_half)

    grad_raw_heads = layer.attend_back(qkv, do, att_t, mass)
    grad_raw_heads, up_x, out_x, down_y = fence(grad_raw_heads, up_x, out_x, down_y)
    down_second = add(links.half(down_first, links.y), down_y)
    down_pair = links.over_pair(links.half(down_second, 1 - links.near))

    up_first = add(links.half(up_total, x), up_x)
    out_first = add(links.half(out_total, x), out_x)
    up_y = links.over_y(links.half(up_first, 1 - links.y))
    out_y = links.over_y(links.half(out_first, 1 - links.y))
    columns = dot(hidden_mine, grad_raw_heads, (0, 0)).astype(BF16)
    columns_x = links.over_x(links.half(columns, 1 - x))
    columns_x, grad_raw_heads, down_pair, gate_y = fence(
        columns_x, grad_raw_heads, down_pair, gate_y
    )
    gate_first = add(links.quarters(gate_total, links.y), gate_y)
    gate_x = links.over_x(links.half(gate_first, 1 - x))
    down_third = add(links.half(down_second, links.near), down_pair)
    down_far = links.over_far(links.half(down_third, 1 - links.far))
    grad_raw = layer.to_tokens(grad_raw_heads, 3)
    summed = layer.sum_sequences(add(links.half(columns, x), columns_x))
    gate_x, up_y, out_y, down_far, summed = fence(gate_x, up_y, out_y, down_far, summed)
    gate_second = add(links.half(gate_first, x), gate_x)
    down_piece = add(links.half(down_third, links.far), down_far)
    joined = jnp.concatenate(
        [
            gate_second,
            add(links.half(up_first, links.y), up_y),
            add(links.half(out_first, links.y), out_y),
        ],
        axis=1,
    )

    joined, down_piece, summed = fence(joined, down_piece, summed)
    joined_pair = links.over_pair(links.half(joined, 1 - links.near))
    summed = join(summed, links.over_far(summed), links.far)
    down_piece = join(down_piece, links.over_far(down_piece), links.far)
    joined_third = add(links.half(joined, links.near), joined_pair)
    joined_third, down_piece, summed, grad_raw = fence(joined_third, down_piece, summed, grad_raw)

    joined_far = links.over_far(links.half(joined_third, 1 - links.far))
    summed = join(summed, links.over_y(summed), links.y)
    down_piece = join(down_piece, links.over_pair(down_piece), links.near)
    grad_first = grad_raw[:, 2 * width :].astype(F32)
    grad_hidden1 = dot(grad_raw, full_qkv, (1, 1))
    grad_inputs = grad_residual + norm_back(grad_hidden1 * gain1, normed1, scale1)
    joined_piece = add(links.half(joined_third, links.far), joined_far)
    joined_piece, down_piece, summed, grad_inputs, grad_first = fence(
        joined_piece, down_piece, summed, grad_inputs, grad_first
    )

    joined_far = links.over_far(joined_piece)
    summed = join(summed, links.over_pair(summed), links.near)
    down_y = links.over_y(down_piece)
    down_piece = join(down_piece, down_y, links.y)
    part = join(joined_piece, joined_far, links.far)
    part, down_piece, summed = fence(part, down_piece, summed)

    def slots(*bits):
        place = [
            (core ^ c) * 4 + (links.y ^ y) * 2 + (links.near ^ near) for c, y, near in bits
        ]
        return jnp.stack(place).astype(jnp.int32)

    part_pair = links.over_pair(part)
    part_y = links.over_y(part)
    part_core = links.over_core(part)
    down_other = links.over_core(down_piece)
    grad_down = jnp.where(
        core == 0,
        jnp.concatenate([down_piece, down_other], axis=1),
        jnp.concatenate([down_other, down_piece], axis=1),
    ).astype(F32)
    grad_wquery, grad_wkey, grad_wvalue, sums = spread(
        core,
        summed,
        links.over_core(summed),
        w_query,
        w_key,
        w_value,
        layer.seqs,
        layer.groups,
    )
    part_pair, part_y, grad_down, grad_wquery, grad_wkey, grad_wvalue = fence(
        part_pair, part_y, grad_down, grad_wquery, grad_wkey, grad_wvalue
    )
    middle = part.shape[0] // 2
    last = (links.over_y(part_pair[:middle]), links.over_pair(part_y[middle:]))
    pair_core, y_core = links.over_core(part_pair), links.over_core(part_y)

    early = slots((0, 0, 0), (1, 0, 0), (0, 0, 1), (0, 1, 0), (1, 0, 1), (1, 1, 0))
    early_parts = (part, part_core, part_pair, part_y, pair_core, y_core)
    low, high, *filled = fence(*last, *finish(early, early_parts, w_gate, w_up, ()))
    late = slots((0, 1, 1), (1, 1, 1))
    late = jnp.concatenate([2 * late, 2 * late + 1])
    late_parts = (low, links.over_core(low), high, links.over_core(high))
    grad_wgate, grad_wup, grad_outproj, ff_sums = finish(late, late_parts, w_gate, w_up, filled)
    shape = tokens.shape
    return (
        output.reshape(shape),
        grad_inputs.reshape(shape),
        grad_first.reshape(shape),
        grad_wquery,
        grad_wkey,
        grad_wvalue,
        grad_outproj,
        grad_wgate,
        grad_wup,
        grad_down,
        jnp.sum(sums, axis=1) / gain_attn.astype(F32),
        jnp.sum(ff_sums, axis=1) / gain_ffn.astype(F32),
    )


def solution(mesh):
    sequence = P("shard", "rep", None)
    matrix = P("shard", None)
    vector = P("shard")
    reps, shards = mesh.shape["rep"], mesh.shape["shard"]
    linked = reps == 16 and shards == 2
    return jax.shard_map(
        functools.partial(local_linked if linked else local, reps),
        mesh=mesh,
        in_specs=(sequence, sequence, vector, sequence) + (matrix,) * 7 + (vector,) * 2,
        out_specs=(sequence,) * 3 + (matrix,) * 7 + (vector,) * 2,
        check_vma=False,
    )
```

```python
import functools

import jax
import jax.numpy as jnp
from jax import lax
from jax.experimental import pallas as pl
from jax.experimental.pallas import tpu as pltpu
from jax.sharding import PartitionSpec as P

HEADS = 16
EPSILON = 1e-05
NEGATIVE = -1e30
ROPE_BASE = 10000.0
BF16 = jnp.bfloat16
F32 = jnp.float32
VMEM_LIMIT = 60 * 1024 * 1024


def dot(left, right, contract):
    return lax.dot_general(
        left, right, ((contract[:1], contract[1:]), ((), ())), preferred_element_type=F32
    )


def norm_rows(values):
    scale = lax.rsqrt(jnp.mean(values * values, axis=-1, keepdims=True) + EPSILON)
    return (values * scale, scale)


def norm_back(gradient, normed, scale):
    return scale * (gradient - normed * jnp.mean(gradient * normed, axis=-1, keepdims=True))


def rope_lanes(positions, lanes, head_dim):
    half = head_dim // 2
    lane = jnp.arange(lanes, dtype=jnp.int32) % head_dim
    frequency = ROPE_BASE ** (-2.0 * (lane % half).astype(F32) / head_dim)
    angles = positions.astype(F32)[:, None] * frequency[None, :]
    sign = jnp.where(lane < half, 1.0, -1.0).astype(F32)
    return (jnp.cos(angles), jnp.sin(angles) * sign[None, :])


def partner(values, head_dim, roll):
    half = head_dim // 2
    lane = lax.broadcasted_iota(jnp.int32, values.shape, values.ndim - 1) % head_dim
    return jnp.where(lane < half, roll(values, half), roll(values, -half))


def lane_roll(values, shift):
    return jnp.roll(values, -shift, axis=-1)


def kernel_roll(values, shift):
    width = values.shape[-1]
    if width % 128 == 0:
        return pltpu.roll(values, (-shift) % width, axis=values.ndim - 1)
    shift = shift % width
    return jnp.concatenate([values[..., shift:], values[..., :shift]], axis=-1)


def head_rows(values, head, head_dim):
    if values.shape[-1] == head_dim:
        return values
    lane = lax.broadcasted_iota(jnp.int32, values.shape, values.ndim - 1)
    mine = (lane >= head * head_dim) & (lane < (head + 1) * head_dim)
    return jnp.where(mine, values, jnp.zeros_like(values))


def masked_scores(key_block, query_block, key_start, query_start, prefix):
    scores = dot(key_block, query_block, (1, 1))
    query_pos = query_start + lax.broadcasted_iota(jnp.int32, (1, scores.shape[1]), 1)
    last = jnp.maximum(query_pos, prefix - 1) - key_start
    key_pos = lax.broadcasted_iota(jnp.int32, scores.shape, 0)
    return jnp.where(key_pos <= last, scores, NEGATIVE)


def attend_kernel(
    head_dim, bq, bk, prefix_ref, q_ref, k_ref, v_ref, att_ref, att_t_ref, mass_ref, v_t, acc
):
    length, width = q_ref.shape
    heads = width // head_dim
    prefix = prefix_ref[0]
    for start in range(0, length, 128):
        v_t[:, start : start + 128] = v_ref[start : start + 128, :].T

    def query_step(i, carry):
        q0 = pl.multiple_of(i * bq, bq)
        q_all = q_ref[pl.ds(q0, bq), :]
        q_heads = [head_rows(q_all, h, head_dim) for h in range(heads)]
        acc[...] = jnp.zeros_like(acc)
        blocks = (jnp.maximum(q0 + bq, prefix) + bk - 1) // bk

        def key_step(j, stats):
            k0 = pl.multiple_of(j * bk, bk)
            k_block = k_ref[pl.ds(k0, bk), :]
            out = []
            for h in range(heads):
                peak, mass = stats[h]
                scores = masked_scores(k_block, q_heads[h], k0, q0, prefix)
                new_peak = jnp.maximum(peak, jnp.max(scores, axis=0, keepdims=True))
                alpha = jnp.exp(peak - new_peak)
                weights = jnp.exp(scores - new_peak)
                mass = mass * alpha + jnp.sum(weights, axis=0, keepdims=True)
                rows = slice(h * head_dim, (h + 1) * head_dim)
                acc[rows, :] = acc[rows, :] * alpha + dot(
                    v_t[rows, pl.ds(k0, bk)], weights.astype(BF16), (1, 0)
                )
                out.append((new_peak, mass))
            return tuple(out)

        first = tuple(
            (jnp.full((1, bq), NEGATIVE, F32), jnp.zeros((1, bq), F32)) for _ in range(heads)
        )
        stats = lax.fori_loop(0, blocks, key_step, first)
        for h in range(heads):
            peak, mass = stats[h]
            rows = slice(h * head_dim, (h + 1) * head_dim)
            att_t_ref[rows, pl.ds(q0, bq)] = acc[rows, :] / mass
            mass_ref[h : h + 1, pl.ds(q0, bq)] = peak + jnp.log(mass)
        for part in range(0, bq, 128):
            place = pl.ds(pl.multiple_of(q0 + part, 128), 128)
            att_ref[place, :] = att_t_ref[:, place].T.astype(BF16)
        return carry

    lax.fori_loop(0, length // bq, query_step, 0)


def attend_back_kernel(
    head_dim,
    bq,
    bk,
    prefix_ref,
    q_ref,
    k_ref,
    v_ref,
    do_ref,
    att_t_ref,
    mass_ref,
    cos_ref,
    sin_ref,
    out_ref,
    k_t,
    delta,
    dq_t,
    dk_acc,
    dv_acc,
):
    length, width = q_ref.shape
    heads = width // head_dim
    prefix = prefix_ref[0]
    dq_t[...] = jnp.zeros_like(dq_t)
    for start in range(0, length, 128):
        place = slice(start, start + 128)
        k_t[:, place] = k_ref[place, :].T
        product = do_ref[place, :].astype(F32).T * att_t_ref[:, place]
        for h in range(heads):
            rows = slice(h * head_dim, (h + 1) * head_dim)
            delta[h : h + 1, place] = jnp.sum(product[rows, :], axis=0, keepdims=True)

    def rope_back(gradient, place):
        return gradient * cos_ref[place, :] + partner(gradient, head_dim, kernel_roll) * sin_ref[
            place, :
        ]

    def key_step(j, carry):
        k0 = pl.multiple_of(j * bk, bk)
        k_block = k_ref[pl.ds(k0, bk), :]
        v_block = v_ref[pl.ds(k0, bk), :]
        dk_acc[...] = jnp.zeros_like(dk_acc)
        dv_acc[...] = jnp.zeros_like(dv_acc)
        begin = jnp.where(k0 < prefix, 0, k0 // bq)

        def query_step(i, inner):
            q0 = pl.multiple_of(i * bq, bq)
            q_all = q_ref[pl.ds(q0, bq), :]
            do_all = do_ref[pl.ds(q0, bq), :]
            for h in range(heads):
                rows = slice(h * head_dim, (h + 1) * head_dim)
                q_head = head_rows(q_all, h, head_dim)
                do_head = head_rows(do_all, h, head_dim)
                scores = masked_scores(k_block, q_head, k0, q0, prefix)
                weights = jnp.exp(scores - mass_ref[h : h + 1, pl.ds(q0, bq)])
                grad_weights = dot(v_block, do_head, (1, 1))
                grad_scores = (weights * (grad_weights - delta[h : h + 1, pl.ds(q0, bq)])).astype(
                    BF16
                )
                dv_acc[...] += dot(weights.astype(BF16), do_head, (1, 0))
                dk_acc[...] += dot(grad_scores, q_head, (1, 0))
                dq_t[rows, pl.ds(q0, bq)] += dot(k_t[rows, pl.ds(k0, bk)], grad_scores, (1, 0))
            return inner

        lax.fori_loop(begin, length // bq, query_step, 0)
        place = pl.ds(k0, bk)
        out_ref[place, width : 2 * width] = rope_back(dk_acc[...], place).astype(BF16)
        out_ref[place, 2 * width :] = dv_acc[...].astype(BF16) * jnp.array(0.5, BF16)
        return carry

    lax.fori_loop(0, length // bk, key_step, 0)
    for start in range(0, length, 128):
        place = slice(start, start + 128)
        out_ref[place, :width] = rope_back(dq_t[:, place].T * 0.125, place).astype(BF16)


def turns(reps, move):
    pairs = []
    for here in range(reps):
        z, y, core = move(here // 4, (here // 2) % 2, here % 2)
        pairs.append((here, (z % (reps // 4)) * 4 + y * 2 + core))
    return pairs


class Links:
    def __init__(self, reps):
        self.to_core = turns(reps, lambda z, y, core: (z, y, 1 - core))
        self.to_y = turns(reps, lambda z, y, core: (z, 1 - y, core))
        self.to_pair = turns(reps, lambda z, y, core: (z ^ 1, y, core))
        self.to_far = turns(reps, lambda z, y, core: (z ^ 2, y, core))
        here = lax.axis_index("rep")
        self.near, self.far = (here // 4) % 2, here // 8
        self.y, self.core = (here // 2) % 2, here % 2
        self.x = lax.axis_index("shard")

    def over_core(self, value):
        return lax.ppermute(value, "rep", self.to_core)

    def over_x(self, value):
        return lax.ppermute(value, "shard", [(0, 1), (1, 0)])

    def over_y(self, value):
        return lax.ppermute(value, "rep", self.to_y)

    def over_pair(self, value):
        return lax.ppermute(value, "rep", self.to_pair)

    def over_far(self, value):
        return lax.ppermute(value, "rep", self.to_far)

    def half(self, total, side):
        return pick(total.reshape(2, -1, total.shape[1]), side)

    def quarters(self, total, side):
        columns = total.shape[1]
        return pick(total.reshape(2, 2, -1, columns), side, 1).reshape(-1, columns)


def pick(values, index, axis=0):
    return lax.dynamic_index_in_dim(values, index, axis, keepdims=False)


def put(values, part, index):
    return lax.dynamic_update_index_in_dim(values, part, index, 0)


def join(mine, other, index):
    first = jnp.concatenate([mine, other], axis=0)
    second = jnp.concatenate([other, mine], axis=0)
    return jnp.where(index == 0, first, second)


def fence(*values):
    return lax.optimization_barrier(values)


def after(value, *earlier):
    return lax.optimization_barrier((value,) + earlier)[0]


def blank(shape, dtype):
    return pl.pallas_call(
        lambda out_ref: None,
        out_shape=jax.ShapeDtypeStruct(shape, dtype),
        out_specs=pl.BlockSpec(memory_space=pl.ANY),
    )()


def add(left, right):
    return (left.astype(F32) + right.astype(F32)).astype(BF16)


def whole(shape):
    return pl.BlockSpec(shape, lambda *_: (0,) * len(shape))


def thirds(qkv):
    length, width = qkv.shape[0], qkv.shape[1] // 3
    if width % 128 == 0:
        specs = [pl.BlockSpec((length, width), lambda *_, at=at: (0, at)) for at in range(3)]
        return (qkv, qkv, qkv), specs
    parts = tuple(qkv[:, at * width : (at + 1) * width] for at in range(3))
    return parts, [whole((length, width))] * 3


def attend(prefix, qkv, head_dim, bq, bk):
    length, width = qkv.shape[0], qkv.shape[1] // 3
    heads = width // head_dim
    flops = 2 * 2 * heads * length * length * head_dim
    operands, specs = thirds(qkv)
    return pl.pallas_call(
        functools.partial(attend_kernel, head_dim, bq, bk),
        out_shape=(
            jax.ShapeDtypeStruct((length, width), BF16),
            jax.ShapeDtypeStruct((width, length), F32),
            jax.ShapeDtypeStruct((heads, length), F32),
        ),
        grid_spec=pltpu.PrefetchScalarGridSpec(
            num_scalar_prefetch=1,
            grid=(1,),
            in_specs=specs,
            out_specs=[whole((length, width)), whole((width, length)), whole((heads, length))],
            scratch_shapes=[pltpu.VMEM((width, length), BF16), pltpu.VMEM((width, bq), F32)],
        ),
        compiler_params=pltpu.CompilerParams(vmem_limit_bytes=VMEM_LIMIT),
        cost_estimate=pl.CostEstimate(flops=1, transcendentals=0, bytes_accessed=1),
    )(prefix, *operands)


def attend_back(prefix, qkv, do, att_t, mass, cosine, sine, head_dim, bq, bk):
    length, width = qkv.shape[0], qkv.shape[1] // 3
    heads = width // head_dim
    flops = 5 * 2 * heads * length * length * head_dim
    rows = whole((length, width))
    operands, specs = thirds(qkv)
    return pl.pallas_call(
        functools.partial(attend_back_kernel, head_dim, bq, bk),
        out_shape=jax.ShapeDtypeStruct((length, 3 * width), BF16),
        grid_spec=pltpu.PrefetchScalarGridSpec(
            num_scalar_prefetch=1,
            grid=(1,),
            in_specs=specs + [rows, whole((width, length)), whole((heads, length)), rows, rows],
            out_specs=whole((length, 3 * width)),
            scratch_shapes=[
                pltpu.VMEM((width, length), BF16),
                pltpu.VMEM((heads, length), F32),
                pltpu.VMEM((width, length), F32),
                pltpu.VMEM((bk, width), F32),
                pltpu.VMEM((bk, width), F32),
            ],
        ),
        compiler_params=pltpu.CompilerParams(vmem_limit_bytes=VMEM_LIMIT),
        cost_estimate=pl.CostEstimate(flops=1, transcendentals=0, bytes_accessed=1),
    )(prefix, *operands, do, att_t, mass, cosine, sine)


def spread_kernel(lanes, core_ref, mine_ref, other_ref, wq_ref, wk_ref, wv_ref, *out_refs):
    sum_ref = out_refs[3]
    core = core_ref[0]
    total = jnp.zeros(sum_ref.shape, F32)
    for near in range(2):
        for y in range(2):
            mine, other = mine_ref[near, y, 0], other_ref[near, y, 0]
            for side, part in enumerate((mine, other)):
                part = jnp.where(core == 0, part, other if side == 0 else mine)
                group = near * 4 + y * 2 + side
                place = slice(group * lanes, (group + 1) * lanes)
                for at, w_ref in enumerate((wq_ref, wk_ref, wv_ref)):
                    values = part[:, at * lanes : (at + 1) * lanes].astype(F32)
                    out_refs[at][:, place] = values
                    total += values * w_ref[:, place].astype(F32)
    sum_ref[...] = total


def spread(core, mine, other, w_query, w_key, w_value, seqs, groups):
    height, width = w_query.shape
    share, lanes = height // seqs, width // groups
    steps = 4
    rows = share // steps
    tile = pl.BlockSpec((rows, width), lambda s, i, core: (s * steps + i, 0))
    part = pl.BlockSpec((2, 2, 1, rows, 3 * lanes), lambda s, i, core: (0, 0, s, i, 0))
    shape = (2, 2, seqs, share, 3 * lanes)
    return pl.pallas_call(
        functools.partial(spread_kernel, lanes),
        out_shape=(jax.ShapeDtypeStruct((height, width), F32),) * 3
        + (jax.ShapeDtypeStruct((height, lanes), F32),),
        grid_spec=pltpu.PrefetchScalarGridSpec(
            num_scalar_prefetch=1,
            grid=(seqs, steps),
            in_specs=[part, part, tile, tile, tile],
            out_specs=[tile, tile, tile]
            + [pl.BlockSpec((rows, lanes), lambda s, i, core: (s * steps + i, 0))],
        ),
        cost_estimate=pl.CostEstimate(flops=1, transcendentals=0, bytes_accessed=1),
    )(
        core.reshape(1).astype(jnp.int32),
        mine.reshape(shape),
        other.reshape(shape),
        w_query,
        w_key,
        w_value,
    )


def finish_kernel(count, ff, slots_ref, *refs):
    parts, (gate_ref, up_ref) = refs[:count], refs[count : count + 2]
    grad_gate_ref, grad_up_ref, grad_out_ref, sum_ref, buffer, arrived = refs[-6:]
    step = pl.program_id(0)

    def fetch(at):
        return pltpu.make_async_copy(parts[at], buffer.at[at % 2], arrived.at[at % 2])

    for at in range(count):

        @pl.when(step == max(at - 1, 0))
        def _():
            fetch(at).start()

    for at in range(count):

        @pl.when(step == at)
        def _():
            fetch(at).wait()

    here = lax.rem(step, 2)
    lanes = sum_ref.shape[1]
    total = jnp.zeros(sum_ref.shape, F32)
    for start in range(0, ff, lanes):
        place = slice(start, start + lanes)
        grad_gate = buffer[here, :, place].astype(F32)
        grad_up = buffer[here, :, ff + start : ff + start + lanes].astype(F32)
        grad_gate_ref[:, place] = grad_gate
        grad_up_ref[:, place] = grad_up
        total += grad_gate * gate_ref[:, place].astype(F32)
        total += grad_up * up_ref[:, place].astype(F32)
    sum_ref[...] = total
    grad_out_ref[...] = buffer[here, :, 2 * ff :].astype(F32)


def finish(slots, parts, w_gate, w_up, filled):
    height, ff = w_gate.shape
    share, columns = parts[0].shape
    count = len(parts)

    def rows(width):
        return pl.BlockSpec((share, width), lambda i, slots: (slots[i], 0))

    anywhere = pl.BlockSpec(memory_space=pl.ANY)
    widths = (ff, ff, columns - 2 * ff, 128)
    return pl.pallas_call(
        functools.partial(finish_kernel, count, ff),
        out_shape=tuple(jax.ShapeDtypeStruct((height, width), F32) for width in widths),
        grid_spec=pltpu.PrefetchScalarGridSpec(
            num_scalar_prefetch=1,
            grid=(count,),
            in_specs=[anywhere] * count + [rows(ff), rows(ff)] + [anywhere] * len(filled),
            out_specs=[rows(width) for width in widths],
            scratch_shapes=[
                pltpu.VMEM((2, share, columns), BF16),
                pltpu.SemaphoreType.DMA((2,)),
            ],
        ),
        input_output_aliases={count + 3 + at: at for at in range(len(filled))},
        compiler_params=pltpu.CompilerParams(vmem_limit_bytes=VMEM_LIMIT),
        cost_estimate=pl.CostEstimate(flops=1, transcendentals=0, bytes_accessed=1),
    )(slots, *parts, w_gate, w_up, *filled)


class Layer:
    def __init__(self, reps, tokens, prefix_len):
        self.reps = reps
        self.seqs, self.rows, self.width = tokens.shape
        self.head_dim = self.width // HEADS
        self.length = self.rows * reps
        self.groups = reps // self.seqs
        self.lanes = self.width // self.groups
        self.total = self.seqs * self.rows
        self.block = min(512, self.length)
        here = lax.axis_index("rep")
        self.my_seq = here // self.groups
        positions = here * self.rows + jnp.arange(self.rows, dtype=jnp.int32)
        cosine, sine = rope_lanes(positions, self.width, self.head_dim)
        self.cosine = jnp.tile(cosine, (self.seqs, 1))
        self.sine = jnp.tile(sine, (self.seqs, 1))
        self.all_tables = rope_lanes(
            jnp.arange(self.length, dtype=jnp.int32), self.lanes, self.head_dim
        )
        self.prefix = lax.dynamic_slice_in_dim(prefix_len, self.my_seq, 1, 0)

    def to_heads(self, values, parts):
        shape = (self.seqs, self.rows, parts, self.groups, self.lanes)
        chunks = values.reshape(shape).transpose(0, 3, 1, 2, 4)
        chunks = chunks.reshape(self.reps * self.rows, parts * self.lanes)
        return lax.all_to_all(chunks, "rep", 0, 0, tiled=True)

    def to_tokens(self, values, parts):
        chunks = lax.all_to_all(values, "rep", 0, 0, tiled=True)
        chunks = chunks.reshape(self.seqs, self.groups, self.rows, parts, self.lanes)
        return chunks.transpose(0, 2, 3, 1, 4).reshape(self.total, parts * self.width)

    def project(self, hidden, full_qkv, first_values):
        width = self.width
        raw = dot(hidden, full_qkv, (1, 0))

        def rope(values):
            return values * self.cosine - partner(values, self.head_dim, lane_roll) * self.sine

        query_rot = (rope(raw[:, :width]) * 0.125).astype(BF16)
        key_rot = rope(raw[:, width : 2 * width]).astype(BF16)
        first = first_values.reshape(self.total, width).astype(F32)
        value_mix = (0.5 * raw[:, 2 * width :] + 0.5 * first).astype(BF16)
        return jnp.concatenate([query_rot, key_rot, value_mix], axis=1)

    def attend(self, qkv):
        return attend(self.prefix, qkv, self.head_dim, self.block, self.block)

    def attend_back(self, qkv, do, att_t, mass):
        return attend_back(
            self.prefix, qkv, do, att_t, mass, *self.all_tables, self.head_dim, self.block, self.block
        )

    def sum_sequences(self, columns):
        share = columns.shape[0] // self.seqs
        mine = lax.dynamic_slice_in_dim(columns, self.my_seq * share, share, 0).astype(F32)
        for turn in range(1, self.seqs):
            slot = (self.my_seq + turn) % self.seqs
            sent = lax.dynamic_slice_in_dim(columns, slot * share, share, 0)
            moves = [
                (s * self.groups + g, ((s + turn) % self.seqs) * self.groups + g)
                for s in range(self.seqs)
                for g in range(self.groups)
            ]
            mine = mine + lax.ppermute(sent, "rep", moves).astype(F32)
        return mine.astype(BF16)


def gain_gradient(gain, *pairs):
    total = sum(jnp.sum(w.astype(F32) * gradient, axis=1) for w, gradient in pairs)
    return total / gain.astype(F32)


def gate_back(grad_swiglu, gate_pre, up_pre, sigma, swish):
    grad_gate_pre = grad_swiglu * up_pre * sigma * (1.0 + gate_pre * (1.0 - sigma))
    return (grad_gate_pre.astype(BF16), (grad_swiglu * swish).astype(BF16))


def local(
    reps,
    tokens,
    first_values,
    prefix_len,
    cotangent,
    w_query,
    w_key,
    w_value,
    w_output,
    w_gate,
    w_up,
    w_down,
    gain_attn,
    gain_ffn,
):
    layer = Layer(reps, tokens, prefix_len)
    total, width, ff = layer.total, layer.width, w_gate.shape[1]
    here = lax.axis_index("rep")

    def gather(weights):
        height = weights[0].shape[0]
        share = height // reps
        if share * reps == height and share % 8 == 0:
            pieces = [lax.dynamic_slice_in_dim(w, here * share, share, 0) for w in weights]
            axes = ("shard", "rep")
        else:
            pieces, axes = list(weights), ("shard",)
        piece = pieces[0] if len(pieces) == 1 else jnp.concatenate(pieces, axis=1)
        return lax.all_gather(piece, axes, axis=0, tiled=True)

    gains = lax.all_gather(jnp.stack([gain_attn, gain_ffn]), "shard", axis=1, tiled=True)
    full_qkv = gather((w_query, w_key, w_value))
    full_output = gather((w_output,))
    full_gate_up = gather((w_gate, w_up))
    full_down = gather((w_down,))
    gain1 = gains[0].astype(F32)
    gain2 = gains[1].astype(F32)

    inputs = tokens.reshape(total, width).astype(F32)
    normed1, scale1 = norm_rows(inputs)
    hidden1 = (normed1 * gain1).astype(BF16)
    hidden1_all = lax.all_gather(hidden1.reshape(tokens.shape), "rep", axis=1, tiled=True)
    qkv = layer.to_heads(layer.project(hidden1, full_qkv, first_values), 3)
    att, att_t, mass = layer.attend(qkv)
    attended = layer.to_tokens(att, 1)

    residual = inputs + dot(attended, full_output, (1, 0))
    normed2, scale2 = norm_rows(residual)
    hidden2 = (normed2 * gain2).astype(BF16)
    gate_up = dot(hidden2, full_gate_up, (1, 0))
    gate_pre, up_pre = gate_up[:, :ff], gate_up[:, ff:]
    sigma = jax.nn.sigmoid(gate_pre)
    swish = gate_pre * sigma
    swiglu = (swish * up_pre).astype(BF16)
    output = (residual + dot(swiglu, full_down, (1, 0))).astype(BF16)

    upstream = cotangent.reshape(total, width)
    grad_swiglu = dot(upstream, full_down, (1, 1))
    grad_gate_up = jnp.concatenate(gate_back(grad_swiglu, gate_pre, up_pre, sigma, swish), axis=1)
    grad_hidden2 = dot(grad_gate_up, full_gate_up, (1, 1))
    grad_residual = upstream.astype(F32) + norm_back(grad_hidden2 * gain2, normed2, scale2)
    grad_residual_low = grad_residual.astype(BF16)
    grad_attended = dot(grad_residual_low, full_output, (1, 1)).astype(BF16)

    def reduce_gather(partial):
        axes = ("shard", "rep")
        piece = lax.psum_scatter(partial.astype(BF16), axes, scatter_dimension=0, tiled=True)
        return lax.all_gather(piece, "rep", axis=0, tiled=True).astype(F32)

    grad_down = reduce_gather(dot(swiglu, upstream, (0, 0)))
    grad_wgate_up = reduce_gather(dot(hidden2, grad_gate_up, (0, 0)))
    grad_outproj = reduce_gather(dot(attended, grad_residual_low, (0, 0)))
    grad_wgate, grad_wup = grad_wgate_up[:, :ff], grad_wgate_up[:, ff:]

    do = layer.to_heads(grad_attended, 1)
    grad_raw_heads = layer.attend_back(qkv, do, att_t, mass)
    grad_raw = layer.to_tokens(grad_raw_heads, 3)
    grad_first = grad_raw[:, 2 * width :].astype(F32)
    grad_hidden1 = dot(grad_raw, full_qkv, (1, 1))
    grad_inputs = grad_residual + norm_back(grad_hidden1 * gain1, normed1, scale1)

    hidden_mine = lax.dynamic_index_in_dim(hidden1_all, layer.my_seq, 0, keepdims=False)
    columns = dot(hidden_mine, grad_raw_heads, (0, 0)).astype(BF16)
    columns = lax.psum_scatter(columns, "shard", scatter_dimension=0, tiled=True)
    height = columns.shape[0]
    mine = layer.sum_sequences(columns)
    gathered = lax.all_gather(mine, "rep", axis=0, tiled=True)
    gathered = gathered.reshape(layer.seqs, layer.groups, -1, 3, layer.lanes)
    grad_wqkv = gathered.transpose(3, 0, 2, 1, 4).reshape(3, height, width).astype(F32)
    shape = tokens.shape
    return (
        output.reshape(shape),
        grad_inputs.reshape(shape),
        grad_first.reshape(shape),
        grad_wqkv[0],
        grad_wqkv[1],
        grad_wqkv[2],
        grad_outproj,
        grad_wgate,
        grad_wup,
        grad_down,
        gain_gradient(
            gain_attn, (w_query, grad_wqkv[0]), (w_key, grad_wqkv[1]), (w_value, grad_wqkv[2])
        ),
        gain_gradient(gain_ffn, (w_gate, grad_wgate), (w_up, grad_wup)),
    )


def local_linked(
    reps,
    tokens,
    first_values,
    prefix_len,
    cotangent,
    w_query,
    w_key,
    w_value,
    w_output,
    w_gate,
    w_up,
    w_down,
    gain_attn,
    gain_ffn,
):
    layer = Layer(reps, tokens, prefix_len)
    links = Links(reps)
    total, width, ff = layer.total, layer.width, w_gate.shape[1]
    core, x = links.core, links.x

    own_gains = jnp.stack([gain_attn, gain_ffn])
    other_gains = links.over_x(own_gains)
    gains = jnp.where(
        x == 0,
        jnp.concatenate([own_gains, other_gains], axis=1),
        jnp.concatenate([other_gains, own_gains], axis=1),
    )
    gain1 = gains[0].astype(F32)
    gain2 = gains[1].astype(F32)

    def half_rows(weights):
        half = weights[0].shape[0] // 2
        pieces = [lax.dynamic_slice_in_dim(w, core * half, half, 0) for w in weights]
        return pieces[0] if len(pieces) == 1 else jnp.concatenate(pieces, axis=1)

    def assemble(weights, near, far, at):
        height = weights[0].shape[0]
        half = near.shape[0]
        columns = sum(w.shape[1] for w in weights)
        full = blank((2 * height, columns), BF16)
        place = 0
        for w in weights:
            full = lax.dynamic_update_slice(full, w, (x * height, place))
            place += w.shape[1]
        for part, owner in ((near, core), (far, 1 - core)):
            part = lax.slice_in_dim(part, at, at + columns, axis=1)
            full = lax.dynamic_update_slice(full, part, ((1 - x) * height + owner * half, 0))
        return full

    half_qkv = after(half_rows((w_query, w_key, w_value)), own_gains)
    near_qkv = links.over_x(half_qkv)
    near_ff = links.over_x(after(half_rows((w_output, w_gate, w_up)), near_qkv))
    full_qkv = assemble((w_query, w_key, w_value), near_qkv, links.over_core(near_qkv), 0)

    inputs = tokens.reshape(total, width).astype(F32)
    normed1, scale1 = norm_rows(inputs)
    hidden1 = (normed1 * gain1).astype(BF16)
    by_seq = after(hidden1, half_qkv).reshape(tokens.shape)
    mine, theirs = pick(by_seq, links.far), pick(by_seq, 1 - links.far)
    halves = join(mine[None], links.over_far(theirs)[None], links.far)
    groups = [list(range(layer.groups)), list(range(layer.groups, reps))]
    hidden1, halves, *layer.all_tables = fence(hidden1, halves, *layer.all_tables)
    hidden_mine = lax.all_gather(halves, "rep", axis_index_groups=groups, axis=1, tiled=True)
    hidden_mine = hidden_mine.reshape(layer.length, width)
    qkv = layer.to_heads(layer.project(hidden1, full_qkv, first_values), 3)
    qkv, hidden_mine = fence(qkv, hidden_mine)
    att, att_t, mass = layer.attend(qkv)
    att, near_ff, down_half = fence(att, near_ff, half_rows((w_down,)))
    near_down = links.over_x(down_half)
    far_ff = links.over_core(near_ff)
    full_output = assemble((w_output,), near_ff, far_ff, 0)
    full_gate_up = assemble((w_gate, w_up), near_ff, far_ff, w_output.shape[1])
    attended = layer.to_tokens(att, 1)
    height = w_down.shape[0]
    own_down = lax.dynamic_update_slice(blank((2 * height, width), BF16), w_down, (x * height, 0))
    attended, own_down = fence(attended, own_down)

    residual = inputs + dot(attended, full_output, (1, 0))
    normed2, scale2 = norm_rows(residual)
    hidden2 = (normed2 * gain2).astype(BF16)
    gate_up = dot(hidden2, full_gate_up, (1, 0))
    gate_pre, up_pre = gate_up[:, :ff], gate_up[:, ff:]
    sigma = jax.nn.sigmoid(gate_pre)
    swish = gate_pre * sigma
    swiglu = (swish * up_pre).astype(BF16)
    near_down = after(near_down, swiglu)
    full_down = own_down
    for part, owner in ((near_down, core), (links.over_core(near_down), 1 - core)):
        row = (1 - x) * height + owner * (height // 2)
        full_down = lax.dynamic_update_slice(full_down, part, (row, 0))
    upstream = cotangent.reshape(total, width)

    def by_core(values, blocks):
        step = values.shape[1] // (2 * blocks)
        sides = [
            [values[:, (2 * b + side) * step : (2 * b + side + 1) * step] for b in range(blocks)]
            for side in range(2)
        ]
        low, high = (s[0] if blocks == 1 else jnp.concatenate(s, axis=1) for s in sides)
        return jnp.where(core == 0, low, high), jnp.where(core == 0, high, low)

    upstream_mine, upstream_other = by_core(upstream, 1)
    hidden2_mine, hidden2_other = by_core(hidden2, 2)
    down_send = dot(swiglu, upstream_other, (0, 0)).astype(BF16)
    grad_swiglu = dot(upstream, full_down, (1, 1))
    grad_gate_pre, grad_up_pre = gate_back(grad_swiglu, gate_pre, up_pre, sigma, swish)
    gate_send = dot(hidden2_other, grad_gate_pre, (0, 0)).astype(BF16)
    swiglu, gate_send, grad_gate_pre, grad_up_pre = fence(
        swiglu, gate_send, grad_gate_pre, grad_up_pre
    )
    gate_core = links.over_core(gate_send)
    down_total = add(dot(swiglu, upstream_mine, (0, 0)), links.over_core(down_send))
    down_half = links.half(down_total, 1 - x)
    down_total, down_half, grad_gate_pre, grad_up_pre = fence(
        down_total, down_half, grad_gate_pre, grad_up_pre
    )
    down_x = links.over_x(down_half)

    up_send = dot(hidden2_other, grad_up_pre, (0, 0)).astype(BF16)
    grad_gate_pre, up_send = fence(grad_gate_pre, up_send)
    up_core = links.over_core(up_send)
    gate_total = add(dot(hidden2_mine, grad_gate_pre, (0, 0)), gate_core)
    gate_half = links.quarters(gate_total, 1 - links.y)
    gate_total, gate_half, grad_gate_pre, grad_up_pre = fence(
        gate_total, gate_half, grad_gate_pre, grad_up_pre
    )

    up_total = add(dot(hidden2_mine, grad_up_pre, (0, 0)), up_core)
    up_half = links.half(up_total, 1 - x)
    up_total, up_half, grad_gate_pre, grad_up_pre = fence(
        up_total, up_half, grad_gate_pre, grad_up_pre
    )
    up_x = links.over_x(up_half)

    grad_gate_up = jnp.concatenate([grad_gate_pre, grad_up_pre], axis=1)
    grad_hidden2 = dot(grad_gate_up, full_gate_up, (1, 1))
    grad_residual = upstream.astype(F32) + norm_back(grad_hidden2 * gain2, normed2, scale2)
    grad_residual_low = grad_residual.astype(BF16)
    grad_attended = dot(grad_residual_low, full_output, (1, 1)).astype(BF16)
    grad_attended, grad_residual_low = fence(grad_attended, grad_residual_low)
    do = layer.to_heads(grad_attended, 1)
    attended_mine, attended_other = by_core(attended, 2)
    out_send = dot(attended_other, grad_residual_low, (0, 0)).astype(BF16)
    out_total = add(dot(attended_mine, grad_residual_low, (0, 0)), links.over_core(out_send))
    out_total, down_x = fence(out_total, down_x)
    down_first = add(links.half(down_total, x), down_x)
    down_y = links.over_y(links.half(down_first, 1 - links.y))
    out_x = links.over_x(links.half(out_total, 1 - x))
    output = (residual + dot(swiglu, full_down, (1, 0))).astype(BF16)
    do, gate_half, down_first, output = fence(do, gate_half, down_first, output)
    gate_y = links.over_y(gate_half)

    grad_raw_heads = layer.attend_back(qkv, do, att_t, mass)
    grad_raw_heads, up_x, out_x, down_y = fence(grad_raw_heads, up_x, out_x, down_y)
    down_second = add(links.half(down_first, links.y), down_y)
    down_pair = links.over_pair(links.half(down_second, 1 - links.near))

    up_first = add(links.half(up_total, x), up_x)
    out_first = add(links.half(out_total, x), out_x)
    up_y = links.over_y(links.half(up_first, 1 - links.y))
    out_y = links.over_y(links.half(out_first, 1 - links.y))
    columns = dot(hidden_mine, grad_raw_heads, (0, 0)).astype(BF16)
    columns_x = links.over_x(links.half(columns, 1 - x))
    columns_x, grad_raw_heads, down_pair, gate_y = fence(
        columns_x, grad_raw_heads, down_pair, gate_y
    )
    gate_first = add(links.quarters(gate_total, links.y), gate_y)
    gate_x = links.over_x(links.half(gate_first, 1 - x))
    down_third = add(links.half(down_second, links.near), down_pair)
    down_far = links.over_far(links.half(down_third, 1 - links.far))
    grad_raw = layer.to_tokens(grad_raw_heads, 3)
    summed = layer.sum_sequences(add(links.half(columns, x), columns_x))
    gate_x, up_y, out_y, down_far, summed = fence(gate_x, up_y, out_y, down_far, summed)
    gate_second = add(links.half(gate_first, x), gate_x)
    down_piece = add(links.half(down_third, links.far), down_far)
    joined = jnp.concatenate(
        [
            gate_second,
            add(links.half(up_first, links.y), up_y),
            add(links.half(out_first, links.y), out_y),
        ],
        axis=1,
    )

    joined, down_piece, summed = fence(joined, down_piece, summed)
    joined_pair = links.over_pair(links.half(joined, 1 - links.near))
    summed = join(summed, links.over_far(summed), links.far)
    down_piece = join(down_piece, links.over_far(down_piece), links.far)
    joined_third = add(links.half(joined, links.near), joined_pair)
    joined_third, down_piece, summed, grad_raw = fence(joined_third, down_piece, summed, grad_raw)

    joined_far = links.over_far(links.half(joined_third, 1 - links.far))
    summed = join(summed, links.over_y(summed), links.y)
    down_piece = join(down_piece, links.over_pair(down_piece), links.near)
    grad_first = grad_raw[:, 2 * width :].astype(F32)
    grad_hidden1 = dot(grad_raw, full_qkv, (1, 1))
    grad_inputs = grad_residual + norm_back(grad_hidden1 * gain1, normed1, scale1)
    joined_piece = add(links.half(joined_third, links.far), joined_far)
    joined_piece, down_piece, summed, grad_inputs, grad_first = fence(
        joined_piece, down_piece, summed, grad_inputs, grad_first
    )

    joined_far = links.over_far(joined_piece)
    summed = join(summed, links.over_pair(summed), links.near)
    down_y = links.over_y(down_piece)
    down_piece = join(down_piece, down_y, links.y)
    part = join(joined_piece, joined_far, links.far)
    part, down_piece = fence(part, down_piece)

    def slots(*bits):
        place = [
            (core ^ c) * 4 + (links.y ^ y) * 2 + (links.near ^ near) for c, y, near in bits
        ]
        return jnp.stack(place).astype(jnp.int32)

    part_pair = links.over_pair(part)
    part_y = links.over_y(part)
    part_core = links.over_core(part)
    down_other = links.over_core(down_piece)
    grad_down = jnp.where(
        core == 0,
        jnp.concatenate([down_piece, down_other], axis=1),
        jnp.concatenate([down_other, down_piece], axis=1),
    ).astype(F32)
    grad_wquery, grad_wkey, grad_wvalue, sums = spread(
        core,
        summed,
        links.over_core(summed),
        w_query,
        w_key,
        w_value,
        layer.seqs,
        layer.groups,
    )
    part_pair, part_y, grad_down, grad_wquery, grad_wkey, grad_wvalue, *filled = fence(
        part_pair,
        part_y,
        grad_down,
        grad_wquery,
        grad_wkey,
        grad_wvalue,
        *finish(slots((0, 0, 0), (1, 0, 0)), (part, part_core), w_gate, w_up, ()),
    )
    middle = part.shape[0] // 2
    last = (links.over_y(part_pair[:middle]), links.over_pair(part_y[middle:]))
    pair_core, y_core = links.over_core(part_pair), links.over_core(part_y)

    early = slots((0, 0, 1), (0, 1, 0), (1, 0, 1), (1, 1, 0))
    early_parts = (part_pair, part_y, pair_core, y_core)
    low, high, *filled = fence(*last, *finish(early, early_parts, w_gate, w_up, filled))
    late = slots((0, 1, 1), (1, 1, 1))
    late = jnp.concatenate([2 * late, 2 * late + 1])
    late_parts = (low, links.over_core(low), high, links.over_core(high))
    grad_wgate, grad_wup, grad_outproj, ff_sums = finish(late, late_parts, w_gate, w_up, filled)
    shape = tokens.shape
    return (
        output.reshape(shape),
        grad_inputs.reshape(shape),
        grad_first.reshape(shape),
        grad_wquery,
        grad_wkey,
        grad_wvalue,
        grad_outproj,
        grad_wgate,
        grad_wup,
        grad_down,
        jnp.sum(sums, axis=1) / gain_attn.astype(F32),
        jnp.sum(ff_sums, axis=1) / gain_ffn.astype(F32),
    )


def solution(mesh):
    sequence = P("shard", "rep", None)
    matrix = P("shard", None)
    vector = P("shard")
    reps, shards = mesh.shape["rep"], mesh.shape["shard"]
    linked = reps == 16 and shards == 2
    return jax.shard_map(
        functools.partial(local_linked if linked else local, reps),
        mesh=mesh,
        in_specs=(sequence, sequence, vector, sequence) + (matrix,) * 7 + (vector,) * 2,
        out_specs=(sequence,) * 3 + (matrix,) * 7 + (vector,) * 2,
        check_vma=False,
    )
```
